32 devices in a mesh: wide: 8 (over z, y), tp: 4 (over x, core).
Axes of the slice: x: 2, y: 2, z: 4, core: 2. Of those that a mesh axis runs over, the one named last changes fastest.
Arguments:
- hidden_in: bfloat16 [2, 2560, 2048], P(None, ('wide', 'tp')), may hold values from -6 to 6
- segments: int32 [2, 2560], P(None, 'wide'), may hold values from 0 to 42, as said below
- attn_gain: bfloat16 [2048], P('wide'), may hold values from 0.5 to 1.5
- query_weight: bfloat16 [2048, 2048], P('wide', 'tp'), may hold values from -0.1875 to 0.1875
- key_weight: bfloat16 [2048, 1024], P('wide', 'tp'), may hold values from -0.125 to 0.125
- value_weight: bfloat16 [2048, 1024], P('wide', 'tp'), may hold values from -0.125 to 0.125
- output_weight: bfloat16 [2048, 2048], P('tp', 'wide'), may hold values from -0.875 to 0.875
- mlp_gain: bfloat16 [2048], P('wide'), may hold values from 0.5 to 1.5
- gate_weight: bfloat16 [2048, 8192], P('wide', 'tp'), may hold values from -0.125 to 0.125
- up_weight: bfloat16 [2048, 8192], P('wide', 'tp'), may hold values from -0.125 to 0.125
- down_weight: bfloat16 [8192, 2048], P('tp', 'wide'), may hold values from -0.0625 to 0.0625
- cotangent: bfloat16 [2, 2560, 2048], P(None, ('wide', 'tp')), may hold values from -6 to 6
Outputs:
- layer_out: bfloat16 [2, 2560, 2048], P(None, ('wide', 'tp'))
- input_grad: float32 [2, 2560, 2048], P(None, ('wide', 'tp'))
- attn_gain_grad: float32 [2048], P('wide')
- query_weight_grad: float32 [2048, 2048], P('wide', 'tp')
- key_weight_grad: float32 [2048, 1024], P('wide', 'tp')
- value_weight_grad: float32 [2048, 1024], P('wide', 'tp')
- output_weight_grad: float32 [2048, 2048], P('tp', 'wide')
- mlp_gain_grad: float32 [2048], P('wide')
- gate_weight_grad: float32 [2048, 8192], P('wide', 'tp')
- up_weight_grad: float32 [2048, 8192], P('wide', 'tp')
- down_weight_grad: float32 [8192, 2048], P('tp', 'wide')
The draws below stay inside these ranges and needn't reach their ends.
Inputs may be any that keep to these rules, and one draw needn't show every extreme that they name: `segments`: along each micro-batch's 2560 positions the document number starts at 0, never falls, rises by at most one from a position to the next, and ends at exactly 42. One document starts at a position from 80 to 160 and ends at a position from 2400 to 2478.
All inputs are finite; a program needn't handle non-finite values.
Results may differ from the reference program's by a relative error of at most 0.025.
Values may be sent and summed in bfloat16 or wider, within the bound.
No kernel may reach another device: no remote copies, remote signals or barrier semaphores. Data moves between devices by JAX's collectives and lax.ppermute only.
A program may use at most 320 MiB of HBM per device.

```python
import math
import jax
import jax.numpy as jnp
from jax import lax

D = 2048
HEADS = 8
KV = 4
HD = 256
FF = 8192
MB = 2
TOK_MB = 320
SEQ = 2560


def draw_segments(key, part):
    positions = jnp.arange(SEQ, dtype=jnp.int32)
    extra_starts = TOK_MB // 8
    collected = []
    for micro_index in range(MB):
        sub_key = jax.random.fold_in(key, 7 + micro_index)
        start_key, end_key, mark_key = jax.random.split(sub_key, 3)
        long_start = jax.random.randint(start_key, (), TOK_MB // 4, TOK_MB // 2 + 1)
        long_end = jax.random.randint(end_key, (), SEQ - TOK_MB // 2, SEQ - TOK_MB // 4 - 1)
        outside = ((positions < long_start) | (positions > long_end + 1)) & (positions > 0)
        random_part = jax.random.randint(mark_key, (SEQ,), 0, 16384)
        scores = jnp.where(outside, random_part * SEQ + positions, -1)
        unused, chosen = lax.top_k(scores, extra_starts)
        marked = jnp.zeros((SEQ,), jnp.int32).at[chosen].set(1)
        begins = (positions == long_start) | (positions == long_end + 1) | (marked == 1)
        collected.append(jnp.cumsum(begins.astype(jnp.int32)).astype(jnp.int32))
    return jnp.stack(collected)


def raised(entries, stream_key, source, target, parts, factor):
    def block_of(position):
        return (jnp.arange(entries.shape[position]) // (entries.shape[position] // parts)).reshape((-1,) + (1,) * (entries.ndim - 1 - position))

    near = jax.random.permutation(stream_key, parts)[block_of(target)]
    other_side = (block_of(target) + parts // 2) % parts
    return jnp.where((block_of(source) == near) | (block_of(source) == other_side), factor * entries, entries)


def shard_levels(key, dims, cuts, low, high):
    gain, own = 1.0, jax.random.fold_in(key, 6)
    for position, shards_of in cuts:
        steps = jnp.exp(jax.random.uniform(jax.random.fold_in(own, position), (shards_of,), jnp.float32, low / len(cuts), high / len(cuts)))
        gain = gain * jnp.repeat(steps, dims[position] // shards_of).reshape([-1 if axis == position else 1 for axis in range(len(dims))])
    return gain


def normal_values(key, dims, width, reach, shards=(), kind=jnp.bfloat16):
    level = shard_levels(key, dims, shards, -0.22, 0.18) if shards else 1.0
    values = jax.random.normal(key, dims, jnp.float32) * width * level
    return jnp.minimum(jnp.maximum(values, -reach), reach).astype(kind)


def heavy_noise(stream_key, shape, width, bound, pieces, heavy, kind=jnp.bfloat16):
    array = width * jax.random.normal(stream_key, shape, jnp.float32)
    if pieces:
        array = array * shard_levels(stream_key, shape, pieces, -0.22, 0.18)
    return jnp.clip(raised(array, jax.random.fold_in(stream_key, 3), *heavy), -bound, bound).astype(kind)


def setup_inputs(seed: int = 0) -> dict:
    key_list = jax.random.split(jax.random.key(seed), 13)
    return {
        "hidden_in": heavy_noise(key_list[0], (MB, SEQ, D), 1.0, 6.0, ((1, 32),), (1, 2, 32, 2.75)),
        "segments": draw_segments(jax.random.fold_in(key_list[12], 71), 0),
        "attn_gain": jnp.clip(1.0 + 0.1 * jax.random.normal(key_list[2], (D,), jnp.float32), 0.5, 1.5).astype(jnp.bfloat16),
        "query_weight": normal_values(key_list[3], (D, HEADS * HD), (D // 2) ** -0.5, 0.1875, ((0, 8), (1, 4))),
        "key_weight": normal_values(key_list[4], (D, KV * HD), D ** -0.5, 0.125, ((0, 8), (1, 4))),
        "value_weight": normal_values(key_list[5], (D, KV * HD), D ** -0.5, 0.125, ((0, 8), (1, 4))),
        "output_weight": normal_values(key_list[6], (HEADS * HD, D), (max(4, HEADS * HD * 64 // SEQ)) ** -0.5, 0.875, ((0, 4), (1, 8))),
        "mlp_gain": jnp.clip(1.0 + 0.1 * jax.random.normal(key_list[7], (D,), jnp.float32), 0.5, 1.5).astype(jnp.bfloat16),
        "gate_weight": normal_values(key_list[8], (D, FF), D ** -0.5, 0.125, ((0, 8), (1, 4))),
        "up_weight": normal_values(key_list[9], (D, FF), D ** -0.5, 0.125, ((0, 8), (1, 4))),
        "down_weight": normal_values(key_list[10], (FF, D), FF ** -0.5, 0.0625, ((0, 4), (1, 8))),
        "cotangent": heavy_noise(key_list[11], (MB, SEQ, D), 1.0, 6.0, ((1, 32),), (1, 2, 32, 2.75)),
    }


EPSILON = 1e-06
ROPE_BASE = 1000042.0
MASKED = -1e+30

@jax.custom_vjp
def low(v):
    return lax.optimization_barrier(v.astype(jnp.bfloat16)).astype(jnp.float32)

@jax.custom_vjp
def low_back(v):
    return v

def low_keep(v):
    return (low(v), None)

def low_pass(kept, grad):
    return (grad,)

def back_keep(v):
    return (v, None)

def back_low(kept, grad):
    return (low(grad),)
low.defvjp(low_keep, low_pass)
low_back.defvjp(back_keep, back_low)

def matmul_high(left, right):
    return jnp.dot(left, right, precision=lax.Precision.HIGHEST, preferred_element_type=jnp.float32)

def norm_rows(values):
    return values * lax.rsqrt(lax.optimization_barrier(jnp.mean(values * values, axis=-1, keepdims=True)) + EPSILON)

def rotary(vectors, positions):
    depth = vectors.shape[-1]
    half_depth = depth // 2
    freqs = jnp.exp(-math.log(ROPE_BASE) * (2.0 * jnp.arange(half_depth, dtype=jnp.float32) / depth))
    angles = positions.astype(jnp.float32)[:, None] * freqs[None, :]
    cosines = jnp.cos(angles)[:, None, :]
    sines = jnp.sin(angles)[:, None, :]
    first_half = vectors[..., :half_depth]
    second_half = vectors[..., half_depth:]
    return jnp.concatenate([first_half * cosines - second_half * sines, second_half * cosines + first_half * sines], axis=-1)

def score_block(query_block, row_positions, row_segments, keys_all, values_all, segments_row):
    length = keys_all.shape[0]
    scores = jnp.einsum('qhd,khd->hqk', query_block, keys_all, precision=lax.Precision.HIGHEST) * HD ** (-0.5)
    scores = low_back(scores)
    key_positions = jnp.arange(length, dtype=jnp.int32)
    allowed = (row_segments[:, None] == segments_row[None, :]) & (key_positions[None, :] <= row_positions[:, None])
    scores = jnp.where(allowed[None], scores, MASKED)
    peak = lax.optimization_barrier(jnp.max(scores, axis=-1, keepdims=True))
    exps = jnp.exp(scores - peak)
    probs = low(exps / lax.optimization_barrier(jnp.sum(exps, axis=-1, keepdims=True)))
    return jnp.einsum('hqk,khd->qhd', probs, values_all, precision=lax.Precision.HIGHEST)

def attention(queries, keys_rot, values, segments_row):
    length = queries.shape[0]
    group_size = HEADS // KV
    keys_all = jnp.repeat(keys_rot, group_size, axis=1)
    values_all = jnp.repeat(values, group_size, axis=1)
    block_rows = math.gcd(length, 512)
    blocks = length // block_rows
    positions = jnp.arange(length, dtype=jnp.int32)
    checked = jax.checkpoint(score_block)

    def one_block(block_inputs):
        query_block, row_positions, row_segments = block_inputs
        return checked(query_block, row_positions, row_segments, keys_all, values_all, segments_row)
    mixed_blocks = lax.map(one_block, (queries.reshape(blocks, block_rows, HEADS, HD), positions.reshape(blocks, block_rows), segments_row.reshape(blocks, block_rows)))
    return mixed_blocks.reshape(length, HEADS * HD)

def block_layer(inputs_row, segments_row, params):
    attn_gain, query_weight, key_weight, value_weight, output_weight, mlp_gain, gate_weight, up_weight, down_weight = params
    length = inputs_row.shape[0]
    positions = jnp.arange(length, dtype=jnp.int32)
    normed = low(norm_rows(inputs_row) * attn_gain)
    queries = low_back(matmul_high(normed, query_weight)).reshape(length, HEADS, HD)
    keys_raw = low_back(matmul_high(normed, key_weight)).reshape(length, KV, HD)
    values = low(low_back(matmul_high(normed, value_weight))).reshape(length, KV, HD)
    queries = low(rotary(queries, positions))
    keys_rot = low(rotary(keys_raw, positions))
    mixed_heads = attention(queries, keys_rot, values, segments_row)
    mixed_heads = low(low_back(mixed_heads))
    hidden = inputs_row + low_back(matmul_high(mixed_heads, output_weight))
    normed2 = low(norm_rows(hidden) * mlp_gain)
    gate_proj = low_back(matmul_high(normed2, gate_weight))
    up_proj = low_back(matmul_high(normed2, up_weight))
    activated = low(gate_proj * jax.nn.sigmoid(gate_proj) * up_proj)
    return hidden + low_back(matmul_high(activated, down_weight))

def reference(hidden_in, segments, attn_gain, query_weight, key_weight, value_weight, output_weight, mlp_gain, gate_weight, up_weight, down_weight, cotangent):
    params = tuple((weight.astype(jnp.float32) for weight in (attn_gain, query_weight, key_weight, value_weight, output_weight, mlp_gain, gate_weight, up_weight, down_weight)))
    inputs_all = hidden_in.astype(jnp.float32)

    def forward(inputs_now, params_now):

        def scan_step(carry, pair_in):
            return (carry, jax.checkpoint(block_layer)(pair_in[0], pair_in[1], params_now))
        unused, results = lax.scan(scan_step, jnp.zeros((), jnp.float32), (inputs_now, segments))
        return results
    results, pullback = jax.vjp(forward, inputs_all, params)
    input_grad, grads = pullback(cotangent.astype(jnp.float32))
    return (results.astype(jnp.bfloat16), input_grad, grads[0], grads[1], grads[2], grads[3], grads[4], grads[5], grads[6], grads[7], grads[8])
```

```python
import math

import jax
import jax.numpy as jnp
from jax import lax
from jax.sharding import PartitionSpec as P

HD = 256
EPSILON = 1e-06
ROPE_BASE = 1000042.0
MASKED = -1e30
BF = jnp.bfloat16
F32 = jnp.float32
AXES = ("wide", "tp")

CORE, XDIR, YDIR, ZLOW = 1, 2, 4, 8
CONTRACT_ROWS = (((0,), (0,)), ((), ()))
CONTRACT_COLUMNS = (((1,), (1,)), ((), ()))


def mm(left, right):
    return jnp.dot(left, right, preferred_element_type=F32)


def mm_nt(left, right):
    return lax.dot_general(left, right, CONTRACT_COLUMNS, preferred_element_type=F32)


def mm_tn(left, right):
    return lax.dot_general(left, right, CONTRACT_ROWS, preferred_element_type=F32)


class Mover:
    def __init__(self, devices):
        self.devices = devices
        self.highs = devices // 16

    def swap(self, value, mask):
        return lax.ppermute(value, AXES, [(i, i ^ mask) for i in range(self.devices)])

    def from_high(self, value, shift, causal=False):
        pairs = []
        for dst in range(self.devices):
            zh = dst // 16
            src_zh = (zh + shift) % self.highs
            if causal and src_zh > zh:
                continue
            pairs.append((src_zh * 16 + dst % 16, dst))
        return lax.ppermute(value, AXES, pairs)

    def to_high(self, value, shift, causal=False):
        pairs = []
        for src in range(self.devices):
            zh = src // 16
            dst_zh = (zh + shift) % self.highs
            if causal and dst_zh > zh:
                continue
            pairs.append((src, dst_zh * 16 + src % 16))
        return lax.ppermute(value, AXES, pairs)


def gather_group(mover, rows):
    core = mover.swap(rows, CORE)
    across = mover.swap(rows, XDIR)
    low = mover.swap(rows, ZLOW)
    both = mover.swap(rows, XDIR | ZLOW)
    parts = [rows, core]
    for part in (across, low, both):
        parts += [part, mover.swap(part, CORE)]
    return jnp.concatenate(parts, axis=0)


def scatter_group(mover, partial):
    rows = partial.shape[0] // 8
    cut = partial.astype(BF).reshape(2, 2, 2, rows, partial.shape[1])
    got = mover.swap(cut[:, :, 1], CORE)
    both = cut[:, :, 0].astype(F32) + got.astype(F32)
    send = both.astype(BF)
    across = mover.swap(send[0, 1], XDIR)
    low = mover.swap(send[1, 0], ZLOW)
    diagonal = mover.swap(send[1, 1], XDIR | ZLOW)
    return both[0, 0] + across.astype(F32) + low.astype(F32) + diagonal.astype(F32)


def pair_order(zl, own, other):
    first = zl == 0
    return jnp.concatenate([jnp.where(first, own, other), jnp.where(first, other, own)], axis=0)


def gather_weight(mover, zl, keep, send):
    got = mover.swap(send, ZLOW)
    pair = pair_order(zl, keep, got)
    parts = [pair, mover.swap(pair, YDIR)]
    for shift in range(1, mover.highs):
        high = mover.from_high(pair, shift)
        parts += [high, mover.swap(high, YDIR)]
    return jnp.concatenate(parts, axis=0)


def scatter_weight(mover, zl, grad):
    highs = mover.highs
    columns = grad.shape[1]
    block = grad.shape[0] // (highs * 2)
    cut = grad.reshape(highs, 2, block, columns)
    got = mover.swap(cut[:, 1].astype(BF), YDIR)
    half = cut[:, 0].astype(F32) + got.astype(F32)
    total = half[0]
    for shift in range(1, highs):
        total = total + mover.to_high(half[shift].astype(BF), shift).astype(F32)
    total = total.reshape(2, block // 2, columns)
    first = zl == 0
    own = jnp.where(first, total[0], total[1])
    other = jnp.where(first, total[1], total[0])
    return own, mover.swap(other.astype(BF), ZLOW).astype(F32)


def halves(zl, array):
    c = array.shape[1] // 2
    left, right = array[:, :c], array[:, c:]
    first = zl == 0
    return jnp.where(first, left, right), jnp.where(first, right, left)


def join(zl, own, received):
    first = zl == 0
    return jnp.concatenate([jnp.where(first, own, received), jnp.where(first, received, own)], axis=1)


def to_group_order(zh, y, highs, rows):
    count, width = rows.shape
    cut = rows.reshape(count, highs, 2, 2, width // (4 * highs))
    parts = []
    for shift in range(highs):
        high = lax.dynamic_index_in_dim(cut, (zh + shift) % highs, 1, keepdims=False)
        for dy in range(2):
            parts.append(lax.dynamic_index_in_dim(high, y ^ dy, 2, keepdims=False))
    return jnp.stack(parts, axis=1).reshape(count, width)


def from_group_order(zh, y, highs, rows):
    count, width = rows.shape
    cut = rows.reshape(count, highs, 2, 2, width // (4 * highs))
    parts = []
    for high in range(highs):
        block = lax.dynamic_index_in_dim(cut, (high - zh) % highs, 1, keepdims=False)
        pieces = [lax.dynamic_index_in_dim(block, y ^ v, 1, keepdims=False) for v in range(2)]
        parts.append(jnp.stack(pieces, axis=2))
    return jnp.stack(parts, axis=1).reshape(count, width)


def rotate(vectors, cosines, sines):
    half = vectors.shape[-1] // 2
    a, b = vectors[..., :half], vectors[..., half:]
    return jnp.concatenate([a * cosines - b * sines, b * cosines + a * sines], axis=-1)


def attention_forward(queries, keys, values, lows, highs, key_positions, scale):
    scores = jnp.einsum("hqd,kd->hqk", queries, keys, preferred_element_type=F32) * scale
    allowed = (key_positions[None, :] >= lows[:, None]) & (key_positions[None, :] <= highs[:, None])
    scores = jnp.where(allowed[None], scores, MASKED)
    peak = jnp.max(scores, axis=-1, keepdims=True)
    exps = jnp.exp(scores - peak)
    total = jnp.sum(exps, axis=-1, keepdims=True)
    mixed = jnp.einsum("hqk,kd->hqd", exps.astype(BF), values, preferred_element_type=F32) / total
    return mixed, (peak + jnp.log(total))[..., 0]


def attention_backward(
    queries, keys, values, lows, highs, key_positions, scale, log_sums, back, delta
):
    scores = jnp.einsum("hqd,kd->hqk", queries, keys, preferred_element_type=F32) * scale
    allowed = (key_positions[None, :] >= lows[:, None]) & (key_positions[None, :] <= highs[:, None])
    probs = jnp.where(allowed[None], jnp.exp(scores - log_sums[..., None]), 0.0)
    prob_back = jnp.einsum("hqd,kd->hqk", back, values, preferred_element_type=F32)
    score_back = (probs * (prob_back - delta[..., None])).astype(BF)
    query_back = (
        jnp.einsum("hqk,kd->hqd", score_back, keys, preferred_element_type=F32) * scale
    )
    key_back = (
        jnp.einsum("hqk,hqd->kd", score_back, queries, preferred_element_type=F32) * scale
    )
    value_back = jnp.einsum("hqk,hqd->kd", probs.astype(BF), back, preferred_element_type=F32)
    return query_back, key_back, value_back


def body(
    hidden_in,
    segments,
    attn_gain,
    query_weight,
    key_weight,
    value_weight,
    output_weight,
    mlp_gain,
    gate_weight,
    up_weight,
    down_weight,
    cotangent,
):
    wide_count = lax.axis_size("wide")
    devices = wide_count * 4
    mover = Mover(devices)
    highs = mover.highs
    wide = lax.axis_index("wide")
    tp = lax.axis_index("tp")
    y, zl, zh = wide & 1, (wide >> 1) & 1, wide >> 2
    first = zl == 0
    micro, local, width = hidden_in.shape
    rows = micro * local
    wide_tokens = segments.shape[1]
    head_rows = 8 * local
    scale = HD ** (-0.5)

    inputs = to_group_order(zh, y, highs, hidden_in.reshape(rows, width).astype(F32))
    scale_one = lax.rsqrt(jnp.mean(inputs * inputs, axis=-1, keepdims=True) + EPSILON)
    plain_one = inputs * scale_one
    normed = gather_group(mover, plain_one.astype(BF))

    gain_one = attn_gain.astype(F32)[:, None]
    gain_two = mlp_gain.astype(F32)[:, None]

    def gained(weight, gain):
        return (weight.astype(F32) * gain).astype(BF)

    query_keep, query_send = halves(zl, gained(query_weight, gain_one))
    pair_weight = jnp.concatenate([key_weight, value_weight], axis=1)
    pair_keep, pair_send = halves(zl, gained(pair_weight, gain_one))
    qkv_full = gather_weight(
        mover,
        zl,
        jnp.concatenate([query_keep, pair_keep], axis=1),
        jnp.concatenate([query_send, pair_send], axis=1),
    )
    out_full = gather_weight(mover, zl, *halves(zl, output_weight.T))
    gate_keep, gate_send = halves(zl, gained(gate_weight, gain_two))
    up_keep, up_send = halves(zl, gained(up_weight, gain_two))
    hidden_units = gate_keep.shape[1]
    gate_up_full = gather_weight(
        mover,
        zl,
        jnp.concatenate([gate_keep, up_keep], axis=1),
        jnp.concatenate([gate_send, up_send], axis=1),
    )
    down_full = gather_weight(mover, zl, *halves(zl, down_weight.T))
    upstream = to_group_order(zh, y, highs, cotangent.reshape(rows, width))
    upstream_all = gather_group(mover, upstream)

    span = jnp.arange(local, dtype=jnp.int32)
    steps = jnp.arange(4, dtype=jnp.int32)
    within = (
        ((zl ^ jnp.arange(2, dtype=jnp.int32))[:, None, None] * 2 * wide_tokens)
        + ((tp ^ steps) * local)[None, :, None]
        + span[None, None, :]
    ).reshape(head_rows)
    row_positions = (zh * 4 + y) * wide_tokens + within
    key_positions = jnp.concatenate(
        [
            (((zh + shift) % highs) * 4 + (y ^ dy)) * wide_tokens + within
            for shift in range(highs)
            for dy in range(2)
        ]
    )
    seg_pair = pair_order(zl, segments[None], mover.swap(segments, ZLOW)[None])
    seg_parts = [seg_pair, mover.swap(seg_pair, YDIR)]
    for shift in range(1, highs):
        high = mover.from_high(seg_pair, shift)
        seg_parts += [high, mover.swap(high, YDIR)]
    seg_all = lax.dynamic_index_in_dim(jnp.stack(seg_parts), zl, 2, keepdims=False)
    own_pair = lax.dynamic_index_in_dim(seg_pair, zl, 1, keepdims=False)
    own_rows = jnp.stack(
        [
            lax.dynamic_slice_in_dim(
                lax.dynamic_index_in_dim(own_pair, zl ^ dzl, 0, keepdims=False),
                (tp ^ dtp) * local,
                local,
                0,
            )
            for dzl in range(2)
            for dtp in range(4)
        ]
    ).reshape(head_rows)
    doc_starts = jnp.sum(
        (seg_all.reshape(1, -1) < own_rows[:, None]).astype(jnp.int32), axis=1
    )

    freqs = jnp.exp(-math.log(ROPE_BASE) * (2.0 * jnp.arange(HD // 2, dtype=F32) / HD))
    angles = row_positions.astype(F32)[:, None] * freqs[None, :]
    cosines, sines = jnp.cos(angles), jnp.sin(angles)

    projected = mm(normed, qkv_full).reshape(8, micro, local, 2 * HD)
    table_c = cosines.reshape(8, 1, local, HD // 2)
    table_s = sines.reshape(8, 1, local, HD // 2)
    queries_own = rotate(projected[..., :HD], table_c, table_s)
    pairs_own = rotate(
        projected[..., HD:], jnp.where(first, table_c, 1.0), jnp.where(first, table_s, 0.0)
    )
    turned = jnp.concatenate([queries_own, pairs_own], axis=-1).astype(BF)

    def swap_micro(array):
        mine = jnp.where(first, array[:, 0], array[:, 1])
        away = jnp.where(first, array[:, 1], array[:, 0])
        got = mover.swap(away, ZLOW)
        got = jnp.concatenate([got[4:], got[:4]], axis=0)
        return mine.reshape(head_rows, -1), got.reshape(head_rows, -1)

    def unswap_micro(mine, away):
        away = away.reshape(8, local, -1)
        away = jnp.concatenate([away[4:], away[:4]], axis=0)
        got = mover.swap(away, ZLOW)
        mine = mine.reshape(8, local, -1)
        return jnp.stack([jnp.where(first, mine, got), jnp.where(first, got, mine)], axis=1)

    mine, got = swap_micro(turned)
    queries = jnp.stack([mine[:, :HD], got[:, :HD]])
    pair = jnp.concatenate(
        [
            jnp.where(first, mine[:, HD:], got[:, HD:]),
            jnp.where(first, got[:, HD:], mine[:, HD:]),
        ],
        axis=1,
    )
    pair_parts = [pair, mover.swap(pair, YDIR)]
    for shift in range(1, highs):
        high = mover.from_high(pair, shift, causal=True)
        pair_parts += [high, mover.swap(high, YDIR)]
    pair_all = jnp.concatenate(pair_parts, axis=0)
    keys, values = pair_all[:, :HD], pair_all[:, HD:]

    mixed, log_sums = attention_forward(
        queries, keys, values, doc_starts, row_positions, key_positions, scale
    )
    mixed_low = mixed.astype(BF)
    mixed_all = unswap_micro(mixed_low[0], mixed_low[1]).reshape(8 * rows, HD)

    hidden = inputs + scatter_group(mover, mm_nt(mixed_all, out_full))
    scale_two = lax.rsqrt(jnp.mean(hidden * hidden, axis=-1, keepdims=True) + EPSILON)
    plain_two = hidden * scale_two
    normed_two = gather_group(mover, plain_two.astype(BF))
    gate_up = mm(normed_two, gate_up_full)
    gate_proj, up_proj = gate_up[:, :hidden_units], gate_up[:, hidden_units:]
    sigmoid = jax.nn.sigmoid(gate_proj)
    silu = gate_proj * sigmoid
    activated = (silu * up_proj).astype(BF)
    layer_out = hidden + scatter_group(mover, mm_nt(activated, down_full))

    act_back = mm(upstream_all, down_full)
    down_grad = mm_tn(upstream_all, activated)
    gate_back = act_back * up_proj * (sigmoid * (1.0 + gate_proj * (1.0 - sigmoid)))
    up_back = act_back * silu
    gate_up_back = jnp.concatenate([gate_back.astype(BF), up_back.astype(BF)], axis=1)
    weighted_two = scatter_group(mover, mm_nt(gate_up_back, gate_up_full))
    gate_up_grad = mm_tn(normed_two, gate_up_back)
    hidden_back = upstream.astype(F32) + scale_two * (
        weighted_two - plain_two * jnp.mean(weighted_two * plain_two, axis=-1, keepdims=True)
    )

    attn_back = gather_group(mover, hidden_back.astype(BF))
    mixed_back = mm(attn_back, out_full).astype(BF)
    out_grad = mm_tn(attn_back, mixed_all)
    mine, got = swap_micro(mixed_back.reshape(8, micro, local, HD))
    back = jnp.stack([mine, got])
    delta = jnp.sum(back.astype(F32) * mixed, axis=-1)
    query_back, key_back, value_back = attention_backward(
        queries, keys, values, doc_starts, row_positions, key_positions, scale, log_sums, back,
        delta,
    )
    pair_back = jnp.concatenate([key_back, value_back], axis=1).reshape(
        highs, 2, head_rows, 2 * HD
    )
    got = mover.swap(pair_back[:, 1].astype(BF), YDIR)
    half = pair_back[:, 0] + got.astype(F32)
    total = half[0]
    for shift in range(1, highs):
        total = total + mover.to_high(half[shift].astype(BF), shift, causal=True).astype(F32)
    key_back = rotate(total[:, :HD], cosines, -sines).astype(BF)
    value_back = total[:, HD:].astype(BF)
    query_back = rotate(query_back, cosines[None], -sines[None]).astype(BF)
    mine = jnp.concatenate([query_back[0], jnp.where(first, key_back, value_back)], axis=1)
    away = jnp.concatenate([query_back[1], jnp.where(first, value_back, key_back)], axis=1)
    qkv_back = unswap_micro(mine, away).reshape(8 * rows, 2 * HD)
    weighted_one = scatter_group(mover, mm_nt(qkv_back, qkv_full))
    qkv_grad = mm_tn(normed, qkv_back)
    input_grad = hidden_back + scale_one * (
        weighted_one - plain_one * jnp.mean(weighted_one * plain_one, axis=-1, keepdims=True)
    )

    down_own, down_got = scatter_weight(mover, zl, down_grad)
    down_shard = join(zl, down_own, down_got).T
    own, got = scatter_weight(mover, zl, gate_up_grad)
    gate_plain = join(zl, own[:, :hidden_units], got[:, :hidden_units])
    up_plain = join(zl, own[:, hidden_units:], got[:, hidden_units:])
    out_own, out_got = scatter_weight(mover, zl, out_grad)
    out_shard = join(zl, out_own, out_got).T
    own, got = scatter_weight(mover, zl, qkv_grad)
    query_plain = join(zl, own[:, :HD], got[:, :HD])
    pair_plain = join(zl, own[:, HD:], got[:, HD:])
    gain_sums = jnp.stack(
        [
            jnp.sum(query_plain * query_weight.astype(F32), axis=1)
            + jnp.sum(pair_plain * pair_weight.astype(F32), axis=1),
            jnp.sum(gate_plain * gate_weight.astype(F32), axis=1)
            + jnp.sum(up_plain * up_weight.astype(F32), axis=1),
        ]
    )
    gain_sums = gain_sums + mover.swap(gain_sums, CORE)
    gain_sums = gain_sums + mover.swap(gain_sums, XDIR)
    pair_shard = pair_plain * gain_one
    shape = hidden_in.shape
    return (
        from_group_order(zh, y, highs, layer_out).astype(BF).reshape(shape),
        from_group_order(zh, y, highs, input_grad).reshape(shape),
        gain_sums[0],
        query_plain * gain_one,
        pair_shard[:, :HD],
        pair_shard[:, HD:],
        out_shard,
        gain_sums[1],
        gate_plain * gain_two,
        up_plain * gain_two,
        down_shard,
    )


def solution(mesh):
    rows = P(None, ("wide", "tp"), None)
    columns = P("wide", "tp")
    flipped = P("tp", "wide")
    gain = P("wide")
    return jax.shard_map(
        body,
        mesh=mesh,
        in_specs=(
            rows,
            P(None, "wide"),
            gain,
            columns,
            columns,
            columns,
            flipped,
            gain,
            columns,
            columns,
            flipped,
            rows,
        ),
        out_specs=(
            rows,
            rows,
            gain,
            columns,
            columns,
            columns,
            flipped,
            gain,
            columns,
            columns,
            flipped,
        ),
        check_vma=False,
    )
```

```python
import functools
import math

import jax
import jax.numpy as jnp
from jax import lax
from jax.experimental import pallas as pl
from jax.experimental.pallas import tpu as pltpu
from jax.sharding import PartitionSpec as P

HD = 256
EPSILON = 1e-06
ROPE_BASE = 1000042.0
MASKED = -1e30
BF = jnp.bfloat16
F32 = jnp.float32
AXES = ("wide", "tp")
VMEM_LIMIT = 56 << 20

CORE, XDIR, YDIR, ZLOW = 1, 2, 4, 8
CONTRACT_ROWS = (((0,), (0,)), ((), ()))
CONTRACT_COLUMNS = (((1,), (1,)), ((), ()))


def mm(left, right):
    return jnp.dot(left, right, preferred_element_type=F32)


def mm_nt(left, right):
    return lax.dot_general(left, right, CONTRACT_COLUMNS, preferred_element_type=F32)


def mm_tn(left, right):
    return lax.dot_general(left, right, CONTRACT_ROWS, preferred_element_type=F32)


ANY = pl.BlockSpec(memory_space=pl.ANY)
WHOLE = pl.BlockSpec(memory_space=pltpu.VMEM)
SCALARS = pl.BlockSpec(memory_space=pltpu.SMEM)


def params(*semantics):
    return pltpu.CompilerParams(
        dimension_semantics=semantics or None, vmem_limit_bytes=VMEM_LIMIT
    )


def cost(flops, *arrays):
    moved = sum(math.prod(a.shape) * jnp.dtype(a.dtype).itemsize for a in arrays)
    return pl.CostEstimate(flops=2 * int(flops), transcendentals=0, bytes_accessed=int(moved))


class Mover:
    def __init__(self, devices):
        self.devices = devices
        self.highs = devices // 16

    def swap(self, value, mask):
        return lax.ppermute(value, AXES, [(i, i ^ mask) for i in range(self.devices)])

    def from_high(self, value, shift, causal=False):
        pairs = []
        for dst in range(self.devices):
            zh = dst // 16
            src_zh = (zh + shift) % self.highs
            if causal and src_zh > zh:
                continue
            pairs.append((src_zh * 16 + dst % 16, dst))
        return lax.ppermute(value, AXES, pairs)

    def to_high(self, value, shift, causal=False):
        pairs = []
        for src in range(self.devices):
            zh = src // 16
            dst_zh = (zh + shift) % self.highs
            if causal and dst_zh > zh:
                continue
            pairs.append((src, dst_zh * 16 + src % 16))
        return lax.ppermute(value, AXES, pairs)


def gathered_kernel(rotary, parts, flags, *refs):
    chunks, refs = refs[:8], refs[8:]
    weights, refs = refs[:parts], refs[parts:]
    if rotary:
        cos_ref, sin_ref = refs[:2]
        refs = refs[2:]
    all_ref, mine_ref, away_ref, rows_buf, weight_buf, sems, out_sem = refs
    rows = chunks[0].shape[0]
    local = rows // 2
    depth = weights[0].shape[0]
    loads = []
    for p in range(parts):
        loads.append(
            pltpu.make_async_copy(
                weights[p], weight_buf.at[pl.ds(p * depth, depth)], sems.at[8 + p]
            )
        )
    for k in range(8):
        loads.append(
            pltpu.make_async_copy(chunks[k], rows_buf.at[pl.ds(k * rows, rows)], sems.at[k])
        )
    for load in loads:
        load.start()
    for p in range(parts):
        loads[p].wait()
    first = flags[0] == 0
    for pair in range(4):
        loads[parts + 2 * pair].wait()
        loads[parts + 2 * pair + 1].wait()
        product = mm(rows_buf[pl.ds(pair * 2 * rows, 2 * rows), :], weight_buf[...])
        for half in range(2):
            k = 2 * pair + half
            out = []
            for m in range(2):
                start = half * rows + m * local
                piece = product[start : start + local]
                if rotary:
                    c = cos_ref[k * local : (k + 1) * local, :]
                    s = sin_ref[k * local : (k + 1) * local, :]
                    a, b, e, f = (
                        piece[:, :128],
                        piece[:, 128:256],
                        piece[:, 256:384],
                        piece[:, 384:512],
                    )
                    ck = jnp.where(first, c, 1.0)
                    sk = jnp.where(first, s, 0.0)
                    piece = jnp.concatenate(
                        [a * c - b * s, b * c + a * s, e * ck - f * sk, f * ck + e * sk], axis=1
                    )
                out.append(piece)
            mine_ref[k * local : (k + 1) * local, :] = jnp.where(first, out[0], out[1]).astype(BF)
            swapped = (k + 4) % 8
            away_ref[swapped * local : (swapped + 1) * local, :] = jnp.where(
                first, out[1], out[0]
            ).astype(BF)
    store = pltpu.make_async_copy(rows_buf, all_ref, out_sem)
    store.start()
    store.wait()


def gathered_matmul(flags, chunks, parts, tables=None):
    rows, width = chunks[0].shape
    columns = parts[0].shape[1]
    half_rows = 4 * rows
    tables = tables or ()
    return pl.pallas_call(
        functools.partial(gathered_kernel, bool(tables), len(parts)),
        out_shape=(
            jax.ShapeDtypeStruct((8 * rows, width), BF),
            jax.ShapeDtypeStruct((half_rows, columns), BF),
            jax.ShapeDtypeStruct((half_rows, columns), BF),
        ),
        in_specs=[SCALARS] + [ANY] * (8 + len(parts)) + [WHOLE] * len(tables),
        out_specs=(ANY, WHOLE, WHOLE),
        scratch_shapes=[
            pltpu.VMEM((8 * rows, width), BF),
            pltpu.VMEM((width, columns), BF),
            pltpu.SemaphoreType.DMA((8 + len(parts),)),
            pltpu.SemaphoreType.DMA,
        ],
        compiler_params=params(),
        cost_estimate=cost(2 * 8 * rows * width * columns, *chunks, *chunks, *parts),
        name="gathered_matmul",
    )(flags, *chunks, *parts, *tables)


def partial_kernel(counts, offsets, parts, *refs):
    lefts, refs = refs[:counts], refs[counts:]
    groups = [refs[i * parts : (i + 1) * parts] for i in range(counts)]
    keep_ref, send_ref = refs[counts * parts :]
    rows = keep_ref.shape[1]
    depth = groups[0][0].shape[0]
    for p in range(parts):
        total = None
        for left, group, start in zip(lefts, groups, offsets):
            term = mm_nt(left[...], group[p][:, start : start + left.shape[1]])
            total = term if total is None else total + term
        low = total.astype(BF)
        keep_ref[0, :, p * depth : (p + 1) * depth] = low[:rows]
        send_ref[0, :, p * depth : (p + 1) * depth] = low[rows:]


def partial_matmul(lefts, groups, offsets):
    rows = lefts[0].shape[0] // 8
    parts = len(groups[0])
    width = groups[0][0].shape[0] * parts
    out = jax.ShapeDtypeStruct((4, rows, width), BF)
    block = pl.BlockSpec((1, rows, width), lambda j: (j, 0, 0))
    flat = [part for group in groups for part in group]
    return pl.pallas_call(
        functools.partial(partial_kernel, len(lefts), tuple(offsets), parts),
        out_shape=(out, out),
        grid=(4,),
        in_specs=[pl.BlockSpec((2 * rows, left.shape[1]), lambda j: (j, 0)) for left in lefts]
        + [
            pl.BlockSpec(part.shape, lambda j: (0, 0), pipeline_mode=pl.Buffered(1))
            for part in flat
        ],
        out_specs=(block, block),
        compiler_params=params("arbitrary"),
        cost_estimate=cost(
            sum(2 * 8 * rows * width * left.shape[1] for left in lefts), *lefts, *flat, out, out
        ),
        name="partial_matmul",
    )(*lefts, *flat)


def combine_kernel(keep, got, own, across, low, diagonal):
    own[...] = keep[0].astype(F32) + got[0].astype(F32)
    for j, out in ((1, across), (2, low), (3, diagonal)):
        out[...] = (keep[j].astype(F32) + got[j].astype(F32)).astype(BF)


def combine(keep, got):
    _, rows, width = keep.shape
    tile = 32 if rows % 32 == 0 else rows
    wide = pl.BlockSpec((4, tile, width), lambda i: (0, i, 0))
    thin = pl.BlockSpec((tile, width), lambda i: (i, 0))
    return pl.pallas_call(
        combine_kernel,
        out_shape=(jax.ShapeDtypeStruct((rows, width), F32),)
        + (jax.ShapeDtypeStruct((rows, width), BF),) * 3,
        grid=(rows // tile,),
        in_specs=[wide, wide],
        out_specs=(thin,) * 4,
        compiler_params=params("arbitrary"),
        cost_estimate=cost(0, keep, keep, got, got),
        name="combine",
    )(keep, got)


def assemble_kernel(*refs):
    chunks, out, sems = refs[:8], refs[8], refs[9]
    rows = chunks[0].shape[0]
    copies = [
        pltpu.make_async_copy(chunks[k], out.at[pl.ds(k * rows, rows)], sems.at[k])
        for k in range(8)
    ]
    for copy in copies:
        copy.start()
    for copy in copies:
        copy.wait()


def assemble(chunks):
    rows, width = chunks[0].shape
    return pl.pallas_call(
        assemble_kernel,
        out_shape=jax.ShapeDtypeStruct((8 * rows, width), BF),
        in_specs=[ANY] * 8,
        out_specs=WHOLE,
        scratch_shapes=[pltpu.SemaphoreType.DMA((8,))],
        compiler_params=params(),
        cost_estimate=cost(0, *chunks, *chunks),
        name="assemble",
    )(*chunks)


def hidden_kernel(parts, x_ref, dy_ref, *refs):
    weights, refs = refs[:parts], refs[parts:]
    back_ref, activated = refs
    depth = weights[0].shape[0]
    units = activated.shape[1]

    def product(left, start):
        out = None
        for p in range(parts):
            term = mm(
                left[:, p * depth : (p + 1) * depth], weights[p][:, start : start + units]
            )
            out = term if out is None else out + term
        return out

    gate = product(x_ref, 0)
    lift = product(x_ref, units)
    back = product(dy_ref, 2 * units)
    sigmoid = 1.0 / (1.0 + jnp.exp(-gate))
    silu = gate * sigmoid
    activated[...] = (silu * lift).astype(BF)
    back_ref[:, units:] = (back * silu).astype(BF)
    back_ref[:, :units] = (back * lift * (sigmoid * (1.0 + gate * (1.0 - sigmoid)))).astype(BF)


def hidden_units(x_all, dy_all, weights):
    total, width = x_all.shape
    depth, columns = weights[0].shape
    units = columns // 3
    tile = 256 if total % 256 == 0 else total
    rows = pl.BlockSpec((tile, width), lambda i: (i, 0))
    return pl.pallas_call(
        functools.partial(hidden_kernel, len(weights)),
        out_shape=(
            jax.ShapeDtypeStruct((total, 2 * units), BF),
            jax.ShapeDtypeStruct((total, units), BF),
        ),
        grid=(total // tile,),
        in_specs=[rows, rows]
        + [
            pl.BlockSpec((depth, columns), lambda i: (0, 0), pipeline_mode=pl.Buffered(1))
            for _ in weights
        ],
        out_specs=(
            pl.BlockSpec((tile, 2 * units), lambda i: (i, 0)),
            pl.BlockSpec((tile, units), lambda i: (i, 0)),
        ),
        compiler_params=params("arbitrary"),
        cost_estimate=cost(2 * total * width * columns, x_all, dy_all, *weights),
        name="hidden_units",
    )(x_all, dy_all, *weights)


def unit_grads_kernel(x_ref, dy_ref, back_ref, act_ref, keep_ref, send_ref):
    units = act_ref.shape[1]

    def fill(out):
        out[0, :, : 2 * units] = mm_tn(x_ref[...], back_ref[...]).astype(BF)
        out[0, :, 2 * units :] = mm_tn(dy_ref[...], act_ref[...]).astype(BF)

    @pl.when(pl.program_id(0) % 2 == 0)
    def _():
        fill(keep_ref)

    @pl.when(pl.program_id(0) % 2 == 1)
    def _():
        fill(send_ref)


def unit_grads(x_all, dy_all, back, act, highs):
    total, width = x_all.shape
    depth = width // (2 * highs)
    columns = back.shape[1] + act.shape[1]
    out = jax.ShapeDtypeStruct((highs, depth, columns), BF)
    block = pl.BlockSpec((1, depth, columns), lambda p: (p // 2, 0, 0))
    rows = pl.BlockSpec((total, depth), lambda p: (0, p))
    return pl.pallas_call(
        unit_grads_kernel,
        out_shape=(out, out),
        grid=(2 * highs,),
        in_specs=[
            rows,
            rows,
            pl.BlockSpec(back.shape, lambda p: (0, 0), pipeline_mode=pl.Buffered(1)),
            pl.BlockSpec(act.shape, lambda p: (0, 0), pipeline_mode=pl.Buffered(1)),
        ],
        out_specs=(block, block),
        compiler_params=params("arbitrary"),
        cost_estimate=cost(2 * total * width * columns, x_all, dy_all, out, out),
        name="unit_grads",
    )(x_all, dy_all, back, act)


def block_of(i, count, flags):
    return jnp.where(i < 2, i, count - 2 * flags[1] + i - 2)


def attend_kernel(parts, flags, bases, mine, got, *refs):
    pairs, refs = refs[:parts], refs[parts:]
    lows, ends, within, mixed, log_sums, own, away, pair_buf, sems = refs
    count = mine.shape[0]
    half = count // 2
    loads = []
    for p in range(parts):
        loads.append(pltpu.make_async_copy(pairs[p], pair_buf.at[p], sems.at[p]))
    for load in loads:
        load.start()
    for load in loads:
        load.wait()
    needed = 2 + 2 * flags[1]
    for head, source in enumerate((mine, got)):
        for side in range(2):
            place = slice(side * half, (side + 1) * half)
            query = source[place, :HD] * jnp.asarray(HD ** (-0.5), BF)
            low, end = lows[place, :], ends[place, :]

            def step(i, carry):
                peak, total, accum = carry
                b = block_of(i, parts, flags)
                scores = mm_nt(query, pair_buf[b, :, :HD])
                position = within[...] + bases[b]
                allowed = (position >= low) & (position <= end)
                scores = jnp.where(allowed, scores, MASKED)
                new_peak = jnp.maximum(peak, jnp.max(scores, axis=1, keepdims=True))
                decay = jnp.exp(peak - new_peak)
                probs = jnp.where(allowed, jnp.exp(scores - new_peak), 0.0)
                total = decay * total + jnp.sum(probs, axis=1, keepdims=True)
                accum = decay * accum + mm(probs.astype(BF), pair_buf[b, :, HD:])
                return new_peak, total, accum

            peak, total, accum = lax.fori_loop(
                0,
                needed,
                step,
                (
                    jnp.full((half, 1), MASKED, F32),
                    jnp.zeros((half, 1), F32),
                    jnp.zeros((half, HD), F32),
                ),
            )
            out = accum / total
            mixed[head, place, :] = out
            log_sums[head, place, :] = peak + jnp.log(total)
            if head == 0:
                own[place, :] = out.astype(BF)
            else:
                away[(1 - side) * half : (2 - side) * half, :] = out.astype(BF)


def attend(flags, bases, mine, got, pairs, lows, ends, within):
    count = mine.shape[0]
    parts = len(pairs)
    low = jax.ShapeDtypeStruct((count, HD), BF)
    mixed_shape = jax.ShapeDtypeStruct((2, count, HD), F32)
    return pl.pallas_call(
        functools.partial(attend_kernel, parts),
        out_shape=(
            mixed_shape,
            jax.ShapeDtypeStruct((2, count, 1), F32),
            low,
            low,
        ),
        in_specs=[SCALARS, SCALARS, WHOLE, WHOLE] + [ANY] * parts + [WHOLE] * 3,
        out_specs=(WHOLE,) * 4,
        scratch_shapes=[
            pltpu.VMEM((parts, count, 2 * HD), BF),
            pltpu.SemaphoreType.DMA((parts,)),
        ],
        compiler_params=params(),
        cost_estimate=cost(16 * count * count * parts * HD, mixed_shape),
        name="attend",
    )(flags, bases, mine, got, *pairs, lows, ends, within)


def attend_back_kernel(parts, flags, bases, mine, got, back_mine, back_got, *refs):
    pairs, refs = refs[:parts], refs[parts:]
    lows, ends, within, stats, deltas, cos_ref, sin_ref = refs[:7]
    keep, send, own, away, pair_buf, query_sum, pair_sum, sems, out_sems = refs[7:]
    count = mine.shape[0]
    half = count // 2
    scale = HD ** (-0.5)
    loads = []
    for p in range(parts):
        loads.append(pltpu.make_async_copy(pairs[p], pair_buf.at[p], sems.at[p]))
    for load in loads:
        load.start()
    query_sum[...] = jnp.zeros_like(query_sum)
    for load in loads:
        load.wait()

    def step(i, carry):
        b = block_of(i, parts, flags)
        keys, values = pair_buf[b, :, :HD], pair_buf[b, :, HD:]
        position = within[...] + bases[b]
        key_back = jnp.zeros((count, HD), F32)
        value_back = jnp.zeros((count, HD), F32)
        for head, (source, backs) in enumerate(((mine, back_mine), (got, back_got))):
            for side in range(2):
                place = slice(side * half, (side + 1) * half)
                query = source[place, :HD] * jnp.asarray(scale, BF)
                back = backs[place, :]
                scores = mm_nt(keys, query)
                allowed = (position >= lows[:, place]) & (position <= ends[:, place])
                probs = jnp.where(
                    allowed, jnp.exp(scores - stats[head : head + 1, place]), 0.0
                )
                prob_back = mm_nt(values, back)
                score_back = (probs * (prob_back - deltas[head : head + 1, place])).astype(BF)
                value_back = value_back + mm(probs.astype(BF), back)
                key_back = key_back + mm(score_back, query)
                query_sum[head, place, :] += mm_tn(score_back, keys)
        pair_sum[:, :HD] = key_back.astype(BF)
        pair_sum[:, HD:] = value_back.astype(BF)
        dest = b // 2

        @pl.when(b % 2 == 0)
        def _():
            store = pltpu.make_async_copy(pair_sum, keep.at[dest], out_sems.at[0])
            store.start()
            store.wait()

        @pl.when(b % 2 == 1)
        def _():
            store = pltpu.make_async_copy(pair_sum, send.at[dest], out_sems.at[1])
            store.start()
            store.wait()

        return carry

    lax.fori_loop(0, 2 + 2 * flags[1], step, 0)
    for head in range(2):
        for side in range(2):
            place = slice(side * half, (side + 1) * half)
            grad = query_sum[head, place, :] * scale
            c, s = cos_ref[place, :], sin_ref[place, :]
            a, b = grad[:, : HD // 2], grad[:, HD // 2 :]
            turned = jnp.concatenate([a * c + b * s, b * c - a * s], axis=1).astype(BF)
            if head == 0:
                own[place, :] = turned
            else:
                away[(1 - side) * half : (2 - side) * half, :] = turned


def attend_back(
    flags, bases, mine, got, back_mine, back_got, pairs, lows, ends, within, stats, deltas, tables
):
    count = mine.shape[0]
    parts = len(pairs)
    low = jax.ShapeDtypeStruct((count, HD), BF)
    grad = jax.ShapeDtypeStruct((parts // 2, count, 2 * HD), BF)
    return pl.pallas_call(
        functools.partial(attend_back_kernel, parts),
        out_shape=(grad, grad, low, low),
        in_specs=[SCALARS, SCALARS] + [WHOLE] * 4 + [ANY] * parts + [WHOLE] * 7,
        out_specs=(ANY, ANY, WHOLE, WHOLE),
        scratch_shapes=[
            pltpu.VMEM((parts, count, 2 * HD), BF),
            pltpu.VMEM((2, count, HD), F32),
            pltpu.VMEM((count, 2 * HD), BF),
            pltpu.SemaphoreType.DMA((parts,)),
            pltpu.SemaphoreType.DMA((2,)),
        ],
        compiler_params=params(),
        cost_estimate=cost(20 * count * count * parts * HD, grad, grad),
        name="attend_back",
    )(
        flags, bases, mine, got, back_mine, back_got, *pairs, lows, ends, within, stats, deltas,
        *tables,
    )


def tie(*values):
    return lax.optimization_barrier(values)


def halves(zl, array):
    c = array.shape[1] // 2
    left, right = array[:, :c], array[:, c:]
    first = zl == 0
    return jnp.where(first, left, right), jnp.where(first, right, left)


def join(zl, own, received):
    first = zl == 0
    return jnp.concatenate([jnp.where(first, own, received), jnp.where(first, received, own)], axis=1)


def to_group_order(zh, y, highs, rows):
    width = rows.shape[1]
    f = width // (4 * highs)
    parts = []
    for shift in range(highs):
        for dy in range(2):
            for low in range(2):
                start = ((((zh + shift) % highs) * 2 + low) * 2 + (y ^ dy)) * f
                parts.append(lax.dynamic_slice_in_dim(rows, start, f, 1))
    return jnp.concatenate(parts, axis=1)


def from_group_order(zh, y, highs, rows):
    width = rows.shape[1]
    f = width // (4 * highs)
    parts = []
    for high in range(highs):
        for low in range(2):
            for v in range(2):
                start = ((((high - zh) % highs) * 2 + (y ^ v)) * 2 + low) * f
                parts.append(lax.dynamic_slice_in_dim(rows, start, f, 1))
    return jnp.concatenate(parts, axis=1)


def turn_back(vectors, cosines, sines):
    half = vectors.shape[-1] // 2
    a, b = vectors[..., :half], vectors[..., half:]
    return jnp.concatenate([a * cosines + b * sines, b * cosines - a * sines], axis=-1)


def body(
    hidden_in,
    segments,
    attn_gain,
    query_weight,
    key_weight,
    value_weight,
    output_weight,
    mlp_gain,
    gate_weight,
    up_weight,
    down_weight,
    cotangent,
):
    wide_count = lax.axis_size("wide")
    devices = wide_count * 4
    mover = Mover(devices)
    highs = mover.highs
    wide = lax.axis_index("wide")
    tp = lax.axis_index("tp")
    y, zl, zh = wide & 1, (wide >> 1) & 1, wide >> 2
    first = zl == 0
    flags = jnp.stack([zl, zh]).astype(jnp.int32)
    micro, local, width = hidden_in.shape
    rows = micro * local
    wide_tokens = segments.shape[1]
    head_rows = 8 * local

    swap = mover.swap

    def pair_of(keep, got):
        return jnp.concatenate(
            [jnp.where(first, keep, got), jnp.where(first, got, keep)], axis=0
        )

    def highs_of(value, causal=False):
        return [mover.from_high(value, shift, causal) for shift in range(1, highs)]

    def with_other_y(own, other, high, high_other):
        parts = [own, other]
        for a, b in zip(high, high_other):
            parts += [a, b]
        return parts

    inputs = to_group_order(zh, y, highs, hidden_in.reshape(rows, width)).astype(F32)
    scale_one = lax.rsqrt(jnp.mean(inputs * inputs, axis=-1, keepdims=True) + EPSILON)
    plain_one = inputs * scale_one
    row = plain_one.astype(BF)
    upstream = to_group_order(zh, y, highs, cotangent.reshape(rows, width))

    gain_one = attn_gain.astype(F32)[:, None]
    gain_two = mlp_gain.astype(F32)[:, None]

    def gained(weight, gain):
        return (weight.astype(F32) * gain).astype(BF)

    query_keep, query_send = halves(zl, gained(query_weight, gain_one))
    pair_weight = jnp.concatenate([key_weight, value_weight], axis=1)
    pair_keep, pair_send = halves(zl, gained(pair_weight, gain_one))
    qkv_keep = jnp.concatenate([query_keep, pair_keep], axis=1)
    qkv_send = jnp.concatenate([query_send, pair_send], axis=1)
    out_keep, out_send = halves(zl, output_weight.T)
    gate_keep, gate_send = halves(zl, gained(gate_weight, gain_two))
    up_keep, up_send = halves(zl, gained(up_weight, gain_two))
    down_keep, down_send = halves(zl, down_weight.T)
    unit_tile = 256
    groups = gate_keep.shape[1] // unit_tile
    unit_keep, unit_send = [], []
    for c in range(groups):
        cut = slice(c * unit_tile, (c + 1) * unit_tile)
        unit_keep.append(
            jnp.concatenate([gate_keep[:, cut], up_keep[:, cut], down_keep[:, cut]], axis=1)
        )
        unit_send.append(
            jnp.concatenate([gate_send[:, cut], up_send[:, cut], down_send[:, cut]], axis=1)
        )

    live = {}

    def cut(*under_way):
        names = [name for name in live if name not in under_way]
        for name, value in zip(names, tie(*[live[name] for name in names])):
            live[name] = value

    def take(*names):
        return [live[name] for name in names]

    def drop(*names):
        return [live.pop(name) for name in names]

    def add_pair(name, keep):
        live["pair" + name] = pair_of(keep, live.pop("zl" + name))

    def start_zl(name, send):
        live["zl" + name] = swap(send, ZLOW)

    def start_y(name):
        live["y" + name] = swap(live["pair" + name], YDIR)

    def start_h(name, causal=False):
        live["h" + name] = highs_of(live["pair" + name], causal)

    def start_hy(name):
        live["hy" + name] = [swap(h, YDIR) for h in live["h" + name]]

    def parts_of(name):
        return with_other_y(*take("pair" + name, "y" + name, "h" + name, "hy" + name))

    def rows_first():
        live["rx"], live["rz"] = swap(live["row"], XDIR), swap(live["row"], ZLOW)

    def rows_second():
        live["rd"] = swap(live["rz"], XDIR)
        live["rc"] = [swap(live[n], CORE) for n in ("row", "rx", "rz")]

    def rows_last():
        row, x, z, d, c = drop("row", "rx", "rz", "rd", "rc")
        return [row, c[0], x, c[1], z, c[2], d, swap(d, CORE)]

    def sums_core(name):
        live["send" + name] = swap(live["send" + name], CORE)

    def sums_combine(name):
        live["sum" + name] = combine(*drop("keep" + name, "send" + name))

    def sums_far(name):
        live["far" + name] = swap(live["sum" + name][3], XDIR)

    def sums_near(name):
        own, near, low, _ = live["sum" + name]
        far = live.pop("far" + name)
        low = (low.astype(F32) + far.astype(F32)).astype(BF)
        live["sum" + name] = (own, swap(low, ZLOW), swap(near, XDIR))

    def sums_total(name):
        own, low, near = live.pop("sum" + name)
        return own + near.astype(F32) + low.astype(F32)

    def grad_y(name):
        live["gy" + name] = swap(live["grad" + name][1], YDIR)

    def grad_half(name):
        kept, moved = live.pop("grad" + name)[0], live.pop("gy" + name)
        half = [kept[shift].astype(F32) + moved[shift].astype(F32) for shift in range(highs)]
        live["half" + name] = [half[0]] + [value.astype(BF) for value in half[1:]]

    def grad_h(name, causal=False):
        own, *others = live.pop("half" + name)
        live["gh" + name] = (
            own,
            [mover.to_high(value, shift + 1, causal) for shift, value in enumerate(others)],
        )

    def grad_total(name):
        own, others = live.pop("gh" + name)
        for value in others:
            own = own + value.astype(F32)
        return own

    def grad_zl(name):
        upper, lower = jnp.split(grad_total(name), 2, axis=0)
        own = jnp.where(first, upper, lower)
        other = jnp.where(first, lower, upper)
        live["shard" + name] = (own, swap(other.astype(BF), ZLOW))

    units = [str(c) for c in range(groups)]

    live["row"] = row
    live["segments"] = segments
    live["usend"] = unit_send
    live["osend"] = out_send
    live["upstream"] = upstream
    rows_first()
    start_zl("Q", qkv_send)
    live["sz"] = swap(segments, ZLOW)
    cut()
    add_pair("Q", qkv_keep)
    start_h("Q")
    start_y("Q")
    rows_second()
    seg_mine, seg_got = drop("segments", "sz")
    seg_pair = jnp.stack(
        [jnp.where(first, seg_mine, seg_got), jnp.where(first, seg_got, seg_mine)]
    )
    live["seg"] = jnp.concatenate([seg_pair, swap(seg_pair, YDIR)])
    start_zl("O", live.pop("osend"))
    start_zl("0", live["usend"][0])
    cut()
    span = jnp.arange(local, dtype=jnp.int32)
    steps = jnp.arange(4, dtype=jnp.int32)
    within = (
        ((zl ^ jnp.arange(2, dtype=jnp.int32))[:, None, None] * 2 * wide_tokens)
        + ((tp ^ steps) * local)[None, :, None]
        + span[None, None, :]
    ).reshape(head_rows)
    row_positions = (zh * 4 + y) * wide_tokens + within
    bases = jnp.stack(
        [
            (((zh + shift) % highs) * 4 + (y ^ dy)) * wide_tokens
            for shift in range(highs)
            for dy in range(2)
        ]
    ).astype(jnp.int32)
    seg_four = live.pop("seg")
    seg_all = jnp.concatenate([seg_four] + highs_of(seg_four))
    seg_all = lax.dynamic_index_in_dim(seg_all, zl, 1, keepdims=False)
    own_pair = lax.dynamic_index_in_dim(seg_four[:2], zl, 1, keepdims=False)
    own_rows = jnp.stack(
        [
            lax.dynamic_slice_in_dim(
                lax.dynamic_index_in_dim(own_pair, zl ^ dzl, 0, keepdims=False),
                (tp ^ dtp) * local,
                local,
                0,
            )
            for dzl in range(2)
            for dtp in range(4)
        ]
    ).reshape(head_rows)
    doc_starts = jnp.sum(
        (seg_all.reshape(1, -1) < own_rows[:, None]).astype(jnp.int32), axis=1
    )
    freqs = jnp.exp(-math.log(ROPE_BASE) * (2.0 * jnp.arange(HD // 2, dtype=F32) / HD))
    angles = row_positions.astype(F32)[:, None] * freqs[None, :]
    tables = (jnp.cos(angles), jnp.sin(angles))

    live["starts"] = doc_starts
    start_hy("Q")
    add_pair("0", unit_keep[0])
    add_pair("O", out_keep)
    start_h("0")
    start_zl("1", live["usend"][1])
    qkv_parts = parts_of("Q")
    normed_all, live["mine"], live["away"] = gathered_matmul(
        flags, rows_last(), qkv_parts, tables
    )
    live["normed"] = normed_all
    cut("h0")
    live["got"] = swap(live.pop("away"), ZLOW)
    start_y("O")
    start_y("0")
    live["dx"] = swap(live["upstream"], XDIR)
    cut()
    mine, got = take("mine", "got")
    live["pairK"] = jnp.concatenate(
        [
            jnp.where(first, mine[:, HD:], got[:, HD:]),
            jnp.where(first, got[:, HD:], mine[:, HD:]),
        ],
        axis=1,
    )
    start_h("K", causal=True)
    start_y("K")
    start_h("O")
    live["dz"] = swap(live["upstream"], ZLOW)
    cut("hO", "dz")
    add_pair("1", unit_keep[1])
    start_hy("K")
    start_h("1")
    pairs = parts_of("K")
    mine, got, doc_starts = take("mine", "got", "starts")
    mixed, log_sums, live["mo"], live["ma"] = attend(
        flags,
        bases,
        mine,
        got,
        pairs,
        doc_starts.reshape(head_rows, 1),
        row_positions.reshape(head_rows, 1),
        within.reshape(1, head_rows),
    )
    live["mixed"] = mixed
    cut("h1")

    def interleave(own, received):
        own = own.reshape(8, local, -1)
        received = received.reshape(8, local, -1)
        both = jnp.stack([jnp.where(first, own, received), jnp.where(first, received, own)], axis=1)
        return both.reshape(8 * rows, -1)

    start_hy("O")
    start_hy("0")
    live["mg"] = swap(live.pop("ma"), ZLOW)
    cut("h1", "hy0")
    mixed_all = interleave(*drop("mo", "mg"))
    out_parts = parts_of("O")
    live["keepA"], live["sendA"] = partial_matmul([mixed_all], [out_parts], [0])
    live["mixed_all"] = mixed_all
    cut("h1", "hy0")
    sums_core("A")
    start_zl("2", live["usend"][2])
    start_y("1")
    cut("y1")
    sums_combine("A")
    add_pair("2", unit_keep[2])
    cut("y1")
    sums_far("A")
    start_h("2")
    start_zl("3", live["usend"][3])
    live["dd"] = swap(live["dz"], XDIR)
    start_hy("1")
    cut("h2", "hy1", "dd")
    sums_near("A")
    add_pair("3", unit_keep[3])
    start_y("2")
    cut("y2")
    live["hidden"] = hidden = inputs + sums_total("A")
    scale_two = lax.rsqrt(jnp.mean(hidden * hidden, axis=-1, keepdims=True) + EPSILON)
    plain_two = hidden * scale_two
    live["row"] = plain_two.astype(BF)
    rows_first()
    d_rows = take("upstream", "dx", "dz", "dd")
    live["dc"] = [swap(d, CORE) for d in d_rows]
    start_hy("2")
    cut("hy2")
    rows_second()
    start_h("3")
    start_y("3")
    d_x, d_z, d_d, d_cores = drop("dx", "dz", "dd", "dc")
    live["dy_all"] = dy_all = assemble(
        [live["upstream"], d_cores[0], d_x, d_cores[1], d_z, d_cores[2], d_d, d_cores[3]]
    )
    cut("h3", "y3")
    live["x_all"] = x_all = assemble(rows_last())
    dy_all = live["dy_all"]
    live["u0"] = hidden_units(x_all, dy_all, parts_of("0"))
    cut("h3", "y3")
    x_all, dy_all = take("x_all", "dy_all")
    live["u1"] = hidden_units(x_all, dy_all, parts_of("1"))
    live["grad0"] = unit_grads(x_all, dy_all, *live["u0"], highs)
    cut()
    x_all, dy_all = take("x_all", "dy_all")
    start_hy("3")
    grad_y("0")
    live["u2"] = hidden_units(x_all, dy_all, parts_of("2"))
    live["grad1"] = unit_grads(x_all, dy_all, *live["u1"], highs)
    cut("gy0")
    x_all, dy_all = take("x_all", "dy_all")
    live["u3"] = hidden_units(x_all, dy_all, parts_of("3"))
    all_parts = [parts_of(c) for c in units]
    live["keepE"], live["sendE"] = partial_matmul(
        [live["u" + c][0] for c in units], all_parts, [0] * groups
    )
    cut()
    sums_core("E")
    grad_y("1")
    grad_half("0")
    cut("gy1")
    sums_combine("E")
    grad_h("0")
    cut("gy1", "gh0")
    sums_far("E")
    x_all, dy_all = take("x_all", "dy_all")
    live["grad2"] = unit_grads(x_all, dy_all, *live["u2"], highs)
    cut("gh0")
    sums_near("E")
    grad_half("1")
    grad_y("2")
    x_all, dy_all = take("x_all", "dy_all")
    live["grad3"] = unit_grads(x_all, dy_all, *live["u3"], highs)
    cut("gy2")
    weighted_two = sums_total("E")
    hidden_back = live["upstream"].astype(F32) + scale_two * (
        weighted_two - plain_two * jnp.mean(weighted_two * plain_two, axis=-1, keepdims=True)
    )
    live["row"] = hidden_back.astype(BF)
    rows_first()
    grad_h("1")
    live["keepD"], live["sendD"] = partial_matmul(
        [live["u" + c][1] for c in units],
        [parts_of(c) for c in units],
        [2 * unit_tile] * groups,
    )
    cut("gh1")
    rows_second()
    grad_half("2")
    grad_y("3")
    cut("gy3")
    grad_h("2")
    live["attn_back"], live["bm"], live["ba"] = gathered_matmul(
        flags, rows_last(), parts_of("O")
    )
    cut("gy3", "gh2")
    live["bg"] = swap(live.pop("ba"), ZLOW)
    cut("gh2")
    back_mine, back_got = drop("bm", "bg")
    grad_half("3")
    grad_h("3")
    deltas = jnp.sum(jnp.stack([back_mine, back_got]).astype(F32) * live["mixed"], axis=-1)
    mine, got, doc_starts = take("mine", "got", "starts")
    keep, send, live["qo"], live["qa"] = attend_back(
        flags,
        bases,
        mine,
        got,
        back_mine,
        back_got,
        parts_of("K"),
        doc_starts.reshape(1, head_rows),
        row_positions.reshape(1, head_rows),
        within.reshape(head_rows, 1),
        log_sums.reshape(2, head_rows),
        deltas,
        tables,
    )
    live["gradK"] = (keep, send)
    cut("gh3")
    depth = width // (2 * highs)

    def narrow_grads(rows_all, grad):
        blocks = [
            mm_tn(rows_all[:, p * depth : (p + 1) * depth], grad) for p in range(2 * highs)
        ]
        kept = jnp.stack(blocks[0::2]).astype(BF)
        return kept, jnp.stack(blocks[1::2]).astype(BF)

    grad_y("K")
    live["qg"] = swap(live.pop("qa"), ZLOW)
    sums_core("D")
    live["gradO"] = narrow_grads(live["attn_back"], live["mixed_all"])
    cut()
    grad_half("K")
    grad_h("K", causal=True)
    grad_y("O")
    sums_combine("D")
    query_back = interleave(*drop("qo", "qg"))
    live["gradQ"] = narrow_grads(live["normed"], query_back)
    live["query_back"] = query_back
    cut("gyO")
    total = grad_total("K")
    key_back = turn_back(total[:, :HD], *tables).astype(BF)
    value_back = total[:, HD:].astype(BF)
    pair_away = jnp.where(first, value_back, key_back).reshape(2, head_rows // 2, HD)
    pair_away = jnp.concatenate([pair_away[1], pair_away[0]], axis=0)
    live["po"] = jnp.where(first, key_back, value_back)
    live["pg"] = swap(pair_away, ZLOW)
    grad_y("Q")
    sums_far("D")
    grad_zl("0")
    cut("gyQ", "farD", "shard0")
    pair_back = interleave(*drop("po", "pg"))
    live["keepN"], live["sendN"] = partial_matmul(
        [live["query_back"], pair_back], [parts_of("Q")] * 2, [0, HD]
    )
    live["gradP"] = narrow_grads(live["normed"], pair_back)
    grad_half("O")
    cut("farD")
    sums_core("N")
    grad_y("P")
    grad_h("O")
    grad_half("Q")
    grad_zl("1")
    sums_near("D")
    cut("gyP", "ghO", "shard1", "sumD")
    sums_combine("N")
    grad_h("Q")
    cut("ghQ", "shard1", "sumD")
    sums_far("N")
    grad_half("P")
    grad_h("P")
    grad_zl("2")
    cut("ghP", "shard2")
    layer_out = live["hidden"] + sums_total("D")
    sums_near("N")
    grad_zl("3")
    grad_zl("O")
    grad_zl("Q")
    cut("shard3", "shardO", "shardQ")
    grad_zl("P")
    weighted_one = sums_total("N")
    input_grad = hidden_back + scale_one * (
        weighted_one - plain_one * jnp.mean(weighted_one * plain_one, axis=-1, keepdims=True)
    )
    shards = [live["shard" + c] for c in units]
    out_own, out_recv = live["shardO"]
    own, recv = live["shardQ"]
    query_plain = join(zl, own, recv.astype(F32))
    own, recv = live["shardP"]
    pair_plain = join(zl, own, recv.astype(F32))

    def unit_columns(which):
        cut = slice(which * unit_tile, (which + 1) * unit_tile)
        return join(
            zl,
            jnp.concatenate([shard[0][:, cut] for shard in shards], axis=1),
            jnp.concatenate([shard[1][:, cut] for shard in shards], axis=1).astype(F32),
        )

    gate_plain, up_plain = unit_columns(0), unit_columns(1)
    down_shard = unit_columns(2).T
    out_shard = join(zl, out_own, out_recv.astype(F32)).T
    gain_sums = jnp.stack(
        [
            jnp.sum(query_plain * query_weight.astype(F32), axis=1)
            + jnp.sum(pair_plain * pair_weight.astype(F32), axis=1),
            jnp.sum(gate_plain * gate_weight.astype(F32), axis=1)
            + jnp.sum(up_plain * up_weight.astype(F32), axis=1),
        ]
    )
    gain_sums = gain_sums + swap(gain_sums, CORE)
    gain_sums = gain_sums + swap(gain_sums, XDIR)
    pair_shard = pair_plain * gain_one
    shape = hidden_in.shape
    return (
        from_group_order(zh, y, highs, layer_out.astype(BF)).reshape(shape),
        from_group_order(zh, y, highs, input_grad).reshape(shape),
        gain_sums[0],
        query_plain * gain_one,
        pair_shard[:, :HD],
        pair_shard[:, HD:],
        out_shard,
        gain_sums[1],
        gate_plain * gain_two,
        up_plain * gain_two,
        down_shard,
    )


def solution(mesh):
    rows = P(None, ("wide", "tp"), None)
    columns = P("wide", "tp")
    flipped = P("tp", "wide")
    gain = P("wide")
    weights = (columns, columns, columns, flipped, gain, columns, columns, flipped)
    return jax.shard_map(
        body,
        mesh=mesh,
        in_specs=(rows, P(None, "wide"), gain) + weights + (rows,),
        out_specs=(rows, rows, gain) + weights,
        check_vma=False,
    )
```

```python
import functools
import math

import jax
import jax.numpy as jnp
from jax import lax
from jax.experimental import pallas as pl
from jax.experimental.pallas import tpu as pltpu
from jax.sharding import PartitionSpec as P

HD = 256
EPSILON = 1e-06
ROPE_BASE = 1000042.0
MASKED = -1e30
BF = jnp.bfloat16
F32 = jnp.float32
AXES = ("wide", "tp")
VMEM_LIMIT = 56 << 20

CORE, XDIR, YDIR, ZLOW = 1, 2, 4, 8
CONTRACT_ROWS = (((0,), (0,)), ((), ()))
CONTRACT_COLUMNS = (((1,), (1,)), ((), ()))


def mm(left, right):
    return jnp.dot(left, right, preferred_element_type=F32)


def mm_nt(left, right):
    return lax.dot_general(left, right, CONTRACT_COLUMNS, preferred_element_type=F32)


def mm_tn(left, right):
    return lax.dot_general(left, right, CONTRACT_ROWS, preferred_element_type=F32)


ANY = pl.BlockSpec(memory_space=pl.ANY)
WHOLE = pl.BlockSpec(memory_space=pltpu.VMEM)
SCALARS = pl.BlockSpec(memory_space=pltpu.SMEM)


def params():
    return pltpu.CompilerParams(vmem_limit_bytes=VMEM_LIMIT)


def cost(flops, *arrays):
    moved = sum(math.prod(a.shape) * jnp.dtype(a.dtype).itemsize for a in arrays)
    return pl.CostEstimate(flops=2 * int(flops), transcendentals=0, bytes_accessed=int(moved))


class Mover:
    def __init__(self, devices):
        self.devices = devices
        self.highs = devices // 16

    def swap(self, value, mask):
        return lax.ppermute(value, AXES, [(i, i ^ mask) for i in range(self.devices)])

    def from_high(self, value, shift, causal=False):
        pairs = []
        for dst in range(self.devices):
            zh = dst // 16
            src_zh = (zh + shift) % self.highs
            if causal and src_zh > zh:
                continue
            pairs.append((src_zh * 16 + dst % 16, dst))
        return lax.ppermute(value, AXES, pairs)

    def to_high(self, value, shift, causal=False):
        pairs = []
        for src in range(self.devices):
            zh = src // 16
            dst_zh = (zh + shift) % self.highs
            if causal and dst_zh > zh:
                continue
            pairs.append((src, dst_zh * 16 + src % 16))
        return lax.ppermute(value, AXES, pairs)


def weight_loads(parts, places, depth, buffer, sems, start):
    loads = []
    for part in parts:
        for low in range(part.shape[0] // depth):
            at = len(loads)
            row = pl.multiple_of(places[at] * depth, depth)
            loads.append(
                pltpu.make_async_copy(
                    part.at[pl.ds(low * depth, depth)],
                    buffer.at[pl.ds(row, depth)],
                    sems.at[start + at],
                )
            )
    return loads


def gathered_kernel(rotary, parts, blocks, places, *refs):
    chunks, refs = refs[:8], refs[8:]
    weights, refs = refs[:parts], refs[parts:]
    if rotary:
        cos_ref, sin_ref, all_ref, out_ref, pair_ref = refs[:5]
    else:
        all_ref, out_ref = refs[:2]
    rows_buf, weight_buf, sems = refs[-3:]
    rows = chunks[0].shape[0]
    depth = weight_buf.shape[0] // blocks
    fills = weight_loads(weights, places, depth, weight_buf, sems, 9)
    loads = [
        pltpu.make_async_copy(chunks[k], rows_buf.at[pl.ds(k * rows, rows)], sems.at[k])
        for k in range(8)
    ]
    for load in fills + loads:
        load.start()
    for fill in fills:
        fill.wait()
    tile = 4 * rows
    for half in range(2):
        for k in range(4):
            loads[4 * half + k].wait()
        place = slice(half * tile, (half + 1) * tile)
        left = rows_buf[place, :]
        if rotary:
            c, s = cos_ref[place, :], sin_ref[place, :]
            for head in range(3):
                product = mm(left, weight_buf[:, head * HD : (head + 1) * HD])
                a, b = product[:, : HD // 2], product[:, HD // 2 :]
                turned = jnp.concatenate([a * c - b * s, b * c + a * s], axis=1).astype(BF)
                if head < 2:
                    out_ref[place, head * HD : (head + 1) * HD] = turned
                else:
                    pair_ref[place, :HD] = turned
            pair_ref[place, HD:] = mm(left, weight_buf[:, 3 * HD :]).astype(BF)
        else:
            out_ref[place, :] = mm(left, weight_buf[...]).astype(BF)
    store = pltpu.make_async_copy(rows_buf, all_ref, sems.at[8])
    store.start()
    store.wait()


def gathered_matmul(places, chunks, parts, tables=None):
    rows, width = chunks[0].shape
    columns = parts[0].shape[1]
    blocks = places.shape[0]
    tables = tables or ()
    out = jax.ShapeDtypeStruct((8 * rows, 2 * HD), BF)
    outs = (out, out) if tables else (out,)
    return pl.pallas_call(
        functools.partial(gathered_kernel, bool(tables), len(parts), blocks),
        out_shape=(jax.ShapeDtypeStruct((8 * rows, width), BF),) + outs,
        in_specs=[SCALARS] + [ANY] * (8 + len(parts)) + [WHOLE] * len(tables),
        out_specs=(ANY,) + (WHOLE,) * len(outs),
        scratch_shapes=[
            pltpu.VMEM((8 * rows, width), BF),
            pltpu.VMEM((width, columns), BF),
            pltpu.SemaphoreType.DMA((9 + blocks,)),
        ],
        compiler_params=params(),
        cost_estimate=cost(2 * 8 * rows * width * columns, *chunks, *chunks, *parts),
        name="gathered",
    )(places, *chunks, *parts, *tables)


def partial_kernel(counts, starts, groups, blocks, places, *refs):
    lefts, refs = refs[:counts], refs[counts:]
    sets = []
    for size in groups:
        sets.append(refs[:size])
        refs = refs[size:]
    keep_ref, send_ref, weight_buf, sems = refs
    rows = keep_ref.shape[1]
    width = weight_buf.shape[0]
    depth = width // blocks

    @pl.when(pl.program_id(0) == 0)
    def _():
        fills = []
        column = 0
        for parts, start, left in zip(sets, starts, lefts):
            size = left.shape[1]
            place = pl.ds(column, size)
            cut = [part.at[:, pl.ds(start, size)] for part in parts]
            fills += weight_loads(
                cut, places, depth, weight_buf.at[:, place], sems, len(fills)
            )
            column += size
        for fill in fills:
            fill.start()
        for fill in fills:
            fill.wait()

    tile = 512 if width % 512 == 0 else width
    for at in range(0, width, tile):
        total = None
        column = 0
        for left in lefts:
            size = left.shape[1]
            term = mm_nt(left[...], weight_buf[at : at + tile, column : column + size])
            total = term if total is None else total + term
            column += size
        low = total.astype(BF)
        keep_ref[0, :, at : at + tile] = low[:rows]
        send_ref[0, :, at : at + tile] = low[rows:]


def partial_matmul(places, lefts, sets, starts):
    rows = lefts[0][0].shape[0] // 8
    blocks = places.shape[0]
    width = sum(part.shape[0] for part in sets[0])
    used = sum(size for _, _, size in lefts)
    out = jax.ShapeDtypeStruct((4, rows, width), BF)
    block = pl.BlockSpec((1, rows, width), lambda j: (j, 0, 0))
    flat = [part for parts in sets for part in parts]

    def rows_of(place, size):
        return pl.BlockSpec((2 * rows, size), lambda j: (j, place))

    return pl.pallas_call(
        functools.partial(
            partial_kernel, len(lefts), tuple(starts), tuple(len(p) for p in sets), blocks
        ),
        out_shape=(out, out),
        grid=(4,),
        in_specs=[SCALARS]
        + [rows_of(place, size) for _, place, size in lefts]
        + [ANY] * len(flat),
        out_specs=(block, block),
        scratch_shapes=[
            pltpu.VMEM((width, used), BF),
            pltpu.SemaphoreType.DMA((blocks * len(lefts),)),
        ],
        compiler_params=params(),
        cost_estimate=cost(2 * 8 * rows * width * used, out, out, out, out),
        name="partial",
    )(places, *[left for left, _, _ in lefts], *flat)


def combine_kernel(keep, got, own, across, low, diagonal):
    own[...] = keep[0].astype(F32) + got[0].astype(F32)
    for j, out in ((1, across), (2, low), (3, diagonal)):
        out[...] = (keep[j].astype(F32) + got[j].astype(F32)).astype(BF)


def combine(keep, got):
    _, rows, width = keep.shape
    tile = rows // 2
    wide = pl.BlockSpec((4, tile, width), lambda i: (0, i, 0))
    thin = pl.BlockSpec((tile, width), lambda i: (i, 0))
    return pl.pallas_call(
        combine_kernel,
        out_shape=(jax.ShapeDtypeStruct((rows, width), F32),)
        + (jax.ShapeDtypeStruct((rows, width), BF),) * 3,
        grid=(rows // tile,),
        in_specs=[wide, wide],
        out_specs=(thin,) * 4,
        compiler_params=params(),
        cost_estimate=cost(0, keep, keep, got, got),
        name="combine",
    )(keep, got)


def assemble_kernel(*refs):
    chunks, out, sems = refs[:8], refs[8], refs[9]
    rows = chunks[0].shape[0]
    copies = [
        pltpu.make_async_copy(chunks[k], out.at[pl.ds(k * rows, rows)], sems.at[k])
        for k in range(8)
    ]
    for copy in copies:
        copy.start()
    for copy in copies:
        copy.wait()


def assemble(chunks):
    rows, width = chunks[0].shape
    return pl.pallas_call(
        assemble_kernel,
        out_shape=jax.ShapeDtypeStruct((8 * rows, width), BF),
        in_specs=[ANY] * 8,
        out_specs=WHOLE,
        scratch_shapes=[pltpu.SemaphoreType.DMA((8,))],
        compiler_params=params(),
        cost_estimate=cost(0, *chunks, *chunks),
        name="assemble",
    )(*chunks)


def hidden_kernel(groups, blocks, places, x_ref, dy_ref, *refs):
    weights = [refs[c * groups[1] : (c + 1) * groups[1]] for c in range(groups[0])]
    back_ref, activated, weight_buf, sems = refs[groups[0] * groups[1] :]
    units = activated.shape[1] // groups[0]
    columns = 3 * units
    depth = weight_buf.shape[0] // blocks

    @pl.when(pl.program_id(0) == 0)
    def _():
        fills = []
        for c, parts in enumerate(weights):
            place = pl.ds(c * columns, columns)
            fills += weight_loads(
                parts, places, depth, weight_buf.at[:, place], sems, len(fills)
            )
        for fill in fills:
            fill.start()
        for fill in fills:
            fill.wait()

    for c in range(groups[0]):
        at = c * columns
        gate = mm(x_ref[...], weight_buf[:, at : at + units])
        lift = mm(x_ref[...], weight_buf[:, at + units : at + 2 * units])
        back = mm(dy_ref[...], weight_buf[:, at + 2 * units : at + columns])
        sigmoid = 1.0 / (1.0 + jnp.exp(-gate))
        silu = gate * sigmoid
        activated[:, c * units : (c + 1) * units] = (silu * lift).astype(BF)
        at = 2 * c * units
        back_ref[:, at + units : at + 2 * units] = (back * silu).astype(BF)
        back_ref[:, at : at + units] = (
            back * lift * (sigmoid * (1.0 + gate * (1.0 - sigmoid)))
        ).astype(BF)


def hidden_units(places, x_all, dy_all, sets):
    total, width = x_all.shape
    columns = sets[0][0].shape[1]
    units = columns // 3
    blocks = places.shape[0]
    groups = (len(sets), len(sets[0]))
    tile = total // 2
    rows = pl.BlockSpec((tile, width), lambda i: (i, 0))
    flat = [part for parts in sets for part in parts]
    return pl.pallas_call(
        functools.partial(hidden_kernel, groups, blocks),
        out_shape=(
            jax.ShapeDtypeStruct((total, 2 * units * groups[0]), BF),
            jax.ShapeDtypeStruct((total, units * groups[0]), BF),
        ),
        grid=(2,),
        in_specs=[SCALARS, rows, rows] + [ANY] * len(flat),
        out_specs=(
            pl.BlockSpec((tile, 2 * units * groups[0]), lambda i: (i, 0)),
            pl.BlockSpec((tile, units * groups[0]), lambda i: (i, 0)),
        ),
        scratch_shapes=[
            pltpu.VMEM((width, columns * groups[0]), BF),
            pltpu.SemaphoreType.DMA((blocks * groups[0],)),
        ],
        compiler_params=params(),
        cost_estimate=cost(2 * total * width * columns * groups[0], x_all, dy_all, *flat),
        name="hidden",
    )(places, x_all, dy_all, *flat)


def grads_kernel(counts, flags, *refs):
    lefts, refs = refs[:counts], refs[counts:]
    rights, refs = refs[:counts], refs[counts:]
    outs, buffer = refs[: 2 * counts], refs[2 * counts]
    depth = buffer.shape[0] // 4
    for k, (left, right) in enumerate(zip(lefts, rights)):
        size = right.shape[1]
        buffer[:, :size] = mm_tn(left[...], right[...]).astype(BF)
        for low in range(2):
            for dy in range(2):
                place = ((flags[0] ^ low) * 2 + (flags[2] ^ dy)) * depth
                outs[2 * k + dy][0, low] = buffer[
                    pl.ds(pl.multiple_of(place, depth), depth), :size
                ]


def weight_grads(flags, highs, lefts, rights):
    total, width = lefts[0].shape
    depth = width // (4 * highs)
    sizes = [right.shape[1] for right in rights]
    shapes, blocks = [], []
    for size in sizes:
        shapes += [jax.ShapeDtypeStruct((highs, 2, depth, size), BF)] * 2
        blocks += [pl.BlockSpec((1, 2, depth, size), lambda h, flags: (h, 0, 0, 0))] * 2

    def rows_of(h, flags):
        return (0, lax.rem(flags[1] + h, highs))

    outs = pl.pallas_call(
        functools.partial(grads_kernel, len(lefts)),
        out_shape=tuple(shapes),
        grid_spec=pltpu.PrefetchScalarGridSpec(
            num_scalar_prefetch=1,
            grid=(highs,),
            in_specs=[pl.BlockSpec((total, 4 * depth), rows_of) for _ in lefts]
            + [pl.BlockSpec(right.shape, lambda h, flags: (0, 0)) for right in rights],
            out_specs=tuple(blocks),
            scratch_shapes=[pltpu.VMEM((4 * depth, max(sizes)), BF)],
        ),
        compiler_params=params(),
        cost_estimate=cost(2 * total * width * sum(sizes), *lefts, *rights, *shapes),
        name="grads",
    )(flags, *lefts, *rights)
    return [outs[2 * k : 2 * k + 2] for k in range(len(lefts))]


def needed_high(i, highs, flags):
    return jnp.where(i < 1, 0, highs - flags[1] + i - 1)


def attend_kernel(parts, flags, bases, queries, *refs):
    pairs, refs = refs[:parts], refs[parts:]
    lows, ends, within, mixed, log_sums, mixed_low, pair_buf, sems = refs
    count = queries.shape[0]
    half = count // 2
    highs = parts // 2
    loads = []
    for p in range(parts):
        place = pl.ds((p % 2) * count, count)
        loads.append(
            pltpu.make_async_copy(pairs[p], pair_buf.at[p // 2, place], sems.at[p])
        )
    for load in loads:
        load.start()
    for load in loads:
        load.wait()
    for head in range(2):
        columns = slice(head * HD, (head + 1) * HD)
        for side in range(2):
            place = slice(side * half, (side + 1) * half)
            query = queries[place, columns] * jnp.asarray(HD ** (-0.5), BF)
            low, end = lows[place, :], ends[place, :]

            def step(i, carry):
                peak, total, accum = carry
                high = needed_high(i, highs, flags)
                scores = mm_nt(query, pair_buf[high, :, :HD])
                position = within[...] + bases[high]
                allowed = (position >= low) & (position <= end)
                scores = jnp.where(allowed, scores, MASKED)
                new_peak = jnp.maximum(peak, jnp.max(scores, axis=1, keepdims=True))
                decay = jnp.exp(peak - new_peak)
                probs = jnp.exp(scores - new_peak)
                total = decay * total + jnp.sum(probs, axis=1, keepdims=True)
                accum = decay * accum + mm(probs.astype(BF), pair_buf[high, :, HD:])
                return new_peak, total, accum

            peak, total, accum = lax.fori_loop(
                0,
                1 + flags[1],
                step,
                (
                    jnp.full((half, 1), MASKED, F32),
                    jnp.zeros((half, 1), F32),
                    jnp.zeros((half, HD), F32),
                ),
            )
            out = accum / total
            mixed[place, columns] = out
            mixed_low[place, columns] = out.astype(BF)
            log_sums[head, place, :] = peak + jnp.log(total)


def attend(flags, bases, queries, pairs, lows, ends, within):
    count = queries.shape[0]
    parts = len(pairs)
    low = jax.ShapeDtypeStruct((count, 2 * HD), BF)
    mixed_shape = jax.ShapeDtypeStruct((count, 2 * HD), F32)
    return pl.pallas_call(
        functools.partial(attend_kernel, parts),
        out_shape=(mixed_shape, jax.ShapeDtypeStruct((2, count, 1), F32), low),
        in_specs=[SCALARS, SCALARS, WHOLE] + [ANY] * parts + [WHOLE] * 3,
        out_specs=(WHOLE,) * 3,
        scratch_shapes=[
            pltpu.VMEM((parts // 2, 2 * count, 2 * HD), BF),
            pltpu.SemaphoreType.DMA((parts,)),
        ],
        compiler_params=params(),
        cost_estimate=cost(16 * count * count * parts * HD, mixed_shape),
        name="attend",
    )(flags, bases, queries, *pairs, lows, ends, within)


def attend_back_kernel(parts, flags, bases, source, back, *refs):
    pairs, refs = refs[:parts], refs[parts:]
    lows, ends, within, stats, deltas, cos_ref, sin_ref, keep, send, out_ref = refs[:10]
    pair_buf, queries, backs, probs_buf, score_buf, query_sum, pair_sum, sems, out_sem = refs[10:]
    count = source.shape[0]
    highs = parts // 2
    scale = HD ** (-0.5)
    loads = []
    for p in range(parts):
        loads.append(pltpu.make_async_copy(pairs[p], pair_buf.at[p], sems.at[p]))
    for load in loads:
        load.start()
    for head in range(2):
        place = slice(head * count, (head + 1) * count)
        columns = slice(head * HD, (head + 1) * HD)
        queries[place, :] = source[:, columns] * jnp.asarray(scale, BF)
        backs[place, :] = back[:, columns]
    query_sum[...] = jnp.zeros_like(query_sum)
    for load in loads:
        load.wait()

    def step(i, carry):
        high = needed_high(i // 2, highs, flags)
        other = lax.rem(i, 2)
        b = 2 * high + other
        keys, values = pair_buf[b, :, :HD], pair_buf[b, :, HD:]
        place = pl.multiple_of(other * count, count)
        position = within[pl.ds(place, count), :] + bases[high]
        allowed = (position >= lows[...]) & (position <= ends[...])
        for head in range(2):
            place = slice(head * count, (head + 1) * count)
            scores = mm_nt(keys, queries[place, :])
            probs = jnp.where(allowed, jnp.exp(scores - stats[head : head + 1, :]), 0.0)
            prob_back = mm_nt(values, backs[place, :])
            probs_buf[:, place] = probs.astype(BF)
            score_buf[:, place] = (probs * (prob_back - deltas[head : head + 1, :])).astype(BF)
        pair_sum[:, :HD] = mm(score_buf[...], queries[...]).astype(BF)
        pair_sum[:, HD:] = mm(probs_buf[...], backs[...]).astype(BF)
        query_sum[...] += mm_tn(score_buf[...], keys)

        @pl.when(other == 0)
        def _():
            store = pltpu.make_async_copy(pair_sum, keep.at[high], out_sem)
            store.start()
            store.wait()

        @pl.when(other == 1)
        def _():
            store = pltpu.make_async_copy(pair_sum, send.at[high], out_sem)
            store.start()
            store.wait()

        return carry

    lax.fori_loop(0, 2 + 2 * flags[1], step, 0)
    c, s = cos_ref[...], sin_ref[...]
    for head in range(2):
        grad = query_sum[head * count : (head + 1) * count, :] * scale
        a, b = grad[:, : HD // 2], grad[:, HD // 2 :]
        turned = jnp.concatenate([a * c + b * s, b * c - a * s], axis=1)
        out_ref[:, head * HD : (head + 1) * HD] = turned.astype(BF)


def attend_back(
    flags, bases, queries, back, pairs, lows, ends, within, stats, deltas, tables
):
    count = queries.shape[0]
    parts = len(pairs)
    low = jax.ShapeDtypeStruct((count, 2 * HD), BF)
    grad = jax.ShapeDtypeStruct((parts // 2, count, 2 * HD), BF)
    return pl.pallas_call(
        functools.partial(attend_back_kernel, parts),
        out_shape=(grad, grad, low),
        in_specs=[SCALARS, SCALARS] + [WHOLE] * 2 + [ANY] * parts + [WHOLE] * 7,
        out_specs=(ANY, ANY, WHOLE),
        scratch_shapes=[
            pltpu.VMEM((parts, count, 2 * HD), BF),
            pltpu.VMEM((2 * count, HD), BF),
            pltpu.VMEM((2 * count, HD), BF),
            pltpu.VMEM((count, 2 * count), BF),
            pltpu.VMEM((count, 2 * count), BF),
            pltpu.VMEM((2 * count, HD), F32),
            pltpu.VMEM((count, 2 * HD), BF),
            pltpu.SemaphoreType.DMA((parts,)),
            pltpu.SemaphoreType.DMA,
        ],
        compiler_params=params(),
        cost_estimate=cost(20 * count * count * parts * HD, grad, grad),
        name="attend_back",
    )(flags, bases, queries, back, *pairs, lows, ends, within, stats, deltas, *tables)


def tie(values):
    return lax.optimization_barrier(values)


class Bag:
    pass


class Weight:
    def __init__(self, keep):
        self.keep = keep


class Sum:
    pass


class Grad:
    pass


def flatten(bag):
    names = sorted(vars(bag))
    return [getattr(bag, name) for name in names], tuple(names)


def unflatten(kind, names, values):
    bag = kind.__new__(kind)
    for name, value in zip(names, values):
        setattr(bag, name, value)
    return bag


for kind in (Bag, Weight, Sum, Grad):
    jax.tree_util.register_pytree_node(kind, flatten, functools.partial(unflatten, kind))


def halves(zl, array):
    c = array.shape[1] // 2
    left, right = array[:, :c], array[:, c:]
    first = zl == 0
    return jnp.where(first, left, right), jnp.where(first, right, left)


def join(zl, own, received):
    first = zl == 0
    return jnp.concatenate([jnp.where(first, own, received), jnp.where(first, received, own)], axis=1)


def turn_back(vectors, cosines, sines):
    half = vectors.shape[-1] // 2
    a, b = vectors[..., :half], vectors[..., half:]
    return jnp.concatenate([a * cosines + b * sines, b * cosines - a * sines], axis=-1)


def body(
    hidden_in,
    segments,
    attn_gain,
    query_weight,
    key_weight,
    value_weight,
    output_weight,
    mlp_gain,
    gate_weight,
    up_weight,
    down_weight,
    cotangent,
):
    wide_count = lax.axis_size("wide")
    devices = wide_count * 4
    mover = Mover(devices)
    highs = mover.highs
    wide = lax.axis_index("wide")
    tp = lax.axis_index("tp")
    y, zl, zh = wide & 1, (wide >> 1) & 1, wide >> 2
    first = zl == 0
    flags = jnp.stack([zl, zh, y]).astype(jnp.int32)
    micro, local, width = hidden_in.shape
    rows = micro * local
    wide_tokens = segments.shape[1]
    head_rows = 8 * local
    scale = HD ** (-0.5)
    swap = mover.swap
    shifts = range(1, highs)
    places = jnp.stack(
        [
            (((zh + shift) % highs) * 2 + (zl ^ low)) * 2 + (y ^ dy)
            for shift in range(highs)
            for dy in range(2)
            for low in range(2)
        ]
    ).astype(jnp.int32)

    def highs_of(value, causal=False):
        return [mover.from_high(value, shift, causal) for shift in shifts]

    def over_y(values):
        return [swap(value, YDIR) for value in values]

    inputs = hidden_in.reshape(rows, width).astype(F32)
    scale_one = lax.rsqrt(jnp.mean(inputs * inputs, axis=-1, keepdims=True) + EPSILON)
    plain_one = inputs * scale_one

    gain_one = attn_gain.astype(F32)[:, None]
    gain_two = mlp_gain.astype(F32)[:, None]

    def gained(weight, gain):
        return (weight.astype(F32) * gain).astype(BF)

    pair_weight = jnp.concatenate([key_weight, value_weight], axis=1)
    gate_keep, gate_send = halves(zl, gained(gate_weight, gain_two))
    up_keep, up_send = halves(zl, gained(up_weight, gain_two))
    down_keep, down_send = halves(zl, down_weight.T)
    units = 512
    groups = gate_keep.shape[1] // units

    def cut_units(c, gate, up, down):
        cut = slice(c * units, (c + 1) * units)
        return jnp.concatenate([gate[:, cut], up[:, cut], down[:, cut]], axis=1)

    live = Bag()

    def cut():
        vars(live).update(vars(tie(live)))

    def pair_of_segments():
        own, got = live.segments, live.seg_got
        return [jnp.stack([jnp.where(first, own, got), jnp.where(first, got, own)])]

    def blocks_of(weight):
        blocks = [weight.keep, weight.got, weight.yk, weight.yg]
        for group in zip(weight.hk, weight.hg, weight.hyk, weight.hyg):
            blocks += group
        return blocks

    def own_first(row):
        low, high = row[:local], row[local:]
        live.row = jnp.where(first, low, high)
        live.rz = swap(jnp.where(first, high, low), ZLOW)
        live.rx = swap(live.row, XDIR)
        live.rc = [swap(live.row, CORE)]

    def rows_first(row):
        live.row, live.rx, live.rz = row, swap(row, XDIR), swap(row, ZLOW)
        live.rc = [swap(row, CORE)]

    def rows_second():
        live.rd = swap(live.rz, XDIR)
        live.rc += [swap(value, CORE) for value in (live.rx, live.rz)]

    def rows_last():
        row, x, z, d, c = live.row, live.rx, live.rz, live.rd, live.rc
        del live.row, live.rx, live.rz, live.rd, live.rc
        return [row, c[0], x, c[1], z, c[2], d, swap(d, CORE)]

    def sums_start(pair):
        part = Sum()
        part.keep, part.send = pair
        return part

    def sums_core(part):
        part.send = swap(part.send, CORE)

    def sums_combine(part):
        part.own, part.near, part.low, part.far = combine(part.keep, part.send)
        del part.keep, part.send

    def sums_far(part):
        part.far = swap(part.far, XDIR)

    def sums_near(part):
        low = (part.low.astype(F32) + part.far.astype(F32)).astype(BF)
        part.low, part.near = swap(low, ZLOW), swap(part.near, XDIR)
        del part.far

    def sums_total(part):
        return part.own + part.near.astype(F32) + part.low.astype(F32)

    def own_x(part):
        part.far, part.near = swap(part.far, XDIR), swap(part.near, XDIR)

    def own_zl(part):
        low = (part.low.astype(F32) + part.far.astype(F32)).astype(BF)
        part.low = swap(low, ZLOW)
        del part.far

    def own_total(part):
        mine, other = part.own + part.near.astype(F32), part.low.astype(F32)
        return jnp.concatenate([jnp.where(first, mine, other), jnp.where(first, other, mine)])

    def grad_start(pair):
        part = Grad()
        part.keep = [pair[0][shift] for shift in range(highs)]
        part.send = [pair[1][shift] for shift in range(highs)]
        return part

    def grad_y_far(part):
        part.send[1:] = [swap(part.send[shift], YDIR) for shift in shifts]

    def grad_y_near(part):
        part.send[0] = swap(part.send[0], YDIR)

    def grad_h(part, low):
        moved = []
        for shift in shifts:
            half = part.keep[shift][low].astype(F32) + part.send[shift][low].astype(F32)
            moved.append(mover.to_high(half.astype(BF), shift))
        if low:
            part.moved_got = moved
        else:
            part.moved_own = moved

    def grad_zl(part):
        totals = []
        for low in range(2):
            total = part.keep[0][low].astype(F32) + part.send[0][low].astype(F32)
            for moved in (part.moved_own, part.moved_got)[low]:
                total = total + moved.astype(F32)
            totals.append(total)
        part.own, part.got = totals[0], swap(totals[1].astype(BF), ZLOW)
        del part.keep, part.send, part.moved_own, part.moved_got

    span = jnp.arange(local, dtype=jnp.int32)
    steps = jnp.arange(4, dtype=jnp.int32)
    within = (
        ((zl ^ jnp.arange(2, dtype=jnp.int32))[:, None, None] * 2 * wide_tokens)
        + ((tp ^ steps) * local)[None, :, None]
        + span[None, None, :]
    ).reshape(head_rows)
    row_positions = (zh * 4 + y) * wide_tokens + within
    bases = jnp.stack([((zh + shift) % highs) * 4 * wide_tokens for shift in range(highs)])
    bases = bases.astype(jnp.int32)
    key_within = jnp.concatenate([within + (y ^ dy) * wide_tokens for dy in range(2)])
    freqs = jnp.exp(-math.log(ROPE_BASE) * (2.0 * jnp.arange(HD // 2, dtype=F32) / HD))
    angles = row_positions.astype(F32)[:, None] * freqs[None, :]
    tables = (jnp.cos(angles), jnp.sin(angles))

    live.upstream = cotangent.reshape(rows, width)
    qkv_own, row_one = tie(
        [
            jnp.concatenate([gained(w, gain_one) for w in (query_weight, pair_weight)], axis=1),
            plain_one.astype(BF),
        ]
    )
    live.q = q = Weight(qkv_own)
    q.hk = highs_of(q.keep)
    q.got = swap(q.keep, ZLOW)
    q.yk = swap(q.keep, YDIR)
    own_first(row_one)
    live.u_send = [cut_units(c, gate_send, up_send, down_send) for c in range(groups)]
    live.u = u = [Weight(cut_units(c, gate_keep, up_keep, down_keep)) for c in range(groups)]
    live.o_own = output_weight.T
    live.segments = segments
    u[0].yk = swap(u[0].keep, YDIR)
    live.seg_got = swap(segments, ZLOW)
    cut()
    q, u = live.q, live.u
    q.hg = highs_of(q.got)
    q.hyk = over_y(q.hk)
    q.yg = swap(q.got, YDIR)
    live.rd = swap(live.rz, XDIR)
    live.o_got = swap(live.o_own, ZLOW)
    cut()
    q, u = live.q, live.u
    q.hyg = over_y(q.hg)
    live.rc += [swap(live.rx, CORE), swap(live.rz, CORE)]
    live.out_pair = jnp.concatenate([live.o_own, live.o_got])
    live.out_h = highs_of(live.out_pair)
    live.seg = pair_of_segments()
    live.seg.append(swap(live.seg[0], YDIR))
    live.normed, live.queries, live.pair = gathered_matmul(
        places, rows_last(), blocks_of(q), tables
    )
    cut()
    u = live.u
    live.pair_h, live.pair_y = highs_of(live.pair, causal=True), swap(live.pair, YDIR)
    live.out_y = swap(live.out_pair, YDIR)
    live.out_hy = over_y(live.out_h)
    live.seg = [jnp.concatenate(live.seg)]
    live.seg += highs_of(live.seg[0])
    live.dz = swap(live.upstream, ZLOW)
    cut()
    seg_all = lax.dynamic_index_in_dim(jnp.concatenate(live.seg), zl, 1, keepdims=False)
    own_pair = lax.dynamic_index_in_dim(live.seg[0][:2], zl, 1, keepdims=False)
    del live.seg
    own_rows = jnp.stack(
        [
            lax.dynamic_slice_in_dim(
                lax.dynamic_index_in_dim(own_pair, zl ^ dzl, 0, keepdims=False),
                (tp ^ dtp) * local,
                local,
                0,
            )
            for dzl in range(2)
            for dtp in range(4)
        ]
    ).reshape(head_rows)
    live.starts = jnp.sum(
        (seg_all.reshape(1, -1) < own_rows[:, None]).astype(jnp.int32), axis=1
    )
    u = live.u
    pair_hy = over_y(live.pair_h)
    u[0].got = swap(live.u_send[0], ZLOW)
    u[0].hk = highs_of(u[0].keep)
    live.dx = swap(live.upstream, XDIR)
    live.dd = swap(live.dz, XDIR)
    live.pairs = [live.pair, live.pair_y]
    for values in zip(live.pair_h, pair_hy):
        live.pairs += values
    del live.pair, live.pair_y, live.pair_h
    live.mixed, live.log_sums, live.mixed_all = attend(
        flags,
        bases,
        live.queries,
        live.pairs,
        live.starts.reshape(head_rows, 1),
        row_positions.reshape(head_rows, 1),
        key_within.reshape(1, 2 * head_rows),
    )
    cut()
    u = live.u
    live.o = [live.out_pair, live.out_y]
    for values in zip(live.out_h, live.out_hy):
        live.o += values
    del live.out_pair, live.out_y, live.out_h, live.out_hy
    live.a = sums_start(partial_matmul(places, [(live.mixed_all, 0, 2 * HD)], [live.o], [0]))
    cut()
    u = live.u
    sums_core(live.a)
    u[0].yg = swap(u[0].got, YDIR)
    u[0].hg = highs_of(u[0].got)
    u[0].hyk = over_y(u[0].hk)
    sums_combine(live.a)
    own_x(live.a)
    cut()
    u = live.u
    own_zl(live.a)
    live.dc = [swap(d, CORE) for d in (live.upstream, live.dx, live.dz, live.dd)]
    cut()
    u = live.u
    live.hidden = hidden = inputs + own_total(live.a)
    del live.a
    scale_two = lax.rsqrt(jnp.mean(hidden * hidden, axis=-1, keepdims=True) + EPSILON)
    plain_two = hidden * scale_two
    rows_first(plain_two.astype(BF))
    u[1].yk = swap(u[1].keep, YDIR)
    u[1].hk = highs_of(u[1].keep)
    cut()
    u = live.u
    rows_second()
    u[0].hyg = over_y(u[0].hg)
    u[1].got = swap(live.u_send[1], ZLOW)
    d_x, d_z, d_d, d_cores = live.dx, live.dz, live.dd, live.dc
    live.dy_all = assemble(
        [live.upstream, d_cores[0], d_x, d_cores[1], d_z, d_cores[2], d_d, d_cores[3]]
    )
    del live.dx, live.dz, live.dd, live.dc
    cut()
    u = live.u
    live.x_all = assemble(rows_last())
    u[1].yg = swap(u[1].got, YDIR)
    u[1].hg = highs_of(u[1].got)
    u[1].hyk = over_y(u[1].hk)
    live.backs, live.acts = [None] * 2, [None] * 2

    def unit_work(c):
        live.backs[c], live.acts[c] = hidden_units(
            places, live.x_all, live.dy_all, [blocks_of(live.u[c])]
        )

    def unit_grads(c):
        pairs = weight_grads(
            flags, highs, [live.x_all, live.dy_all], [live.backs[c], live.acts[c]]
        )
        return [grad_start(pair) for pair in pairs]

    unit_work(0)
    cut()
    u = live.u
    u[1].hyg = over_y(u[1].hg)
    live.g = unit_grads(0)
    cut()
    g = live.g
    unit_work(1)
    cut()
    g = live.g
    grad_y_far(g[1])
    live.unit_blocks = [blocks_of(weight) for weight in live.u]
    del live.u
    live.e = sums_start(
        partial_matmul(
            places,
            [(back, 0, 2 * units) for back in live.backs],
            live.unit_blocks,
            [0] * groups,
        )
    )
    cut()
    g = live.g
    sums_core(live.e)
    grad_y_far(g[0])
    grad_h(g[1], 0)
    grad_h(g[1], 1)
    live.g += unit_grads(1)
    cut()
    g = live.g
    sums_combine(live.e)
    sums_far(live.e)
    grad_h(g[0], 0)
    grad_y_far(g[2])
    cut()
    g = live.g
    sums_near(live.e)
    grad_y_far(g[3])
    cut()
    weighted_two = sums_total(live.e)
    del live.e
    hidden_back = live.upstream.astype(F32) + scale_two * (
        weighted_two - plain_two * jnp.mean(weighted_two * plain_two, axis=-1, keepdims=True)
    )
    g = live.g
    own_first(hidden_back.astype(BF))
    grad_y_near(g[0])
    grad_h(g[2], 1)
    live.d = sums_start(
        partial_matmul(
            places,
            [(act, 0, units) for act in live.acts],
            live.unit_blocks,
            [2 * units] * groups,
        )
    )
    del live.acts, live.backs, live.unit_blocks
    cut()
    g = live.g
    rows_second()
    grad_y_near(g[1])
    grad_h(g[3], 1)
    cut()
    g = live.g
    grad_zl(g[1])
    grad_y_near(g[3])
    grad_h(g[3], 0)
    sums_core(live.d)
    live.attn_back, live.back = gathered_matmul(places, rows_last(), live.o)
    cut()
    g = live.g
    grad_y_near(g[2])
    grad_h(g[2], 0)
    sums_combine(live.d)
    sums_far(live.d)
    deltas = jnp.sum((live.back.astype(F32) * live.mixed).reshape(head_rows, 2, HD), axis=-1).T
    keep, send, live.query_back = attend_back(
        flags,
        bases,
        live.queries,
        live.back,
        live.pairs,
        live.starts.reshape(1, head_rows),
        row_positions.reshape(1, head_rows),
        key_within.reshape(2 * head_rows, 1),
        live.log_sums.reshape(2, head_rows),
        deltas,
        tables,
    )
    live.k_keep = [keep[shift] for shift in range(highs)]
    live.k_send = [send[shift] for shift in range(highs)]
    cut()
    g = live.g
    live.k_send[1:] = [swap(live.k_send[shift], YDIR) for shift in shifts]
    grad_h(g[0], 1)
    sums_near(live.d)
    (grads_out,) = weight_grads(flags, highs, [live.attn_back], [live.mixed_all])
    live.g_out = grad_start(grads_out)
    cut()
    g = live.g
    live.k_moved = []
    for shift in shifts:
        half = live.k_keep[shift].astype(F32) + live.k_send[shift].astype(F32)
        live.k_moved.append(mover.to_high(half.astype(BF), shift, causal=True))
    live.k_near = swap(live.k_send[0], YDIR)
    grad_zl(g[0])
    grad_y_far(live.g_out)
    (grads_q,) = weight_grads(flags, highs, [live.normed], [live.query_back])
    live.g_q = grad_start(grads_q)
    cut()
    g = live.g
    total = live.k_keep[0].astype(F32) + live.k_near.astype(F32)
    for moved in live.k_moved:
        total = total + moved.astype(F32)
    del live.k_keep, live.k_send, live.k_moved, live.k_near
    key_back = turn_back(total[:, :HD], *tables).astype(BF)
    live.pair_back = jnp.concatenate([key_back, total[:, HD:].astype(BF)], axis=1)
    grad_zl(g[3])
    grad_h(live.g_out, 0)
    grad_y_far(live.g_q)
    (grads_p,) = weight_grads(flags, highs, [live.normed], [live.pair_back])
    live.g_p = grad_start(grads_p)
    cut()
    g = live.g
    grad_zl(g[2])
    grad_y_near(live.g_out)
    grad_h(live.g_out, 1)
    grad_y_near(live.g_q)
    grad_h(live.g_q, 1)
    live.n = sums_start(
        partial_matmul(
            places,
            [(live.query_back, 0, 2 * HD), (live.pair_back, 0, 2 * HD)],
            [blocks_of(live.q)] * 2,
            [0, 2 * HD],
        )
    )
    cut()
    g = live.g
    sums_core(live.n)
    grad_zl(live.g_out)
    grad_h(live.g_q, 0)
    grad_y_far(live.g_p)
    cut()
    g = live.g
    sums_combine(live.n)
    own_x(live.n)
    grad_zl(live.g_q)
    grad_h(live.g_p, 0)
    cut()
    g = live.g
    own_zl(live.n)
    grad_y_near(live.g_p)
    grad_h(live.g_p, 1)
    cut()
    layer_out = live.hidden + sums_total(live.d)
    weighted_one = own_total(live.n)
    input_grad = hidden_back + scale_one * (
        weighted_one - plain_one * jnp.mean(weighted_one * plain_one, axis=-1, keepdims=True)
    )
    g = live.g
    grad_zl(live.g_p)
    def unit_columns(pieces):
        cuts = [(part, slice(at * units, (at + 1) * units)) for part, at in pieces]
        return join(
            zl,
            jnp.concatenate([part.own[:, cut] for part, cut in cuts], axis=1),
            jnp.concatenate([part.got[:, cut] for part, cut in cuts], axis=1).astype(F32),
        )

    def columns_of(part):
        return part.own + part.got.astype(F32)

    gate_plain = unit_columns([(g[0], 0), (g[2], 0)])
    up_plain = unit_columns([(g[0], 1), (g[2], 1)])
    query_plain, pair_plain = columns_of(live.g_q), columns_of(live.g_p)
    gain_sums = jnp.stack(
        [
            jnp.sum(query_plain * query_weight.astype(F32), axis=1)
            + jnp.sum(pair_plain * pair_weight.astype(F32), axis=1),
            jnp.sum(gate_plain * gate_weight.astype(F32), axis=1)
            + jnp.sum(up_plain * up_weight.astype(F32), axis=1),
        ]
    )
    gain_sums = gain_sums + swap(gain_sums, CORE)
    gain_sums = gain_sums + swap(gain_sums, XDIR)
    pair_shard = pair_plain * gain_one
    shape = hidden_in.shape
    return (
        layer_out.astype(BF).reshape(shape),
        input_grad.reshape(shape),
        gain_sums[0],
        query_plain * gain_one,
        pair_shard[:, :HD],
        pair_shard[:, HD:],
        columns_of(live.g_out).T,
        gain_sums[1],
        gate_plain * gain_two,
        up_plain * gain_two,
        unit_columns([(g[1], 0), (g[3], 0)]).T,
    )


def solution(mesh):
    rows = P(None, ("wide", "tp"), None)
    columns = P("wide", "tp")
    flipped = P("tp", "wide")
    gain = P("wide")
    weights = (columns, columns, columns, flipped, gain, columns, columns, flipped)
    return jax.shard_map(
        body,
        mesh=mesh,
        in_specs=(rows, P(None, "wide"), gain) + weights + (rows,),
        out_specs=(rows, rows, gain) + weights,
        check_vma=False,
    )
```

```python
import functools
import math

import jax
import jax.numpy as jnp
from jax import lax
from jax.experimental import pallas as pl
from jax.experimental.pallas import tpu as pltpu
from jax.sharding import PartitionSpec as P

HD = 256
EPSILON = 1e-06
ROPE_BASE = 1000042.0
MASKED = -1e30
BF = jnp.bfloat16
F32 = jnp.float32
AXES = ("wide", "tp")
VMEM_LIMIT = 56 << 20

CORE, XDIR, YDIR, ZLOW = 1, 2, 4, 8
CONTRACT_ROWS = (((0,), (0,)), ((), ()))
CONTRACT_COLUMNS = (((1,), (1,)), ((), ()))


def mm(left, right):
    return jnp.dot(left, right, preferred_element_type=F32)


def mm_nt(left, right):
    return lax.dot_general(left, right, CONTRACT_COLUMNS, preferred_element_type=F32)


def mm_tn(left, right):
    return lax.dot_general(left, right, CONTRACT_ROWS, preferred_element_type=F32)


ANY = pl.BlockSpec(memory_space=pl.ANY)
WHOLE = pl.BlockSpec(memory_space=pltpu.VMEM)
SCALARS = pl.BlockSpec(memory_space=pltpu.SMEM)


def params():
    return pltpu.CompilerParams(vmem_limit_bytes=VMEM_LIMIT)


def cost(flops, *arrays):
    moved = sum(math.prod(a.shape) * jnp.dtype(a.dtype).itemsize for a in arrays)
    return pl.CostEstimate(flops=2 * int(flops), transcendentals=0, bytes_accessed=int(moved))


class Mover:
    def __init__(self, devices):
        self.devices = devices
        self.highs = devices // 16

    def swap(self, value, mask):
        return lax.ppermute(value, AXES, [(i, i ^ mask) for i in range(self.devices)])

    def from_high(self, value, shift, causal=False):
        pairs = []
        for dst in range(self.devices):
            zh = dst // 16
            src_zh = (zh + shift) % self.highs
            if causal and src_zh > zh:
                continue
            pairs.append((src_zh * 16 + dst % 16, dst))
        return lax.ppermute(value, AXES, pairs)

    def to_high(self, value, shift, causal=False):
        pairs = []
        for src in range(self.devices):
            zh = src // 16
            dst_zh = (zh + shift) % self.highs
            if causal and dst_zh > zh:
                continue
            pairs.append((src, dst_zh * 16 + src % 16))
        return lax.ppermute(value, AXES, pairs)


def weight_loads(parts, places, depth, buffer, sems, start):
    loads = []
    for part in parts:
        for low in range(part.shape[0] // depth):
            at = len(loads)
            row = pl.multiple_of(places[at] * depth, depth)
            loads.append(
                pltpu.make_async_copy(
                    part.at[pl.ds(low * depth, depth)],
                    buffer.at[pl.ds(row, depth)],
                    sems.at[start + at],
                )
            )
    return loads


def gathered_kernel(rotary, stacked, parts, blocks, places, *refs):
    stacks, refs = refs[:stacked], refs[stacked:]
    weights, refs = refs[:parts], refs[parts:]
    if rotary:
        cos_ref, sin_ref, all_ref, out_ref, pair_ref = refs[:5]
    else:
        mixed_ref, all_ref, out_ref, delta_ref = refs[:4]
    rows_buf, weight_buf, sems = refs[-3:]
    rows = rows_buf.shape[0] // 8
    if stacked == 4:
        chunks = [stacks[k % 4].at[pl.ds(k // 4 * rows, rows)] for k in range(8)]
    else:
        chunks = stacks
    depth = weight_buf.shape[0] // blocks
    fills = weight_loads(weights, places, depth, weight_buf, sems, 9)
    loads = [
        pltpu.make_async_copy(chunks[k], rows_buf.at[pl.ds(k * rows, rows)], sems.at[k])
        for k in range(8)
    ]
    for load in fills + loads:
        load.start()
    for fill in fills:
        fill.wait()
    tile = 4 * rows
    for half in range(2):
        for k in range(4):
            loads[4 * half + k].wait()
        place = slice(half * tile, (half + 1) * tile)
        left = rows_buf[place, :]
        if rotary:
            c, s = cos_ref[place, :], sin_ref[place, :]
            for head in range(3):
                product = mm(left, weight_buf[:, head * HD : (head + 1) * HD])
                a, b = product[:, : HD // 2], product[:, HD // 2 :]
                turned = jnp.concatenate([a * c - b * s, b * c + a * s], axis=1).astype(BF)
                if head < 2:
                    out_ref[place, head * HD : (head + 1) * HD] = turned
                else:
                    pair_ref[place, :HD] = turned
            pair_ref[place, HD:] = mm(left, weight_buf[:, 3 * HD :]).astype(BF)
        else:
            low = mm(left, weight_buf[...]).astype(BF)
            out_ref[place, :] = low
            product = low.astype(F32) * mixed_ref[place, :]
            for head in range(2):
                delta_ref[place, head : head + 1] = jnp.sum(
                    product[:, head * HD : (head + 1) * HD], axis=1, keepdims=True
                )
    store = pltpu.make_async_copy(rows_buf, all_ref, sems.at[8])
    store.start()
    store.wait()


def gathered_matmul(places, chunks, parts, tables=None, mixed=None):
    rows, width = chunks[0].shape
    rows = rows * len(chunks) // 8
    columns = parts[0].shape[1]
    blocks = places.shape[0]
    more = tables or (mixed,)
    out = jax.ShapeDtypeStruct((8 * rows, 2 * HD), BF)
    outs = (out, out) if tables else (out, jax.ShapeDtypeStruct((8 * rows, 2), F32))
    return pl.pallas_call(
        functools.partial(gathered_kernel, bool(tables), len(chunks), len(parts), blocks),
        out_shape=(jax.ShapeDtypeStruct((8 * rows, width), BF),) + outs,
        in_specs=[SCALARS] + [ANY] * (len(chunks) + len(parts)) + [WHOLE] * len(more),
        out_specs=(ANY,) + (WHOLE,) * len(outs),
        scratch_shapes=[
            pltpu.VMEM((8 * rows, width), BF),
            pltpu.VMEM((width, columns), BF),
            pltpu.SemaphoreType.DMA((9 + blocks,)),
        ],
        compiler_params=params(),
        cost_estimate=cost(2 * 8 * rows * width * columns, *chunks, *chunks, *parts),
        name="gathered",
    )(places, *chunks, *parts, *more)


def partial_kernel(counts, starts, groups, blocks, places, *refs):
    lefts, refs = refs[:counts], refs[counts:]
    sets = []
    for size in groups:
        sets.append(refs[:size])
        refs = refs[size:]
    keep_ref, send_ref, weight_buf, sems = refs
    rows = keep_ref.shape[1]
    width = weight_buf.shape[0]
    depth = width // blocks

    @pl.when(pl.program_id(0) == 0)
    def _():
        fills = []
        column = 0
        for parts, start, left in zip(sets, starts, lefts):
            size = left.shape[1]
            place = pl.ds(column, size)
            cut = [part.at[:, pl.ds(start, size)] for part in parts]
            fills += weight_loads(
                cut, places, depth, weight_buf.at[:, place], sems, len(fills)
            )
            column += size
        for fill in fills:
            fill.start()
        for fill in fills:
            fill.wait()

    tile = 512 if width % 512 == 0 else width
    for at in range(0, width, tile):
        total = None
        column = 0
        for left in lefts:
            size = left.shape[1]
            term = mm_nt(left[...], weight_buf[at : at + tile, column : column + size])
            total = term if total is None else total + term
            column += size
        low = total.astype(BF)
        keep_ref[0, :, at : at + tile] = low[:rows]
        send_ref[0, :, at : at + tile] = low[rows:]


def partial_matmul(places, lefts, sets, starts):
    rows = lefts[0][0].shape[0] // 8
    blocks = places.shape[0]
    width = sum(part.shape[0] for part in sets[0])
    used = sum(size for _, _, size in lefts)
    out = jax.ShapeDtypeStruct((4, rows, width), BF)
    block = pl.BlockSpec((1, rows, width), lambda j: (j, 0, 0))
    flat = [part for parts in sets for part in parts]

    def rows_of(place, size):
        return pl.BlockSpec((2 * rows, size), lambda j: (j, place))

    return pl.pallas_call(
        functools.partial(
            partial_kernel, len(lefts), tuple(starts), tuple(len(p) for p in sets), blocks
        ),
        out_shape=(out, out),
        grid=(4,),
        in_specs=[SCALARS]
        + [rows_of(place, size) for _, place, size in lefts]
        + [ANY] * len(flat),
        out_specs=(block, block),
        scratch_shapes=[
            pltpu.VMEM((width, used), BF),
            pltpu.SemaphoreType.DMA((blocks * len(lefts),)),
        ],
        compiler_params=params(),
        cost_estimate=cost(2 * 8 * rows * width * used, out, out, out, out),
        name="partial",
    )(places, *[left for left, _, _ in lefts], *flat)


def combine_kernel(keep, got, own, across, low, diagonal):
    own[...] = keep[0].astype(F32) + got[0].astype(F32)
    for j, out in ((1, across), (2, low), (3, diagonal)):
        out[...] = (keep[j].astype(F32) + got[j].astype(F32)).astype(BF)


def combine(keep, got):
    _, rows, width = keep.shape
    tile = rows // 2
    wide = pl.BlockSpec((4, tile, width), lambda i: (0, i, 0))
    thin = pl.BlockSpec((tile, width), lambda i: (i, 0))
    return pl.pallas_call(
        combine_kernel,
        out_shape=(jax.ShapeDtypeStruct((rows, width), F32),)
        + (jax.ShapeDtypeStruct((rows, width), BF),) * 3,
        grid=(rows // tile,),
        in_specs=[wide, wide],
        out_specs=(thin,) * 4,
        compiler_params=params(),
        cost_estimate=cost(0, keep, keep, got, got),
        name="combine",
    )(keep, got)


def assemble_kernel(*refs):
    chunks, out, sems = refs[:8], refs[8], refs[9]
    rows = chunks[0].shape[0]
    copies = [
        pltpu.make_async_copy(chunks[k], out.at[pl.ds(k * rows, rows)], sems.at[k])
        for k in range(8)
    ]
    for copy in copies:
        copy.start()
    for copy in copies:
        copy.wait()


def assemble(chunks):
    rows, width = chunks[0].shape
    return pl.pallas_call(
        assemble_kernel,
        out_shape=jax.ShapeDtypeStruct((8 * rows, width), BF),
        in_specs=[ANY] * 8,
        out_specs=WHOLE,
        scratch_shapes=[pltpu.SemaphoreType.DMA((8,))],
        compiler_params=params(),
        cost_estimate=cost(0, *chunks, *chunks),
        name="assemble",
    )(*chunks)


def hidden_kernel(counts, blocks, places, dy_ref, *refs):
    chunks, refs = refs[: counts[0]], refs[counts[0] :]
    weights, refs = refs[: counts[1]], refs[counts[1] :]
    x_all, back_ref, activated, x_buf, weight_buf, sems = refs
    step = pl.program_id(0)
    units = activated.shape[1]
    depth = weight_buf.shape[0] // blocks
    rows = chunks[0].shape[0]
    tile = dy_ref.shape[0]
    fills = weight_loads(weights, places, depth, weight_buf, sems, 0)
    pieces = counts[0] if counts[0] > 1 else 2
    size = x_buf.shape[0] // pieces
    loads = []
    for k in range(pieces):
        source = chunks[k] if counts[0] > 1 else chunks[0].at[pl.ds(k * size, size)]
        loads.append(
            pltpu.make_async_copy(source, x_buf.at[pl.ds(k * size, size)], sems.at[blocks + k])
        )
    store = pltpu.make_async_copy(x_buf, x_all, sems.at[blocks + pieces])

    @pl.when(step == 0)
    def _():
        for load in loads + fills:
            load.start()
        for load in loads[: pieces // 2] + fills:
            load.wait()

    @pl.when(step == 1)
    def _():
        for load in loads[pieces // 2 :]:
            load.wait()
        store.start()

    x = x_buf[pl.ds(pl.multiple_of(step * tile, tile), tile), :]
    gate = mm(x, weight_buf[:, :units])
    lift = mm(x, weight_buf[:, units : 2 * units])
    back = mm(dy_ref[...], weight_buf[:, 2 * units :])
    sigmoid = 1.0 / (1.0 + jnp.exp(-gate))
    silu = gate * sigmoid
    activated[...] = (silu * lift).astype(BF)
    back_ref[:, units:] = (back * silu).astype(BF)
    back_ref[:, :units] = (back * lift * (sigmoid * (1.0 + gate * (1.0 - sigmoid)))).astype(BF)

    @pl.when(step == 1)
    def _():
        store.wait()


def hidden_units(places, chunks, dy_all, parts):
    total, width = dy_all.shape
    columns = parts[0].shape[1]
    units = columns // 3
    blocks = places.shape[0]
    tile = total // 2
    return pl.pallas_call(
        functools.partial(hidden_kernel, (len(chunks), len(parts)), blocks),
        out_shape=(
            jax.ShapeDtypeStruct((total, width), BF),
            jax.ShapeDtypeStruct((total, 2 * units), BF),
            jax.ShapeDtypeStruct((total, units), BF),
        ),
        grid=(2,),
        in_specs=[SCALARS, pl.BlockSpec((tile, width), lambda i: (i, 0))]
        + [ANY] * (len(chunks) + len(parts)),
        out_specs=(
            ANY,
            pl.BlockSpec((tile, 2 * units), lambda i: (i, 0)),
            pl.BlockSpec((tile, units), lambda i: (i, 0)),
        ),
        scratch_shapes=[
            pltpu.VMEM((total, width), BF),
            pltpu.VMEM((width, columns), BF),
            pltpu.SemaphoreType.DMA((blocks + max(len(chunks), 2) + 1,)),
        ],
        compiler_params=params(),
        cost_estimate=cost(2 * total * width * columns, dy_all, dy_all, *parts),
        name="hidden",
    )(places, dy_all, *chunks, *parts)


def grads_kernel(counts, highs, flags, *refs):
    lefts, refs = refs[:counts], refs[counts:]
    rights, refs = refs[:counts], refs[counts:]
    outs, refs = refs[: 2 * highs * counts], refs[2 * highs * counts :]
    buffer, sems = refs[-2:]
    sorts = refs[:-2]
    step = pl.program_id(0)
    slot = lax.rem(step, 2)
    depth = buffer.shape[0] // 4

    def stores(high):
        return [
            pltpu.make_async_copy(
                sorts[k].at[high % 2, dy],
                outs[(k * highs + high) * 2 + dy],
                sems.at[high % 2, 2 * k + dy],
            )
            for k in range(counts)
            for dy in range(2)
        ]

    for high in range(2, highs):

        @pl.when(step == high)
        def _(high=high):
            for store in stores(high - 2):
                store.wait()

    for k, (left, right) in enumerate(zip(lefts, rights)):
        size = right.shape[1]
        buffer[:, :size] = mm_tn(left[...], right[...]).astype(BF)
        for low in range(2):
            for dy in range(2):
                place = ((flags[0] ^ low) * 2 + (flags[2] ^ dy)) * depth
                sorts[k][slot, dy, low] = buffer[
                    pl.ds(pl.multiple_of(place, depth), depth), :size
                ]
    for high in range(highs):

        @pl.when(step == high)
        def _(high=high):
            for store in stores(high):
                store.start()
            if high == highs - 1:
                for store in stores(high - 1) + stores(high):
                    store.wait()


def weight_grads(flags, highs, lefts, rights):
    total, width = lefts[0].shape
    depth = width // (4 * highs)
    sizes = [right.shape[1] for right in rights]
    shapes = []
    for size in sizes:
        shapes += [jax.ShapeDtypeStruct((2, depth, size), BF)] * (2 * highs)

    def rows_of(h, flags):
        return (0, lax.rem(flags[1] + h, highs))

    outs = pl.pallas_call(
        functools.partial(grads_kernel, len(lefts), highs),
        out_shape=tuple(shapes),
        grid_spec=pltpu.PrefetchScalarGridSpec(
            num_scalar_prefetch=1,
            grid=(highs,),
            in_specs=[pl.BlockSpec((total, 4 * depth), rows_of) for _ in lefts]
            + [pl.BlockSpec(right.shape, lambda h, flags: (0, 0)) for right in rights],
            out_specs=(ANY,) * len(shapes),
            scratch_shapes=[pltpu.VMEM((2, 2, 2, depth, size), BF) for size in sizes]
            + [
                pltpu.VMEM((4 * depth, max(sizes)), BF),
                pltpu.SemaphoreType.DMA((2, 2 * len(sizes))),
            ],
        ),
        compiler_params=params(),
        cost_estimate=cost(2 * total * width * sum(sizes), *lefts, *rights, *shapes),
        name="grads",
    )(flags, *lefts, *rights)
    each = 2 * highs
    return [
        (list(outs[k * each : (k + 1) * each : 2]), list(outs[k * each + 1 : (k + 1) * each : 2]))
        for k in range(len(lefts))
    ]


def attend_kernel(own, parts, flags, bases, queries, *refs):
    if own:
        pairs, refs = refs[:parts], refs[parts:]
        lows, ends, within, sums, peaks, totals, pair_buf, sems = refs
    else:
        sums, peaks, totals, *refs = refs
        pairs, refs = refs[:parts], refs[parts:]
        lows, ends, within, mixed, log_sums, mixed_low, pair_buf, sems = refs
    count = queries.shape[0]
    half = count // 2
    highs = parts // 2
    loads = []
    for p in range(parts):
        place = pl.ds((p % 2) * count, count)
        loads.append(
            pltpu.make_async_copy(pairs[p], pair_buf.at[p // 2, place], sems.at[p])
        )
    for load in loads:
        load.start()
    for load in loads:
        load.wait()
    for head in range(2):
        columns = slice(head * HD, (head + 1) * HD)
        for side in range(2):
            place = slice(side * half, (side + 1) * half)
            query = queries[place, columns] * jnp.asarray(HD ** (-0.5), BF)
            low, end = lows[place, :], ends[place, :]

            def step(high, base, carry):
                peak, total, accum = carry
                scores = mm_nt(query, pair_buf[high, :, :HD])
                position = within[...] + base
                allowed = (position >= low) & (position <= end)
                scores = jnp.where(allowed, scores, MASKED)
                new_peak = jnp.maximum(peak, jnp.max(scores, axis=1, keepdims=True))
                decay = jnp.exp(peak - new_peak)
                probs = jnp.exp(scores - new_peak)
                total = decay * total + jnp.sum(probs, axis=1, keepdims=True)
                accum = decay * accum + mm(probs.astype(BF), pair_buf[high, :, HD:])
                return new_peak, total, accum

            if own:
                start = (
                    jnp.full((half, 1), MASKED, F32),
                    jnp.zeros((half, 1), F32),
                    jnp.zeros((half, HD), F32),
                )
                peak, total, accum = step(0, bases[0], start)
                peaks[head, place, :] = peak
                totals[head, place, :] = total
                sums[place, columns] = accum
                continue

            def far_step(i, carry):
                high = highs - flags[1] + i
                return step(high, bases[high + 1], carry)

            start = (peaks[head, place, :], totals[head, place, :], sums[place, columns])
            peak, total, accum = lax.fori_loop(0, flags[1], far_step, start)
            out = accum / total
            mixed[place, columns] = out
            mixed_low[place, columns] = out.astype(BF)
            log_sums[head, place, :] = peak + jnp.log(total)


def attend(flags, bases, queries, pairs, lows, ends, within, before=None):
    count = queries.shape[0]
    parts = len(pairs)
    low = jax.ShapeDtypeStruct((count, 2 * HD), BF)
    mixed = jax.ShapeDtypeStruct((count, 2 * HD), F32)
    column = jax.ShapeDtypeStruct((2, count, 1), F32)
    before = before or ()
    return pl.pallas_call(
        functools.partial(attend_kernel, not before, parts),
        out_shape=(mixed, column, low) if before else (mixed, column, column),
        in_specs=[SCALARS, SCALARS]
        + [WHOLE] * (1 + len(before))
        + [ANY] * parts
        + [WHOLE] * 3,
        out_specs=(WHOLE,) * 3,
        scratch_shapes=[
            pltpu.VMEM((parts // 2, 2 * count, 2 * HD), BF),
            pltpu.SemaphoreType.DMA((parts,)),
        ],
        compiler_params=params(),
        cost_estimate=cost(16 * count * count * parts * HD, mixed),
        name="attend",
    )(flags, bases, queries, *before, *pairs, lows, ends, within)


def attend_back_kernel(own, parts, flags, bases, source, back, *refs):
    pairs, refs = refs[:parts], refs[parts:]
    lows, ends, within, stats, deltas, *refs = refs
    if own:
        sum_in, cos_ref, sin_ref, *refs = refs
    outs, out_ref, refs = refs[:parts], refs[parts], refs[parts + 1 :]
    pair_buf, queries, backs, probs_buf, score_buf, query_sum, pair_sum, sems, out_sem = refs
    count = source.shape[0]
    highs = parts // 2
    scale = HD ** (-0.5)
    loads = []
    for p in range(parts):
        loads.append(pltpu.make_async_copy(pairs[p], pair_buf.at[p], sems.at[p]))
    for load in loads:
        load.start()
    for head in range(2):
        place = slice(head * count, (head + 1) * count)
        columns = slice(head * HD, (head + 1) * HD)
        queries[place, :] = source[:, columns] * jnp.asarray(scale, BF)
        backs[place, :] = back[:, columns]
    query_sum[...] = sum_in[...] if own else jnp.zeros_like(query_sum)
    for load in loads:
        load.wait()

    def step(i, carry):
        if own:
            b, base = i, bases[0]
        else:
            b = 2 * (highs - flags[1]) + i
            base = bases[b // 2 + 1]
        keys, values = pair_buf[b, :, :HD], pair_buf[b, :, HD:]
        place = pl.multiple_of(lax.rem(i, 2) * count, count)
        position = within[pl.ds(place, count), :] + base
        allowed = (position >= lows[...]) & (position <= ends[...])
        for head in range(2):
            place = slice(head * count, (head + 1) * count)
            scores = mm_nt(keys, queries[place, :])
            probs = jnp.where(allowed, jnp.exp(scores - stats[head : head + 1, :]), 0.0)
            prob_back = mm_nt(values, backs[place, :])
            probs_buf[:, place] = probs.astype(BF)
            score_buf[:, place] = (probs * (prob_back - deltas[head : head + 1, :])).astype(BF)
        pair_sum[:, :HD] = mm(score_buf[...], queries[...]).astype(BF)
        pair_sum[:, HD:] = mm(probs_buf[...], backs[...]).astype(BF)
        query_sum[...] += mm_tn(score_buf[...], keys)
        for p in range(parts):

            @pl.when(b == p)
            def _(p=p):
                store = pltpu.make_async_copy(pair_sum, outs[p], out_sem)
                store.start()
                store.wait()

        return carry

    lax.fori_loop(0, 2 if own else 2 * flags[1], step, 0)
    if not own:
        out_ref[...] = query_sum[...]
        return
    c, s = cos_ref[...], sin_ref[...]
    for head in range(2):
        grad = query_sum[head * count : (head + 1) * count, :] * scale
        a, b = grad[:, : HD // 2], grad[:, HD // 2 :]
        turned = jnp.concatenate([a * c + b * s, b * c - a * s], axis=1)
        out_ref[:, head * HD : (head + 1) * HD] = turned.astype(BF)


def attend_back(flags, bases, queries, back, pairs, lows, ends, within, stats, deltas, more=()):
    count = queries.shape[0]
    parts = len(pairs)
    low = jax.ShapeDtypeStruct((count, 2 * HD), BF)
    last = low if more else jax.ShapeDtypeStruct((2 * count, HD), F32)
    outs = pl.pallas_call(
        functools.partial(attend_back_kernel, bool(more), parts),
        out_shape=(low,) * parts + (last,),
        in_specs=[SCALARS, SCALARS]
        + [WHOLE] * 2
        + [ANY] * parts
        + [WHOLE] * (5 + len(more)),
        out_specs=(ANY,) * parts + (WHOLE,),
        scratch_shapes=[
            pltpu.VMEM((parts, count, 2 * HD), BF),
            pltpu.VMEM((2 * count, HD), BF),
            pltpu.VMEM((2 * count, HD), BF),
            pltpu.VMEM((count, 2 * count), BF),
            pltpu.VMEM((count, 2 * count), BF),
            pltpu.VMEM((2 * count, HD), F32),
            pltpu.VMEM((count, 2 * HD), BF),
            pltpu.SemaphoreType.DMA((parts,)),
            pltpu.SemaphoreType.DMA,
        ],
        compiler_params=params(),
        cost_estimate=cost(20 * count * count * parts * HD, low, low),
        name="attend_back",
    )(flags, bases, queries, back, *pairs, lows, ends, within, stats, deltas, *more)
    return list(outs[0:parts:2]), list(outs[1:parts:2]), outs[parts]


def tie(values):
    return lax.optimization_barrier(values)


class Bag:
    pass


class Weight:
    def __init__(self, keep):
        self.keep = keep


class Sum:
    pass


class Grad:
    pass


def flatten(bag):
    names = sorted(vars(bag))
    return [getattr(bag, name) for name in names], tuple(names)


def unflatten(kind, names, values):
    bag = kind.__new__(kind)
    for name, value in zip(names, values):
        setattr(bag, name, value)
    return bag


for kind in (Bag, Weight, Sum, Grad):
    jax.tree_util.register_pytree_node(kind, flatten, functools.partial(unflatten, kind))


def halves(zl, array):
    c = array.shape[1] // 2
    left, right = array[:, :c], array[:, c:]
    first = zl == 0
    return jnp.where(first, left, right), jnp.where(first, right, left)


def join(zl, own, received):
    first = zl == 0
    return jnp.concatenate([jnp.where(first, own, received), jnp.where(first, received, own)], axis=1)


def turn_back(vectors, cosines, sines):
    half = vectors.shape[-1] // 2
    a, b = vectors[..., :half], vectors[..., half:]
    return jnp.concatenate([a * cosines + b * sines, b * cosines - a * sines], axis=-1)


def body(
    hidden_in,
    segments,
    attn_gain,
    query_weight,
    key_weight,
    value_weight,
    output_weight,
    mlp_gain,
    gate_weight,
    up_weight,
    down_weight,
    cotangent,
):
    wide_count = lax.axis_size("wide")
    devices = wide_count * 4
    mover = Mover(devices)
    highs = mover.highs
    wide = lax.axis_index("wide")
    tp = lax.axis_index("tp")
    y, zl, zh = wide & 1, (wide >> 1) & 1, wide >> 2
    first = zl == 0
    flags = jnp.stack([zl, zh, y]).astype(jnp.int32)
    micro, local, width = hidden_in.shape
    rows = micro * local
    wide_tokens = segments.shape[1]
    head_rows = 8 * local
    scale = HD ** (-0.5)
    swap = mover.swap
    shifts = range(1, highs)
    places = jnp.stack(
        [
            (((zh + shift) % highs) * 2 + (zl ^ low)) * 2 + (y ^ dy)
            for shift in range(highs)
            for dy in range(2)
            for low in range(2)
        ]
    ).astype(jnp.int32)

    def highs_of(value, causal=False):
        return [mover.from_high(value, shift, causal) for shift in shifts]

    def over_y(values):
        return [swap(value, YDIR) for value in values]

    inputs = hidden_in.reshape(rows, width).astype(F32)
    scale_one = lax.rsqrt(jnp.mean(inputs * inputs, axis=-1, keepdims=True) + EPSILON)
    plain_one = inputs * scale_one

    gain_one = attn_gain.astype(F32)[:, None]
    gain_two = mlp_gain.astype(F32)[:, None]

    def gained(weight, gain):
        return (weight.astype(F32) * gain).astype(BF)

    pair_weight = jnp.concatenate([key_weight, value_weight], axis=1)
    gate_keep, gate_send = halves(zl, gained(gate_weight, gain_two))
    up_keep, up_send = halves(zl, gained(up_weight, gain_two))
    down_keep, down_send = halves(zl, down_weight.T)
    units = 512
    groups = gate_keep.shape[1] // units

    def cut_units(c, gate, up, down):
        cut = slice(c * units, (c + 1) * units)
        return jnp.concatenate([gate[:, cut], up[:, cut], down[:, cut]], axis=1)

    live = Bag()

    def cut():
        vars(live).update(vars(tie(live)))

    def pair_of_segments():
        own, got = live.segments, live.seg_got
        return [jnp.stack([jnp.where(first, own, got), jnp.where(first, got, own)])]

    def blocks_of(weight):
        blocks = [weight.keep, weight.got, weight.yk, weight.yg]
        for group in zip(weight.hk, weight.hg, weight.hyk, weight.hyg):
            blocks += group
        return blocks

    def own_first(row):
        low, high = row[:local], row[local:]
        live.row = jnp.where(first, low, high)
        live.rz = swap(jnp.where(first, high, low), ZLOW)
        live.rx = swap(live.row, XDIR)
        live.rc = [swap(live.row, CORE)]

    def rows_first(row):
        live.row, live.rx, live.rz = row, swap(row, XDIR), swap(row, ZLOW)
        live.rc = [swap(row, CORE)]

    def rows_second():
        live.rd = swap(live.rz, XDIR)
        live.rc += [swap(value, CORE) for value in (live.rx, live.rz)]

    def rows_last():
        row, x, z, d, c = live.row, live.rx, live.rz, live.rd, live.rc
        del live.row, live.rx, live.rz, live.rd, live.rc
        return [row, c[0], x, c[1], z, c[2], d, swap(d, CORE)]

    def stack_first(row):
        low, high = row[:local], row[local:]
        live.row = jnp.where(first, low, high)
        live.rz = swap(jnp.where(first, high, low), ZLOW)

    def stack_second():
        live.stack = jnp.concatenate([live.row, live.rz])
        live.stack_x = swap(live.stack, XDIR)
        live.stack_c = swap(live.stack, CORE)
        del live.row, live.rz

    def stack_last():
        stacks = [live.stack, live.stack_c, live.stack_x, swap(live.stack_x, CORE)]
        del live.stack, live.stack_c, live.stack_x
        return stacks

    def sums_start(pair):
        part = Sum()
        part.keep, part.send = pair
        return part

    def sums_core(part):
        part.send = swap(part.send, CORE)

    def sums_combine(part):
        part.own, part.near, part.low, part.far = combine(part.keep, part.send)
        del part.keep, part.send

    def sums_far(part):
        part.far = swap(part.far, XDIR)

    def sums_near(part):
        low = (part.low.astype(F32) + part.far.astype(F32)).astype(BF)
        part.low, part.near = swap(low, ZLOW), swap(part.near, XDIR)
        del part.far

    def sums_total(part):
        return part.own + part.near.astype(F32) + part.low.astype(F32)

    def own_x(part):
        part.far, part.near = swap(part.far, XDIR), swap(part.near, XDIR)

    def own_zl(part):
        low = (part.low.astype(F32) + part.far.astype(F32)).astype(BF)
        part.low = swap(low, ZLOW)
        del part.far

    def own_total(part):
        mine, other = part.own + part.near.astype(F32), part.low.astype(F32)
        return jnp.concatenate([jnp.where(first, mine, other), jnp.where(first, other, mine)])

    def grad_start(pair):
        part = Grad()
        part.keep, part.send = pair
        return part

    def grad_y_far(part):
        part.send[1:] = [swap(part.send[shift], YDIR) for shift in shifts]

    def grad_y_near(part):
        part.send[0] = swap(part.send[0], YDIR)

    def grad_h(part, low):
        moved = []
        for shift in shifts:
            half = part.keep[shift][low].astype(F32) + part.send[shift][low].astype(F32)
            moved.append(mover.to_high(half.astype(BF), shift))
        if low:
            part.moved_got = moved
        else:
            part.moved_own = moved

    def grad_zl(part):
        totals = []
        for low in range(2):
            total = part.keep[0][low].astype(F32) + part.send[0][low].astype(F32)
            for moved in (part.moved_own, part.moved_got)[low]:
                total = total + moved.astype(F32)
            totals.append(total)
        part.own, part.got = totals[0], swap(totals[1].astype(BF), ZLOW)
        del part.keep, part.send, part.moved_own, part.moved_got

    span = jnp.arange(local, dtype=jnp.int32)
    steps = jnp.arange(4, dtype=jnp.int32)
    within = (
        ((zl ^ jnp.arange(2, dtype=jnp.int32))[:, None, None] * 2 * wide_tokens)
        + ((tp ^ steps) * local)[None, :, None]
        + span[None, None, :]
    ).reshape(head_rows)
    row_positions = (zh * 4 + y) * wide_tokens + within
    bases = jnp.stack([((zh + shift) % highs) * 4 * wide_tokens for shift in range(highs)])
    bases = bases.astype(jnp.int32)
    key_within = jnp.concatenate([within + (y ^ dy) * wide_tokens for dy in range(2)])
    freqs = jnp.exp(-math.log(ROPE_BASE) * (2.0 * jnp.arange(HD // 2, dtype=F32) / HD))
    angles = row_positions.astype(F32)[:, None] * freqs[None, :]
    tables = (jnp.cos(angles), jnp.sin(angles))

    live.upstream = cotangent.reshape(rows, width)
    qkv_own, row_one = tie(
        [
            jnp.concatenate([gained(w, gain_one) for w in (query_weight, pair_weight)], axis=1),
            plain_one.astype(BF),
        ]
    )
    live.q = q = Weight(qkv_own)
    q.hk = highs_of(q.keep)
    q.got = swap(q.keep, ZLOW)
    q.yk = swap(q.keep, YDIR)
    stack_first(row_one)
    live.u_send = [cut_units(c, gate_send, up_send, down_send) for c in range(groups)]
    live.u = u = [Weight(cut_units(c, gate_keep, up_keep, down_keep)) for c in range(groups)]
    live.o_own = output_weight.T
    live.segments = segments
    live.seg_got = swap(segments, ZLOW)
    cut()
    q, u = live.q, live.u
    q.hg = highs_of(q.got)
    q.hyk = over_y(q.hk)
    q.yg = swap(q.got, YDIR)
    stack_second()
    live.o_got = swap(live.o_own, ZLOW)
    live.seg = pair_of_segments()
    live.seg.append(swap(live.seg[0], YDIR))
    cut()
    q, u = live.q, live.u
    q.hyg = over_y(q.hg)
    live.out_pair = jnp.concatenate([live.o_own, live.o_got])
    live.out_h = highs_of(live.out_pair)
    live.seg = [jnp.concatenate(live.seg)]
    live.seg += highs_of(live.seg[0])
    live.dx = swap(live.upstream, XDIR)
    live.normed, live.queries, live.pair = gathered_matmul(
        places, stack_last(), blocks_of(q), tables
    )
    cut()
    u = live.u
    live.pair_h, live.pair_y = highs_of(live.pair, causal=True), swap(live.pair, YDIR)
    live.out_y = swap(live.out_pair, YDIR)
    live.dz = swap(live.upstream, ZLOW)
    seg_all = lax.dynamic_index_in_dim(jnp.concatenate(live.seg), zl, 1, keepdims=False)
    own_pair = lax.dynamic_index_in_dim(live.seg[0][:2], zl, 1, keepdims=False)
    del live.seg
    own_rows = jnp.stack(
        [
            lax.dynamic_slice_in_dim(
                lax.dynamic_index_in_dim(own_pair, zl ^ dzl, 0, keepdims=False),
                (tp ^ dtp) * local,
                local,
                0,
            )
            for dzl in range(2)
            for dtp in range(4)
        ]
    ).reshape(head_rows)
    live.starts = jnp.sum(
        (seg_all.reshape(1, -1) < own_rows[:, None]).astype(jnp.int32), axis=1
    )
    spots = (
        live.starts.reshape(head_rows, 1),
        row_positions.reshape(head_rows, 1),
        key_within.reshape(1, 2 * head_rows),
    )
    live.before = attend(flags, bases, live.queries, [live.pair, live.pair_y], *spots)
    cut()
    u = live.u
    pair_hy = over_y(live.pair_h)
    u[0].got = swap(live.u_send[0], ZLOW)
    u[0].hk = highs_of(u[0].keep)
    live.out_hy = over_y(live.out_h)
    live.dd = swap(live.dz, XDIR)
    live.own_pairs, live.far_pairs = [live.pair, live.pair_y], []
    for values in zip(live.pair_h, pair_hy):
        live.far_pairs += values
    del live.pair, live.pair_y, live.pair_h
    live.mixed, live.log_sums, live.mixed_all = attend(
        flags, bases, live.queries, live.far_pairs, *spots, live.before
    )
    del live.before
    cut()
    live.log_sums = live.log_sums.reshape(2, head_rows)
    u = live.u
    live.o = [live.out_pair, live.out_y]
    for values in zip(live.out_h, live.out_hy):
        live.o += values
    del live.out_pair, live.out_y, live.out_h, live.out_hy
    live.a = sums_start(partial_matmul(places, [(live.mixed_all, 0, 2 * HD)], [live.o], [0]))
    cut()
    u = live.u
    sums_core(live.a)
    u[0].hyk = over_y(u[0].hk)
    u[1].got = swap(live.u_send[1], ZLOW)
    sums_combine(live.a)
    own_x(live.a)
    cut()
    u = live.u
    own_zl(live.a)
    live.dc = [swap(d, CORE) for d in (live.upstream, live.dx, live.dz, live.dd)]
    cut()
    u = live.u
    live.hidden = hidden = inputs + own_total(live.a)
    del live.a
    scale_two = lax.rsqrt(jnp.mean(hidden * hidden, axis=-1, keepdims=True) + EPSILON)
    plain_two = hidden * scale_two
    rows_first(plain_two.astype(BF))
    u[0].yg = swap(u[0].got, YDIR)
    u[0].hg = highs_of(u[0].got)
    u[1].yg = swap(u[1].got, YDIR)
    cut()
    u = live.u
    rows_second()
    u[0].yk = swap(u[0].keep, YDIR)
    u[0].hyg = over_y(u[0].hg)
    u[1].hg = highs_of(u[1].got)
    d_x, d_z, d_d, d_cores = live.dx, live.dz, live.dd, live.dc
    live.dy_all = assemble(
        [live.upstream, d_cores[0], d_x, d_cores[1], d_z, d_cores[2], d_d, d_cores[3]]
    )
    del live.dx, live.dz, live.dd, live.dc
    cut()
    u = live.u
    chunks = rows_last()
    u[1].yk = swap(u[1].keep, YDIR)
    u[1].hk = highs_of(u[1].keep)
    u[1].hyg = over_y(u[1].hg)
    live.backs, live.acts = [None] * 2, [None] * 2

    def unit_work(c, source):
        live.x_all, live.backs[c], live.acts[c] = hidden_units(
            places, source, live.dy_all, blocks_of(live.u[c])
        )

    def unit_grads(c):
        pairs = weight_grads(
            flags, highs, [live.x_all, live.dy_all], [live.backs[c], live.acts[c]]
        )
        return [grad_start(pair) for pair in pairs]

    unit_work(0, chunks)
    live.g = unit_grads(0)
    cut()
    u, g = live.u, live.g
    u[1].hyk = over_y(u[1].hk)
    cut()
    u, g = live.u, live.g
    grad_y_far(g[1])
    unit_work(1, [live.x_all])
    cut()
    g = live.g
    grad_y_far(g[0])
    grad_h(g[1], 1)
    live.unit_blocks = [blocks_of(weight) for weight in live.u]
    del live.u
    live.e = sums_start(
        partial_matmul(
            places,
            [(back, 0, 2 * units) for back in live.backs],
            live.unit_blocks,
            [0] * groups,
        )
    )
    cut()
    g = live.g
    sums_core(live.e)
    grad_y_near(g[0])
    grad_h(g[0], 1)
    live.g += unit_grads(1)
    cut()
    g = live.g
    sums_combine(live.e)
    sums_far(live.e)
    grad_h(g[1], 0)
    grad_y_far(g[3])
    cut()
    g = live.g
    sums_near(live.e)
    grad_h(g[0], 0)
    grad_y_far(g[2])
    cut()
    weighted_two = sums_total(live.e)
    del live.e
    hidden_back = live.upstream.astype(F32) + scale_two * (
        weighted_two - plain_two * jnp.mean(weighted_two * plain_two, axis=-1, keepdims=True)
    )
    g = live.g
    own_first(hidden_back.astype(BF))
    grad_y_near(g[2])
    grad_h(g[2], 0)
    live.d = sums_start(
        partial_matmul(
            places,
            [(act, 0, units) for act in live.acts],
            live.unit_blocks,
            [2 * units] * groups,
        )
    )
    del live.acts, live.backs, live.unit_blocks
    cut()
    g = live.g
    rows_second()
    grad_y_near(g[3])
    grad_h(g[3], 0)
    cut()
    g = live.g
    grad_y_near(g[1])
    grad_h(g[3], 1)
    sums_core(live.d)
    live.attn_back, live.back, live.deltas = gathered_matmul(
        places, rows_last(), live.o, mixed=live.mixed
    )
    cut()
    g = live.g
    live.turned = (
        live.starts.reshape(1, head_rows),
        row_positions.reshape(1, head_rows),
        key_within.reshape(2 * head_rows, 1),
        live.log_sums,
        live.deltas.T,
    )
    live.k_keep, live.k_send, live.query_sum = attend_back(
        flags, bases, live.queries, live.back, live.far_pairs, *live.turned
    )
    cut()
    g = live.g
    live.k_send = [swap(value, YDIR) for value in live.k_send]
    grad_zl(g[1])
    grad_h(g[2], 1)
    grad_zl(g[3])
    keep, send, live.query_back = attend_back(
        flags,
        bases,
        live.queries,
        live.back,
        live.own_pairs,
        *live.turned,
        (live.query_sum, *tables),
    )
    live.k_keep, live.k_send = keep + live.k_keep, send + live.k_send
    del live.turned, live.query_sum
    sums_combine(live.d)
    (grads_out,) = weight_grads(flags, highs, [live.attn_back], [live.mixed_all])
    live.g_out = grad_start(grads_out)
    cut()
    g = live.g
    live.k_moved = []
    for shift in shifts:
        half = live.k_keep[shift].astype(F32) + live.k_send[shift].astype(F32)
        live.k_moved.append(mover.to_high(half.astype(BF), shift, causal=True))
    live.k_near = swap(live.k_send[0], YDIR)
    grad_zl(g[2])
    grad_y_far(live.g_out)
    sums_far(live.d)
    (grads_q,) = weight_grads(flags, highs, [live.normed], [live.query_back])
    live.g_q = grad_start(grads_q)
    cut()
    g = live.g
    total = live.k_keep[0].astype(F32) + live.k_near.astype(F32)
    for moved in live.k_moved:
        total = total + moved.astype(F32)
    del live.k_keep, live.k_send, live.k_moved, live.k_near
    key_back = turn_back(total[:, :HD], *tables).astype(BF)
    live.pair_back = jnp.concatenate([key_back, total[:, HD:].astype(BF)], axis=1)
    grad_zl(g[0])
    grad_h(live.g_out, 0)
    grad_h(live.g_out, 1)
    grad_y_far(live.g_q)
    grad_y_near(live.g_q)
    (grads_p,) = weight_grads(flags, highs, [live.normed], [live.pair_back])
    live.g_p = grad_start(grads_p)
    cut()
    g = live.g
    grad_h(live.g_q, 0)
    grad_h(live.g_q, 1)
    grad_y_far(live.g_p)
    sums_near(live.d)
    live.n = sums_start(
        partial_matmul(
            places,
            [(live.query_back, 0, 2 * HD), (live.pair_back, 0, 2 * HD)],
            [blocks_of(live.q)] * 2,
            [0, 2 * HD],
        )
    )
    cut()
    g = live.g
    sums_core(live.n)
    grad_y_near(live.g_out)
    grad_zl(live.g_q)
    grad_h(live.g_p, 1)
    cut()
    g = live.g
    sums_combine(live.n)
    own_x(live.n)
    grad_zl(live.g_out)
    grad_y_near(live.g_p)
    grad_h(live.g_p, 0)
    cut()
    g = live.g
    own_zl(live.n)
    grad_zl(live.g_p)

    def unit_columns(part, at):
        cut = slice(at * units, (at + 1) * units)
        own = jnp.concatenate([piece.own[:, cut] for piece in part], axis=1)
        return join(
            zl, own, jnp.concatenate([piece.got[:, cut] for piece in part], axis=1).astype(F32)
        )

    gate_plain, up_plain = unit_columns(g[0::2], 0), unit_columns(g[0::2], 1)
    live.shards = (gate_plain * gain_two, up_plain * gain_two, unit_columns(g[1::2], 0).T)
    live.gain_two = jnp.sum(gate_plain * gate_weight.astype(F32), axis=1) + jnp.sum(
        up_plain * up_weight.astype(F32), axis=1
    )
    live.layer_out = (live.hidden + sums_total(live.d)).astype(BF)
    cut()
    weighted_one = own_total(live.n)
    input_grad = hidden_back + scale_one * (
        weighted_one - plain_one * jnp.mean(weighted_one * plain_one, axis=-1, keepdims=True)
    )
    g = live.g
    def columns_of(part):
        return part.own + part.got.astype(F32)

    query_plain, pair_plain = columns_of(live.g_q), columns_of(live.g_p)
    gain_sums = jnp.stack(
        [
            jnp.sum(query_plain * query_weight.astype(F32), axis=1)
            + jnp.sum(pair_plain * pair_weight.astype(F32), axis=1),
            live.gain_two,
        ]
    )
    gain_sums = gain_sums + swap(gain_sums, CORE)
    gain_sums = gain_sums + swap(gain_sums, XDIR)
    pair_shard = pair_plain * gain_one
    shape = hidden_in.shape
    return (
        live.layer_out.reshape(shape),
        input_grad.reshape(shape),
        gain_sums[0],
        query_plain * gain_one,
        pair_shard[:, :HD],
        pair_shard[:, HD:],
        columns_of(live.g_out).T,
        gain_sums[1],
        *live.shards,
    )


def solution(mesh):
    rows = P(None, ("wide", "tp"), None)
    columns = P("wide", "tp")
    flipped = P("tp", "wide")
    gain = P("wide")
    weights = (columns, columns, columns, flipped, gain, columns, columns, flipped)
    return jax.shard_map(
        body,
        mesh=mesh,
        in_specs=(rows, P(None, "wide"), gain) + weights + (rows,),
        out_specs=(rows, rows, gain) + weights,
        check_vma=False,
    )
```

```python
import functools
import math

import jax
import jax.numpy as jnp
from jax import lax
from jax.experimental import pallas as pl
from jax.experimental.pallas import tpu as pltpu
from jax.sharding import PartitionSpec as P

HD = 256
EPSILON = 1e-06
ROPE_BASE = 1000042.0
MASKED = -1e30
BF = jnp.bfloat16
F32 = jnp.float32
AXES = ("wide", "tp")
VMEM_LIMIT = 56 << 20

CORE, XDIR, YDIR, ZLOW = 1, 2, 4, 8
CONTRACT_ROWS = (((0,), (0,)), ((), ()))
CONTRACT_COLUMNS = (((1,), (1,)), ((), ()))


def mm(left, right):
    return jnp.dot(left, right, preferred_element_type=F32)


def mm_nt(left, right):
    return lax.dot_general(left, right, CONTRACT_COLUMNS, preferred_element_type=F32)


def mm_tn(left, right):
    return lax.dot_general(left, right, CONTRACT_ROWS, preferred_element_type=F32)


ANY = pl.BlockSpec(memory_space=pl.ANY)
WHOLE = pl.BlockSpec(memory_space=pltpu.VMEM)
SCALARS = pl.BlockSpec(memory_space=pltpu.SMEM)


def params():
    return pltpu.CompilerParams(vmem_limit_bytes=VMEM_LIMIT)


def cost(flops, *arrays):
    moved = sum(math.prod(a.shape) * jnp.dtype(a.dtype).itemsize for a in arrays)
    return pl.CostEstimate(flops=12 * int(flops), transcendentals=0, bytes_accessed=int(moved))


class Mover:
    def __init__(self, devices):
        self.devices = devices
        self.highs = devices // 16

    def swap(self, value, mask):
        return lax.ppermute(value, AXES, [(i, i ^ mask) for i in range(self.devices)])

    def from_high(self, value, shift, causal=False):
        pairs = []
        for dst in range(self.devices):
            zh = dst // 16
            src_zh = (zh + shift) % self.highs
            if causal and src_zh > zh:
                continue
            pairs.append((src_zh * 16 + dst % 16, dst))
        return lax.ppermute(value, AXES, pairs)

    def to_high(self, value, shift, causal=False):
        pairs = []
        for src in range(self.devices):
            zh = src // 16
            dst_zh = (zh + shift) % self.highs
            if causal and dst_zh > zh:
                continue
            pairs.append((src, dst_zh * 16 + src % 16))
        return lax.ppermute(value, AXES, pairs)


def weight_loads(parts, places, depth, buffer, sems, start):
    loads = []
    for part in parts:
        for low in range(part.shape[0] // depth):
            at = len(loads)
            row = pl.multiple_of(places[at] * depth, depth)
            loads.append(
                pltpu.make_async_copy(
                    part.at[pl.ds(low * depth, depth)],
                    buffer.at[pl.ds(row, depth)],
                    sems.at[start + at],
                )
            )
    return loads


def gathered_kernel(rotary, stacked, parts, blocks, places, *refs):
    stacks, refs = refs[:stacked], refs[stacked:]
    weights, refs = refs[:parts], refs[parts:]
    if rotary:
        cos_ref, sin_ref, all_ref, out_ref, pair_ref = refs[:5]
    else:
        mixed_ref, all_ref, out_ref, delta_ref = refs[:4]
    rows_buf, weight_buf, sems = refs[-3:]
    rows = rows_buf.shape[0] // 8
    if stacked == 4:
        chunks = [stacks[k % 4].at[pl.ds(k // 4 * rows, rows)] for k in range(8)]
    else:
        chunks = stacks
    depth = weight_buf.shape[0] // blocks
    fills = weight_loads(weights, places, depth, weight_buf, sems, 9)
    loads = [
        pltpu.make_async_copy(chunks[k], rows_buf.at[pl.ds(k * rows, rows)], sems.at[k])
        for k in range(8)
    ]
    for load in fills + loads:
        load.start()
    for fill in fills:
        fill.wait()
    tile = 4 * rows
    for half in range(2):
        for k in range(4):
            loads[4 * half + k].wait()
        place = slice(half * tile, (half + 1) * tile)
        left = rows_buf[place, :]
        if rotary:
            c, s = cos_ref[place, :], sin_ref[place, :]
            for head in range(3):
                product = mm(left, weight_buf[:, head * HD : (head + 1) * HD])
                a, b = product[:, : HD // 2], product[:, HD // 2 :]
                turned = jnp.concatenate([a * c - b * s, b * c + a * s], axis=1).astype(BF)
                if head < 2:
                    out_ref[place, head * HD : (head + 1) * HD] = turned
                else:
                    pair_ref[place, :HD] = turned
            pair_ref[place, HD:] = mm(left, weight_buf[:, 3 * HD :]).astype(BF)
        else:
            low = mm(left, weight_buf[...]).astype(BF)
            out_ref[place, :] = low
            product = low.astype(F32) * mixed_ref[place, :]
            for head in range(2):
                delta_ref[place, head : head + 1] = jnp.sum(
                    product[:, head * HD : (head + 1) * HD], axis=1, keepdims=True
                )
    store = pltpu.make_async_copy(rows_buf, all_ref, sems.at[8])
    store.start()
    store.wait()


def gathered_matmul(places, chunks, parts, tables=None, mixed=None):
    rows, width = chunks[0].shape
    rows = rows * len(chunks) // 8
    columns = parts[0].shape[1]
    blocks = places.shape[0]
    more = tables or (mixed,)
    out = jax.ShapeDtypeStruct((8 * rows, 2 * HD), BF)
    outs = (out, out) if tables else (out, jax.ShapeDtypeStruct((8 * rows, 2), F32))
    return pl.pallas_call(
        functools.partial(gathered_kernel, bool(tables), len(chunks), len(parts), blocks),
        out_shape=(jax.ShapeDtypeStruct((8 * rows, width), BF),) + outs,
        in_specs=[SCALARS] + [ANY] * (len(chunks) + len(parts)) + [WHOLE] * len(more),
        out_specs=(ANY,) + (WHOLE,) * len(outs),
        scratch_shapes=[
            pltpu.VMEM((8 * rows, width), BF),
            pltpu.VMEM((width, columns), BF),
            pltpu.SemaphoreType.DMA((9 + blocks,)),
        ],
        compiler_params=params(),
        cost_estimate=cost(2 * 8 * rows * width * columns, *chunks, *chunks, *parts),
        name="gathered",
    )(places, *chunks, *parts, *more)


def partial_kernel(counts, starts, groups, blocks, places, *refs):
    lefts, refs = refs[:counts], refs[counts:]
    sets = []
    for size in groups:
        sets.append(refs[:size])
        refs = refs[size:]
    keep_ref, send_ref, weight_buf, sems = refs
    rows = keep_ref.shape[1]
    width = weight_buf.shape[0]
    depth = width // blocks

    @pl.when(pl.program_id(0) == 0)
    def _():
        fills = []
        column = 0
        for parts, start, left in zip(sets, starts, lefts):
            size = left.shape[1]
            place = pl.ds(column, size)
            cut = [part.at[:, pl.ds(start, size)] for part in parts]
            fills += weight_loads(
                cut, places, depth, weight_buf.at[:, place], sems, len(fills)
            )
            column += size
        for fill in fills:
            fill.start()
        for fill in fills:
            fill.wait()

    tile = 512 if width % 512 == 0 else width
    for at in range(0, width, tile):
        total = None
        column = 0
        for left in lefts:
            size = left.shape[1]
            term = mm_nt(left[...], weight_buf[at : at + tile, column : column + size])
            total = term if total is None else total + term
            column += size
        low = total.astype(BF)
        keep_ref[0, :, at : at + tile] = low[:rows]
        send_ref[0, :, at : at + tile] = low[rows:]


def partial_matmul(places, lefts, sets, starts):
    rows = lefts[0][0].shape[0] // 8
    blocks = places.shape[0]
    width = sum(part.shape[0] for part in sets[0])
    used = sum(size for _, _, size in lefts)
    out = jax.ShapeDtypeStruct((4, rows, width), BF)
    block = pl.BlockSpec((1, rows, width), lambda j: (j, 0, 0))
    flat = [part for parts in sets for part in parts]

    def rows_of(place, size):
        return pl.BlockSpec((2 * rows, size), lambda j: (j, place))

    return pl.pallas_call(
        functools.partial(
            partial_kernel, len(lefts), tuple(starts), tuple(len(p) for p in sets), blocks
        ),
        out_shape=(out, out),
        grid=(4,),
        in_specs=[SCALARS]
        + [rows_of(place, size) for _, place, size in lefts]
        + [ANY] * len(flat),
        out_specs=(block, block),
        scratch_shapes=[
            pltpu.VMEM((width, used), BF),
            pltpu.SemaphoreType.DMA((blocks * len(lefts),)),
        ],
        compiler_params=params(),
        cost_estimate=cost(2 * 8 * rows * width * used, out, out, out, out),
        name="partial",
    )(places, *[left for left, _, _ in lefts], *flat)


def combine_kernel(keep, got, own, across, low, diagonal):
    own[...] = keep[0].astype(F32) + got[0].astype(F32)
    for j, out in ((1, across), (2, low), (3, diagonal)):
        out[...] = (keep[j].astype(F32) + got[j].astype(F32)).astype(BF)


def combine(keep, got):
    _, rows, width = keep.shape
    tile = rows // 2
    wide = pl.BlockSpec((4, tile, width), lambda i: (0, i, 0))
    thin = pl.BlockSpec((tile, width), lambda i: (i, 0))
    return pl.pallas_call(
        combine_kernel,
        out_shape=(jax.ShapeDtypeStruct((rows, width), F32),)
        + (jax.ShapeDtypeStruct((rows, width), BF),) * 3,
        grid=(rows // tile,),
        in_specs=[wide, wide],
        out_specs=(thin,) * 4,
        compiler_params=params(),
        cost_estimate=cost(0, keep, keep, got, got),
        name="combine",
    )(keep, got)


def assemble_kernel(*refs):
    chunks, out, sems = refs[:8], refs[8], refs[9]
    rows = chunks[0].shape[0]
    copies = [
        pltpu.make_async_copy(chunks[k], out.at[pl.ds(k * rows, rows)], sems.at[k])
        for k in range(8)
    ]
    for copy in copies:
        copy.start()
    for copy in copies:
        copy.wait()


def assemble(chunks):
    rows, width = chunks[0].shape
    return pl.pallas_call(
        assemble_kernel,
        out_shape=jax.ShapeDtypeStruct((8 * rows, width), BF),
        in_specs=[ANY] * 8,
        out_specs=WHOLE,
        scratch_shapes=[pltpu.SemaphoreType.DMA((8,))],
        compiler_params=params(),
        cost_estimate=cost(0, *chunks, *chunks),
        name="assemble",
    )(*chunks)


def hidden_kernel(counts, blocks, places, dy_ref, *refs):
    chunks, refs = refs[: counts[0]], refs[counts[0] :]
    weights, refs = refs[: counts[1]], refs[counts[1] :]
    x_all, back_ref, activated, x_buf, weight_buf, sems = refs
    step = pl.program_id(0)
    units = activated.shape[1]
    depth = weight_buf.shape[0] // blocks
    rows = chunks[0].shape[0]
    tile = dy_ref.shape[0]
    fills = weight_loads(weights, places, depth, weight_buf, sems, 0)
    pieces = counts[0] if counts[0] > 1 else 2
    size = x_buf.shape[0] // pieces
    loads = []
    for k in range(pieces):
        source = chunks[k] if counts[0] > 1 else chunks[0].at[pl.ds(k * size, size)]
        loads.append(
            pltpu.make_async_copy(source, x_buf.at[pl.ds(k * size, size)], sems.at[blocks + k])
        )
    store = pltpu.make_async_copy(x_buf, x_all, sems.at[blocks + pieces])

    @pl.when(step == 0)
    def _():
        for load in loads + fills:
            load.start()
        for load in loads[: pieces // 2] + fills:
            load.wait()

    @pl.when(step == 1)
    def _():
        for load in loads[pieces // 2 :]:
            load.wait()
        store.start()

    x = x_buf[pl.ds(pl.multiple_of(step * tile, tile), tile), :]
    gate = mm(x, weight_buf[:, :units])
    lift = mm(x, weight_buf[:, units : 2 * units])
    back = mm(dy_ref[...], weight_buf[:, 2 * units :])
    sigmoid = 1.0 / (1.0 + jnp.exp(-gate))
    silu = gate * sigmoid
    activated[...] = (silu * lift).astype(BF)
    back_ref[:, units:] = (back * silu).astype(BF)
    back_ref[:, :units] = (back * lift * (sigmoid * (1.0 + gate * (1.0 - sigmoid)))).astype(BF)

    @pl.when(step == 1)
    def _():
        store.wait()


def hidden_units(places, chunks, dy_all, parts):
    total, width = dy_all.shape
    columns = parts[0].shape[1]
    units = columns // 3
    blocks = places.shape[0]
    tile = total // 2
    return pl.pallas_call(
        functools.partial(hidden_kernel, (len(chunks), len(parts)), blocks),
        out_shape=(
            jax.ShapeDtypeStruct((total, width), BF),
            jax.ShapeDtypeStruct((total, 2 * units), BF),
            jax.ShapeDtypeStruct((total, units), BF),
        ),
        grid=(2,),
        in_specs=[SCALARS, pl.BlockSpec((tile, width), lambda i: (i, 0))]
        + [ANY] * (len(chunks) + len(parts)),
        out_specs=(
            ANY,
            pl.BlockSpec((tile, 2 * units), lambda i: (i, 0)),
            pl.BlockSpec((tile, units), lambda i: (i, 0)),
        ),
        scratch_shapes=[
            pltpu.VMEM((total, width), BF),
            pltpu.VMEM((width, columns), BF),
            pltpu.SemaphoreType.DMA((blocks + max(len(chunks), 2) + 1,)),
        ],
        compiler_params=params(),
        cost_estimate=cost(2 * total * width * columns, dy_all, dy_all, *parts),
        name="hidden",
    )(places, dy_all, *chunks, *parts)


def grads_kernel(counts, highs, flags, *refs):
    lefts, refs = refs[:counts], refs[counts:]
    rights, refs = refs[:counts], refs[counts:]
    outs, refs = refs[: 2 * highs * counts], refs[2 * highs * counts :]
    buffer, sems = refs[-2:]
    sorts = refs[:-2]
    step = pl.program_id(0)
    slot = lax.rem(step, 2)
    depth = buffer.shape[0] // 4

    def stores(high):
        return [
            pltpu.make_async_copy(
                sorts[k].at[high % 2, dy],
                outs[(k * highs + high) * 2 + dy],
                sems.at[high % 2, 2 * k + dy],
            )
            for k in range(counts)
            for dy in range(2)
        ]

    for high in range(2, highs):

        @pl.when(step == high)
        def _(high=high):
            for store in stores(high - 2):
                store.wait()

    for k, (left, right) in enumerate(zip(lefts, rights)):
        size = right.shape[1]
        buffer[:, :size] = mm_tn(left[...], right[...]).astype(BF)
        for low in range(2):
            for dy in range(2):
                place = ((flags[0] ^ low) * 2 + (flags[2] ^ dy)) * depth
                sorts[k][slot, dy, low] = buffer[
                    pl.ds(pl.multiple_of(place, depth), depth), :size
                ]
    for high in range(highs):

        @pl.when(step == high)
        def _(high=high):
            for store in stores(high):
                store.start()
            if high == highs - 1:
                for store in stores(high - 1) + stores(high):
                    store.wait()


def weight_grads(flags, highs, lefts, rights):
    total, width = lefts[0].shape
    depth = width // (4 * highs)
    sizes = [right.shape[1] for right in rights]
    shapes = []
    for size in sizes:
        shapes += [jax.ShapeDtypeStruct((2, depth, size), BF)] * (2 * highs)

    def rows_of(h, flags):
        return (0, lax.rem(flags[1] + h, highs))

    outs = pl.pallas_call(
        functools.partial(grads_kernel, len(lefts), highs),
        out_shape=tuple(shapes),
        grid_spec=pltpu.PrefetchScalarGridSpec(
            num_scalar_prefetch=1,
            grid=(highs,),
            in_specs=[pl.BlockSpec((total, 4 * depth), rows_of) for _ in lefts]
            + [pl.BlockSpec(right.shape, lambda h, flags: (0, 0)) for right in rights],
            out_specs=(ANY,) * len(shapes),
            scratch_shapes=[pltpu.VMEM((2, 2, 2, depth, size), BF) for size in sizes]
            + [
                pltpu.VMEM((4 * depth, max(sizes)), BF),
                pltpu.SemaphoreType.DMA((2, 2 * len(sizes))),
            ],
        ),
        compiler_params=params(),
        cost_estimate=cost(2 * total * width * sum(sizes), *lefts, *rights, *shapes),
        name="grads",
    )(flags, *lefts, *rights)
    each = 2 * highs
    return [
        (list(outs[k * each : (k + 1) * each : 2]), list(outs[k * each + 1 : (k + 1) * each : 2]))
        for k in range(len(lefts))
    ]


def attend_kernel(own, parts, flags, bases, queries, *refs):
    if own:
        pairs, refs = refs[:parts], refs[parts:]
        lows, ends, within, sums, peaks, totals, pair_buf, sems = refs
    else:
        sums, peaks, totals, *refs = refs
        pairs, refs = refs[:parts], refs[parts:]
        lows, ends, within, mixed, log_sums, mixed_low, pair_buf, sems = refs
    count = queries.shape[0]
    half = count // 2
    highs = parts // 2
    loads = []
    for p in range(parts):
        place = pl.ds((p % 2) * count, count)
        loads.append(
            pltpu.make_async_copy(pairs[p], pair_buf.at[p // 2, place], sems.at[p])
        )
    for load in loads:
        load.start()
    for load in loads:
        load.wait()
    for head in range(2):
        columns = slice(head * HD, (head + 1) * HD)
        for side in range(2):
            place = slice(side * half, (side + 1) * half)
            query = queries[place, columns] * jnp.asarray(HD ** (-0.5), BF)
            low, end = lows[place, :], ends[place, :]

            def step(high, base, carry):
                peak, total, accum = carry
                scores = mm_nt(query, pair_buf[high, :, :HD])
                position = within[...] + base
                allowed = (position >= low) & (position <= end)
                scores = jnp.where(allowed, scores, MASKED)
                new_peak = jnp.maximum(peak, jnp.max(scores, axis=1, keepdims=True))
                decay = jnp.exp(peak - new_peak)
                probs = jnp.exp(scores - new_peak)
                total = decay * total + jnp.sum(probs, axis=1, keepdims=True)
                accum = decay * accum + mm(probs.astype(BF), pair_buf[high, :, HD:])
                return new_peak, total, accum

            if own:
                start = (
                    jnp.full((half, 1), MASKED, F32),
                    jnp.zeros((half, 1), F32),
                    jnp.zeros((half, HD), F32),
                )
                peak, total, accum = step(0, bases[0], start)
                peaks[head, place, :] = peak
                totals[head, place, :] = total
                sums[place, columns] = accum
                continue

            def far_step(i, carry):
                high = highs - flags[1] + i
                return step(high, bases[high + 1], carry)

            start = (peaks[head, place, :], totals[head, place, :], sums[place, columns])
            peak, total, accum = lax.fori_loop(0, flags[1], far_step, start)
            out = accum / total
            mixed[place, columns] = out
            mixed_low[place, columns] = out.astype(BF)
            log_sums[head, place, :] = peak + jnp.log(total)


def attend(flags, bases, queries, pairs, lows, ends, within, before=None):
    count = queries.shape[0]
    parts = len(pairs)
    low = jax.ShapeDtypeStruct((count, 2 * HD), BF)
    mixed = jax.ShapeDtypeStruct((count, 2 * HD), F32)
    column = jax.ShapeDtypeStruct((2, count, 1), F32)
    before = before or ()
    return pl.pallas_call(
        functools.partial(attend_kernel, not before, parts),
        out_shape=(mixed, column, low) if before else (mixed, column, column),
        in_specs=[SCALARS, SCALARS]
        + [WHOLE] * (1 + len(before))
        + [ANY] * parts
        + [WHOLE] * 3,
        out_specs=(WHOLE,) * 3,
        scratch_shapes=[
            pltpu.VMEM((parts // 2, 2 * count, 2 * HD), BF),
            pltpu.SemaphoreType.DMA((parts,)),
        ],
        compiler_params=params(),
        cost_estimate=cost(16 * count * count * parts * HD, mixed),
        name="attend",
    )(flags, bases, queries, *before, *pairs, lows, ends, within)


def attend_back_kernel(own, parts, flags, bases, source, back, *refs):
    pairs, refs = refs[:parts], refs[parts:]
    lows, ends, within, stats, deltas, *refs = refs
    if own:
        sum_in, cos_ref, sin_ref, *refs = refs
    outs, out_ref, refs = refs[:parts], refs[parts], refs[parts + 1 :]
    pair_buf, queries, backs, probs_buf, score_buf, query_sum, pair_sum, sems, out_sem = refs
    count = source.shape[0]
    highs = parts // 2
    scale = HD ** (-0.5)
    loads = []
    for p in range(parts):
        loads.append(pltpu.make_async_copy(pairs[p], pair_buf.at[p], sems.at[p]))
    for load in loads:
        load.start()
    for head in range(2):
        place = slice(head * count, (head + 1) * count)
        columns = slice(head * HD, (head + 1) * HD)
        queries[place, :] = source[:, columns] * jnp.asarray(scale, BF)
        backs[place, :] = back[:, columns]
    query_sum[...] = sum_in[...] if own else jnp.zeros_like(query_sum)
    for load in loads:
        load.wait()

    def step(i, carry):
        if own:
            b, base = i, bases[0]
        else:
            b = 2 * (highs - flags[1]) + i
            base = bases[b // 2 + 1]
        keys, values = pair_buf[b, :, :HD], pair_buf[b, :, HD:]
        place = pl.multiple_of(lax.rem(i, 2) * count, count)
        position = within[pl.ds(place, count), :] + base
        allowed = (position >= lows[...]) & (position <= ends[...])
        for head in range(2):
            place = slice(head * count, (head + 1) * count)
            scores = mm_nt(keys, queries[place, :])
            probs = jnp.where(allowed, jnp.exp(scores - stats[head : head + 1, :]), 0.0)
            prob_back = mm_nt(values, backs[place, :])
            probs_buf[:, place] = probs.astype(BF)
            score_buf[:, place] = (probs * (prob_back - deltas[head : head + 1, :])).astype(BF)
        pair_sum[:, :HD] = mm(score_buf[...], queries[...]).astype(BF)
        pair_sum[:, HD:] = mm(probs_buf[...], backs[...]).astype(BF)
        query_sum[...] += mm_tn(score_buf[...], keys)
        for p in range(parts):

            @pl.when(b == p)
            def _(p=p):
                store = pltpu.make_async_copy(pair_sum, outs[p], out_sem)
                store.start()
                store.wait()

        return carry

    lax.fori_loop(0, 2 if own else 2 * flags[1], step, 0)
    if not own:
        out_ref[...] = query_sum[...]
        return
    c, s = cos_ref[...], sin_ref[...]
    for head in range(2):
        grad = query_sum[head * count : (head + 1) * count, :] * scale
        a, b = grad[:, : HD // 2], grad[:, HD // 2 :]
        turned = jnp.concatenate([a * c + b * s, b * c - a * s], axis=1)
        out_ref[:, head * HD : (head + 1) * HD] = turned.astype(BF)


def attend_back(flags, bases, queries, back, pairs, lows, ends, within, stats, deltas, more=()):
    count = queries.shape[0]
    parts = len(pairs)
    low = jax.ShapeDtypeStruct((count, 2 * HD), BF)
    last = low if more else jax.ShapeDtypeStruct((2 * count, HD), F32)
    outs = pl.pallas_call(
        functools.partial(attend_back_kernel, bool(more), parts),
        out_shape=(low,) * parts + (last,),
        in_specs=[SCALARS, SCALARS]
        + [WHOLE] * 2
        + [ANY] * parts
        + [WHOLE] * (5 + len(more)),
        out_specs=(ANY,) * parts + (WHOLE,),
        scratch_shapes=[
            pltpu.VMEM((parts, count, 2 * HD), BF),
            pltpu.VMEM((2 * count, HD), BF),
            pltpu.VMEM((2 * count, HD), BF),
            pltpu.VMEM((count, 2 * count), BF),
            pltpu.VMEM((count, 2 * count), BF),
            pltpu.VMEM((2 * count, HD), F32),
            pltpu.VMEM((count, 2 * HD), BF),
            pltpu.SemaphoreType.DMA((parts,)),
            pltpu.SemaphoreType.DMA,
        ],
        compiler_params=params(),
        cost_estimate=cost(20 * count * count * parts * HD, low, low),
        name="attend_back",
    )(flags, bases, queries, back, *pairs, lows, ends, within, stats, deltas, *more)
    return list(outs[0:parts:2]), list(outs[1:parts:2]), outs[parts]


def tie(values):
    return lax.optimization_barrier(values)


class Bag:
    pass


class Weight:
    def __init__(self, keep):
        self.keep = keep


class Sum:
    pass


class Grad:
    pass


def flatten(bag):
    names = sorted(vars(bag))
    return [getattr(bag, name) for name in names], tuple(names)


def unflatten(kind, names, values):
    bag = kind.__new__(kind)
    for name, value in zip(names, values):
        setattr(bag, name, value)
    return bag


for kind in (Bag, Weight, Sum, Grad):
    jax.tree_util.register_pytree_node(kind, flatten, functools.partial(unflatten, kind))


def halves(zl, array):
    c = array.shape[1] // 2
    left, right = array[:, :c], array[:, c:]
    first = zl == 0
    return jnp.where(first, left, right), jnp.where(first, right, left)


def join(zl, own, received):
    first = zl == 0
    return jnp.concatenate([jnp.where(first, own, received), jnp.where(first, received, own)], axis=1)


def turn_back(vectors, cosines, sines):
    half = vectors.shape[-1] // 2
    a, b = vectors[..., :half], vectors[..., half:]
    return jnp.concatenate([a * cosines + b * sines, b * cosines - a * sines], axis=-1)


def body(
    hidden_in,
    segments,
    attn_gain,
    query_weight,
    key_weight,
    value_weight,
    output_weight,
    mlp_gain,
    gate_weight,
    up_weight,
    down_weight,
    cotangent,
):
    wide_count = lax.axis_size("wide")
    devices = wide_count * 4
    mover = Mover(devices)
    highs = mover.highs
    wide = lax.axis_index("wide")
    tp = lax.axis_index("tp")
    y, zl, zh = wide & 1, (wide >> 1) & 1, wide >> 2
    first = zl == 0
    flags = jnp.stack([zl, zh, y]).astype(jnp.int32)
    micro, local, width = hidden_in.shape
    rows = micro * local
    wide_tokens = segments.shape[1]
    head_rows = 8 * local
    scale = HD ** (-0.5)
    swap = mover.swap
    shifts = range(1, highs)
    places = jnp.stack(
        [
            (((zh + shift) % highs) * 2 + (zl ^ low)) * 2 + (y ^ dy)
            for shift in range(highs)
            for dy in range(2)
            for low in range(2)
        ]
    ).astype(jnp.int32)

    def highs_of(value, causal=False):
        return [mover.from_high(value, shift, causal) for shift in shifts]

    def over_y(values):
        return [swap(value, YDIR) for value in values]

    inputs = hidden_in.reshape(rows, width).astype(F32)
    scale_one = lax.rsqrt(jnp.mean(inputs * inputs, axis=-1, keepdims=True) + EPSILON)
    plain_one = inputs * scale_one

    gain_one = attn_gain.astype(F32)[:, None]
    gain_two = mlp_gain.astype(F32)[:, None]

    def gained(weight, gain):
        return (weight.astype(F32) * gain).astype(BF)

    pair_weight = jnp.concatenate([key_weight, value_weight], axis=1)
    gate_keep, gate_send = halves(zl, gained(gate_weight, gain_two))
    up_keep, up_send = halves(zl, gained(up_weight, gain_two))
    down_keep, down_send = halves(zl, down_weight.T)
    units = 512
    groups = gate_keep.shape[1] // units

    def cut_units(c, gate, up, down):
        cut = slice(c * units, (c + 1) * units)
        return jnp.concatenate([gate[:, cut], up[:, cut], down[:, cut]], axis=1)

    live = Bag()

    def cut():
        vars(live).update(vars(tie(live)))

    def pair_of_segments():
        own, got = live.segments, live.seg_got
        return [jnp.stack([jnp.where(first, own, got), jnp.where(first, got, own)])]

    def blocks_of(weight):
        blocks = [weight.keep, weight.got, weight.yk, weight.yg]
        for group in zip(weight.hk, weight.hg, weight.hyk, weight.hyg):
            blocks += group
        return blocks

    def own_first(row):
        low, high = row[:local], row[local:]
        live.row = jnp.where(first, low, high)
        live.rz = swap(jnp.where(first, high, low), ZLOW)
        live.rx = swap(live.row, XDIR)
        live.rc = [swap(live.row, CORE)]

    def rows_first(row):
        live.row, live.rx, live.rz = row, swap(row, XDIR), swap(row, ZLOW)
        live.rc = [swap(row, CORE)]

    def rows_second():
        live.rd = swap(live.rz, XDIR)
        live.rc += [swap(value, CORE) for value in (live.rx, live.rz)]

    def rows_last():
        row, x, z, d, c = live.row, live.rx, live.rz, live.rd, live.rc
        del live.row, live.rx, live.rz, live.rd, live.rc
        return [row, c[0], x, c[1], z, c[2], d, swap(d, CORE)]

    def stack_first(row):
        low, high = row[:local], row[local:]
        live.row = jnp.where(first, low, high)
        live.rz = swap(jnp.where(first, high, low), ZLOW)

    def stack_second():
        live.stack = jnp.concatenate([live.row, live.rz])
        live.stack_x = swap(live.stack, XDIR)
        live.stack_c = swap(live.stack, CORE)
        del live.row, live.rz

    def stack_last():
        stacks = [live.stack, live.stack_c, live.stack_x, swap(live.stack_x, CORE)]
        del live.stack, live.stack_c, live.stack_x
        return stacks

    def sums_start(pair):
        part = Sum()
        part.keep, part.send = pair
        return part

    def sums_core(part):
        part.send = swap(part.send, CORE)

    def sums_combine(part):
        part.own, part.near, part.low, part.far = combine(part.keep, part.send)
        del part.keep, part.send

    def sums_far(part):
        part.far = swap(part.far, XDIR)

    def sums_near(part):
        low = (part.low.astype(F32) + part.far.astype(F32)).astype(BF)
        part.low, part.near = swap(low, ZLOW), swap(part.near, XDIR)
        del part.far

    def sums_total(part):
        return part.own + part.near.astype(F32) + part.low.astype(F32)

    def own_x(part):
        part.far, part.near = swap(part.far, XDIR), swap(part.near, XDIR)

    def own_zl(part):
        low = (part.low.astype(F32) + part.far.astype(F32)).astype(BF)
        part.low = swap(low, ZLOW)
        del part.far

    def own_total(part):
        mine, other = part.own + part.near.astype(F32), part.low.astype(F32)
        return jnp.concatenate([jnp.where(first, mine, other), jnp.where(first, other, mine)])

    def grad_start(pair):
        part = Grad()
        part.keep, part.send = pair
        return part

    def grad_y_far(part):
        part.send[1:] = [swap(part.send[shift], YDIR) for shift in shifts]

    def grad_y_near(part):
        part.send[0] = swap(part.send[0], YDIR)

    def grad_h(part, low):
        moved = []
        for shift in shifts:
            half = part.keep[shift][low].astype(F32) + part.send[shift][low].astype(F32)
            moved.append(mover.to_high(half.astype(BF), shift))
        if low:
            part.moved_got = moved
        else:
            part.moved_own = moved

    def grad_zl(part):
        totals = []
        for low in range(2):
            total = part.keep[0][low].astype(F32) + part.send[0][low].astype(F32)
            for moved in (part.moved_own, part.moved_got)[low]:
                total = total + moved.astype(F32)
            totals.append(total)
        part.own, part.got = totals[0], swap(totals[1].astype(BF), ZLOW)
        del part.keep, part.send, part.moved_own, part.moved_got

    span = jnp.arange(local, dtype=jnp.int32)
    steps = jnp.arange(4, dtype=jnp.int32)
    within = (
        ((zl ^ jnp.arange(2, dtype=jnp.int32))[:, None, None] * 2 * wide_tokens)
        + ((tp ^ steps) * local)[None, :, None]
        + span[None, None, :]
    ).reshape(head_rows)
    row_positions = (zh * 4 + y) * wide_tokens + within
    bases = jnp.stack([((zh + shift) % highs) * 4 * wide_tokens for shift in range(highs)])
    bases = bases.astype(jnp.int32)
    key_within = jnp.concatenate([within + (y ^ dy) * wide_tokens for dy in range(2)])
    freqs = jnp.exp(-math.log(ROPE_BASE) * (2.0 * jnp.arange(HD // 2, dtype=F32) / HD))
    angles = row_positions.astype(F32)[:, None] * freqs[None, :]
    tables = (jnp.cos(angles), jnp.sin(angles))

    live.upstream = cotangent.reshape(rows, width)
    qkv_own, row_one = tie(
        [
            jnp.concatenate([gained(w, gain_one) for w in (query_weight, pair_weight)], axis=1),
            plain_one.astype(BF),
        ]
    )
    live.q = q = Weight(qkv_own)
    q.hk = highs_of(q.keep)
    q.got = swap(q.keep, ZLOW)
    q.yk = swap(q.keep, YDIR)
    stack_first(row_one)
    live.u_send = [cut_units(c, gate_send, up_send, down_send) for c in range(groups)]
    live.u = u = [Weight(cut_units(c, gate_keep, up_keep, down_keep)) for c in range(groups)]
    live.o_own = output_weight.T
    live.segments = segments
    u[0].yk = swap(u[0].keep, YDIR)
    live.seg_got = swap(segments, ZLOW)
    cut()
    q, u = live.q, live.u
    q.hg = highs_of(q.got)
    q.hyk = over_y(q.hk)
    q.yg = swap(q.got, YDIR)
    stack_second()
    live.o_got = swap(live.o_own, ZLOW)
    live.seg = pair_of_segments()
    live.seg.append(swap(live.seg[0], YDIR))
    cut()
    q, u = live.q, live.u
    q.hyg = over_y(q.hg)
    live.out_pair = jnp.concatenate([live.o_own, live.o_got])
    live.out_h = highs_of(live.out_pair)
    live.seg = [jnp.concatenate(live.seg)]
    live.seg += highs_of(live.seg[0])
    live.dx = swap(live.upstream, XDIR)
    live.normed, live.queries, live.pair = gathered_matmul(
        places, stack_last(), blocks_of(q), tables
    )
    cut()
    u = live.u
    live.pair_h, live.pair_y = highs_of(live.pair, causal=True), swap(live.pair, YDIR)
    live.out_hy = over_y(live.out_h)
    live.dz = swap(live.upstream, ZLOW)
    seg_all = lax.dynamic_index_in_dim(jnp.concatenate(live.seg), zl, 1, keepdims=False)
    own_pair = lax.dynamic_index_in_dim(live.seg[0][:2], zl, 1, keepdims=False)
    del live.seg
    own_rows = jnp.stack(
        [
            lax.dynamic_slice_in_dim(
                lax.dynamic_index_in_dim(own_pair, zl ^ dzl, 0, keepdims=False),
                (tp ^ dtp) * local,
                local,
                0,
            )
            for dzl in range(2)
            for dtp in range(4)
        ]
    ).reshape(head_rows)
    live.starts = jnp.sum(
        (seg_all.reshape(1, -1) < own_rows[:, None]).astype(jnp.int32), axis=1
    )
    spots = (
        live.starts.reshape(head_rows, 1),
        row_positions.reshape(head_rows, 1),
        key_within.reshape(1, 2 * head_rows),
    )
    live.before = attend(flags, bases, live.queries, [live.pair, live.pair_y], *spots)
    cut()
    u = live.u
    pair_hy = over_y(live.pair_h)
    u[0].got = swap(live.u_send[0], ZLOW)
    u[0].hk = highs_of(u[0].keep)
    live.out_y = swap(live.out_pair, YDIR)
    live.dd = swap(live.dz, XDIR)
    live.own_pairs, live.far_pairs = [live.pair, live.pair_y], []
    for values in zip(live.pair_h, pair_hy):
        live.far_pairs += values
    del live.pair, live.pair_y, live.pair_h
    live.mixed, live.log_sums, live.mixed_all = attend(
        flags, bases, live.queries, live.far_pairs, *spots, live.before
    )
    del live.before
    cut()
    u = live.u
    live.o = [live.out_pair, live.out_y]
    for values in zip(live.out_h, live.out_hy):
        live.o += values
    del live.out_pair, live.out_y, live.out_h, live.out_hy
    live.a = sums_start(partial_matmul(places, [(live.mixed_all, 0, 2 * HD)], [live.o], [0]))
    cut()
    u = live.u
    sums_core(live.a)
    u[0].yg = swap(u[0].got, YDIR)
    u[1].got = swap(live.u_send[1], ZLOW)
    sums_combine(live.a)
    own_x(live.a)
    cut()
    u = live.u
    own_zl(live.a)
    live.log_sums = live.log_sums.reshape(2, head_rows)
    live.dc = [swap(d, CORE) for d in (live.upstream, live.dx, live.dz, live.dd)]
    cut()
    u = live.u
    live.hidden = hidden = inputs + own_total(live.a)
    del live.a
    scale_two = lax.rsqrt(jnp.mean(hidden * hidden, axis=-1, keepdims=True) + EPSILON)
    plain_two = hidden * scale_two
    rows_first(plain_two.astype(BF))
    u[0].hg = highs_of(u[0].got)
    u[1].yg = swap(u[1].got, YDIR)
    cut()
    u = live.u
    rows_second()
    u[0].hyk = over_y(u[0].hk)
    u[0].hyg = over_y(u[0].hg)
    u[1].hg = highs_of(u[1].got)
    d_x, d_z, d_d, d_cores = live.dx, live.dz, live.dd, live.dc
    live.dy_all = assemble(
        [live.upstream, d_cores[0], d_x, d_cores[1], d_z, d_cores[2], d_d, d_cores[3]]
    )
    del live.dx, live.dz, live.dd, live.dc
    cut()
    u = live.u
    chunks = rows_last()
    u[1].yk = swap(u[1].keep, YDIR)
    u[1].hk = highs_of(u[1].keep)
    u[1].hyg = over_y(u[1].hg)
    live.backs, live.acts = [None] * 2, [None] * 2

    def unit_work(c, source):
        live.x_all, live.backs[c], live.acts[c] = hidden_units(
            places, source, live.dy_all, blocks_of(live.u[c])
        )

    def unit_grads(c):
        pairs = weight_grads(
            flags, highs, [live.x_all, live.dy_all], [live.backs[c], live.acts[c]]
        )
        return [grad_start(pair) for pair in pairs]

    unit_work(0, chunks)
    live.g = unit_grads(0)
    cut()
    u, g = live.u, live.g
    u[1].hyk = over_y(u[1].hk)
    cut()
    u, g = live.u, live.g
    grad_y_far(g[1])
    unit_work(1, [live.x_all])
    cut()
    g = live.g
    grad_y_far(g[0])
    grad_h(g[1], 0)
    grad_h(g[1], 1)
    live.unit_blocks = [blocks_of(weight) for weight in live.u]
    del live.u
    live.e = sums_start(
        partial_matmul(
            places,
            [(back, 0, 2 * units) for back in live.backs],
            live.unit_blocks,
            [0] * groups,
        )
    )
    cut()
    g = live.g
    sums_core(live.e)
    grad_y_near(g[0])
    grad_h(g[0], 1)
    sums_combine(live.e)
    sums_far(live.e)
    live.g += unit_grads(1)
    cut()
    g = live.g
    sums_near(live.e)
    grad_h(g[0], 0)
    grad_y_far(g[2])
    cut()
    weighted_two = sums_total(live.e)
    del live.e
    hidden_back = live.upstream.astype(F32) + scale_two * (
        weighted_two - plain_two * jnp.mean(weighted_two * plain_two, axis=-1, keepdims=True)
    )
    g = live.g
    own_first(hidden_back.astype(BF))
    grad_y_near(g[2])
    grad_h(g[2], 0)
    live.d = sums_start(
        partial_matmul(
            places,
            [(act, 0, units) for act in live.acts],
            live.unit_blocks,
            [2 * units] * groups,
        )
    )
    del live.acts, live.backs, live.unit_blocks
    cut()
    g = live.g
    rows_second()
    grad_zl(g[0])
    grad_y_far(g[3])
    cut()
    g = live.g
    grad_y_near(g[3])
    grad_h(g[3], 0)
    sums_core(live.d)
    live.attn_back, live.back, live.deltas = gathered_matmul(
        places, rows_last(), live.o, mixed=live.mixed
    )
    cut()
    g = live.g
    grad_y_near(g[1])
    grad_h(g[3], 1)
    live.turned = (
        live.starts.reshape(1, head_rows),
        row_positions.reshape(1, head_rows),
        key_within.reshape(2 * head_rows, 1),
        live.log_sums,
        live.deltas.T,
    )
    live.k_keep, live.k_send, live.query_sum = attend_back(
        flags, bases, live.queries, live.back, live.far_pairs, *live.turned
    )
    cut()
    g = live.g
    live.k_send = [swap(value, YDIR) for value in live.k_send]
    grad_zl(g[1])
    grad_h(g[2], 1)
    grad_zl(g[3])
    keep, send, live.query_back = attend_back(
        flags,
        bases,
        live.queries,
        live.back,
        live.own_pairs,
        *live.turned,
        (live.query_sum, *tables),
    )
    live.k_keep, live.k_send = keep + live.k_keep, send + live.k_send
    del live.turned, live.query_sum
    sums_combine(live.d)
    (grads_out,) = weight_grads(flags, highs, [live.attn_back], [live.mixed_all])
    live.g_out = grad_start(grads_out)
    cut()
    g = live.g
    live.k_moved = []
    for shift in shifts:
        half = live.k_keep[shift].astype(F32) + live.k_send[shift].astype(F32)
        live.k_moved.append(mover.to_high(half.astype(BF), shift, causal=True))
    live.k_near = swap(live.k_send[0], YDIR)
    grad_zl(g[2])
    grad_y_far(live.g_out)
    sums_far(live.d)
    (grads_q,) = weight_grads(flags, highs, [live.normed], [live.query_back])
    live.g_q = grad_start(grads_q)
    cut()
    g = live.g
    total = live.k_keep[0].astype(F32) + live.k_near.astype(F32)
    for moved in live.k_moved:
        total = total + moved.astype(F32)
    del live.k_keep, live.k_send, live.k_moved, live.k_near
    key_back = turn_back(total[:, :HD], *tables).astype(BF)
    live.pair_back = jnp.concatenate([key_back, total[:, HD:].astype(BF)], axis=1)
    grad_y_near(live.g_out)
    grad_h(live.g_out, 0)
    grad_h(live.g_out, 1)
    grad_y_far(live.g_q)
    sums_near(live.d)
    (grads_p,) = weight_grads(flags, highs, [live.normed], [live.pair_back])
    live.g_p = grad_start(grads_p)
    cut()
    g = live.g
    grad_zl(live.g_out)
    grad_y_near(live.g_q)
    grad_h(live.g_q, 0)
    grad_h(live.g_q, 1)
    grad_y_far(live.g_p)
    live.n = sums_start(
        partial_matmul(
            places,
            [(live.query_back, 0, 2 * HD), (live.pair_back, 0, 2 * HD)],
            [blocks_of(live.q)] * 2,
            [0, 2 * HD],
        )
    )
    cut()
    g = live.g
    sums_core(live.n)
    grad_zl(live.g_q)
    grad_y_near(live.g_p)
    grad_h(live.g_p, 0)
    grad_h(live.g_p, 1)
    sums_combine(live.n)
    own_x(live.n)
    cut()
    g = live.g
    own_zl(live.n)
    grad_zl(live.g_p)

    def unit_columns(part, at):
        cut = slice(at * units, (at + 1) * units)
        own = jnp.concatenate([piece.own[:, cut] for piece in part], axis=1)
        return join(
            zl, own, jnp.concatenate([piece.got[:, cut] for piece in part], axis=1).astype(F32)
        )

    gate_plain, up_plain = unit_columns(g[0::2], 0), unit_columns(g[0::2], 1)
    live.shards = (gate_plain * gain_two, up_plain * gain_two, unit_columns(g[1::2], 0).T)
    live.gain_two = jnp.sum(gate_plain * gate_weight.astype(F32), axis=1) + jnp.sum(
        up_plain * up_weight.astype(F32), axis=1
    )
    live.layer_out = (live.hidden + sums_total(live.d)).astype(BF)
    cut()
    weighted_one = own_total(live.n)
    input_grad = hidden_back + scale_one * (
        weighted_one - plain_one * jnp.mean(weighted_one * plain_one, axis=-1, keepdims=True)
    )
    g = live.g
    def columns_of(part):
        return part.own + part.got.astype(F32)

    query_plain, pair_plain = columns_of(live.g_q), columns_of(live.g_p)
    gain_sums = jnp.stack(
        [
            jnp.sum(query_plain * query_weight.astype(F32), axis=1)
            + jnp.sum(pair_plain * pair_weight.astype(F32), axis=1),
            live.gain_two,
        ]
    )
    gain_sums = gain_sums + sum(swap(gain_sums, m) for m in (CORE, XDIR, CORE | XDIR))
    pair_shard = pair_plain * gain_one
    shape = hidden_in.shape
    return (
        live.layer_out.reshape(shape),
        input_grad.reshape(shape),
        gain_sums[0],
        query_plain * gain_one,
        pair_shard[:, :HD],
        pair_shard[:, HD:],
        columns_of(live.g_out).T,
        gain_sums[1],
        *live.shards,
    )


def solution(mesh):
    rows = P(None, ("wide", "tp"), None)
    columns = P("wide", "tp")
    flipped = P("tp", "wide")
    gain = P("wide")
    weights = (columns, columns, columns, flipped, gain, columns, columns, flipped)
    return jax.shard_map(
        body,
        mesh=mesh,
        in_specs=(rows, P(None, "wide"), gain) + weights + (rows,),
        out_specs=(rows, rows, gain) + weights,
        check_vma=False,
    )
```

```python
import functools
import math

import jax
import jax.numpy as jnp
from jax import lax
from jax.experimental import pallas as pl
from jax.experimental.pallas import tpu as pltpu
from jax.sharding import PartitionSpec as P

HD = 256
EPSILON = 1e-06
ROPE_BASE = 1000042.0
MASKED = -1e30
BF = jnp.bfloat16
F32 = jnp.float32
AXES = ("wide", "tp")
VMEM_LIMIT = 56 << 20

CORE, XDIR, YDIR, ZLOW = 1, 2, 4, 8
CONTRACT_ROWS = (((0,), (0,)), ((), ()))
CONTRACT_COLUMNS = (((1,), (1,)), ((), ()))


def mm(left, right):
    return jnp.dot(left, right, preferred_element_type=F32)


def mm_nt(left, right):
    return lax.dot_general(left, right, CONTRACT_COLUMNS, preferred_element_type=F32)


def mm_tn(left, right):
    return lax.dot_general(left, right, CONTRACT_ROWS, preferred_element_type=F32)


ANY = pl.BlockSpec(memory_space=pl.ANY)
WHOLE = pl.BlockSpec(memory_space=pltpu.VMEM)
SCALARS = pl.BlockSpec(memory_space=pltpu.SMEM)


def params():
    return pltpu.CompilerParams(vmem_limit_bytes=VMEM_LIMIT)


def cost(flops, *arrays):
    moved = sum(math.prod(a.shape) * jnp.dtype(a.dtype).itemsize for a in arrays)
    return pl.CostEstimate(flops=20 * int(flops), transcendentals=0, bytes_accessed=int(moved))


class Mover:
    def __init__(self, devices):
        self.devices = devices
        self.highs = devices // 16

    def swap(self, value, mask):
        return lax.ppermute(value, AXES, [(i, i ^ mask) for i in range(self.devices)])

    def from_high(self, value, shift, causal=False):
        pairs = []
        for dst in range(self.devices):
            zh = dst // 16
            src_zh = (zh + shift) % self.highs
            if causal and src_zh > zh:
                continue
            pairs.append((src_zh * 16 + dst % 16, dst))
        return lax.ppermute(value, AXES, pairs)

    def to_high(self, value, shift, causal=False):
        pairs = []
        for src in range(self.devices):
            zh = src // 16
            dst_zh = (zh + shift) % self.highs
            if causal and dst_zh > zh:
                continue
            pairs.append((src, dst_zh * 16 + src % 16))
        return lax.ppermute(value, AXES, pairs)


def weight_loads(parts, places, depth, buffer, sems, start):
    loads = []
    for part in parts:
        for low in range(part.shape[0] // depth):
            at = len(loads)
            row = pl.multiple_of(places[at] * depth, depth)
            loads.append(
                pltpu.make_async_copy(
                    part.at[pl.ds(low * depth, depth)],
                    buffer.at[pl.ds(row, depth)],
                    sems.at[start + at],
                )
            )
    return loads


def gathered_kernel(rotary, stacked, parts, blocks, places, *refs):
    stacks, refs = refs[:stacked], refs[stacked:]
    weights, refs = refs[:parts], refs[parts:]
    if rotary:
        cos_ref, sin_ref, all_ref, out_ref, pair_ref = refs[:5]
    else:
        mixed_ref, all_ref, out_ref, delta_ref = refs[:4]
    rows_buf, weight_buf, sems = refs[-3:]
    rows = rows_buf.shape[0] // 8
    if stacked == 4:
        chunks = [stacks[k % 4].at[pl.ds(k // 4 * rows, rows)] for k in range(8)]
    else:
        chunks = stacks
    depth = weight_buf.shape[0] // blocks
    fills = weight_loads(weights, places, depth, weight_buf, sems, 9)
    loads = [
        pltpu.make_async_copy(chunks[k], rows_buf.at[pl.ds(k * rows, rows)], sems.at[k])
        for k in range(8)
    ]
    for load in fills + loads:
        load.start()
    for fill in fills:
        fill.wait()
    tile = 4 * rows
    for half in range(2):
        for k in range(4):
            loads[4 * half + k].wait()
        place = slice(half * tile, (half + 1) * tile)
        left = rows_buf[place, :]
        if rotary:
            c, s = cos_ref[place, :], sin_ref[place, :]
            for head in range(3):
                product = mm(left, weight_buf[:, head * HD : (head + 1) * HD])
                a, b = product[:, : HD // 2], product[:, HD // 2 :]
                turned = jnp.concatenate([a * c - b * s, b * c + a * s], axis=1).astype(BF)
                if head < 2:
                    out_ref[place, head * HD : (head + 1) * HD] = turned
                else:
                    pair_ref[place, :HD] = turned
            pair_ref[place, HD:] = mm(left, weight_buf[:, 3 * HD :]).astype(BF)
        else:
            low = mm(left, weight_buf[...]).astype(BF)
            out_ref[place, :] = low
            product = low.astype(F32) * mixed_ref[place, :]
            for head in range(2):
                delta_ref[place, head : head + 1] = jnp.sum(
                    product[:, head * HD : (head + 1) * HD], axis=1, keepdims=True
                )
    store = pltpu.make_async_copy(rows_buf, all_ref, sems.at[8])
    store.start()
    store.wait()


def gathered_matmul(places, chunks, parts, tables=None, mixed=None):
    rows, width = chunks[0].shape
    rows = rows * len(chunks) // 8
    columns = parts[0].shape[1]
    blocks = places.shape[0]
    more = tables or (mixed,)
    out = jax.ShapeDtypeStruct((8 * rows, 2 * HD), BF)
    outs = (out, out) if tables else (out, jax.ShapeDtypeStruct((8 * rows, 2), F32))
    return pl.pallas_call(
        functools.partial(gathered_kernel, bool(tables), len(chunks), len(parts), blocks),
        out_shape=(jax.ShapeDtypeStruct((8 * rows, width), BF),) + outs,
        in_specs=[SCALARS] + [ANY] * (len(chunks) + len(parts)) + [WHOLE] * len(more),
        out_specs=(ANY,) + (WHOLE,) * len(outs),
        scratch_shapes=[
            pltpu.VMEM((8 * rows, width), BF),
            pltpu.VMEM((width, columns), BF),
            pltpu.SemaphoreType.DMA((9 + blocks,)),
        ],
        compiler_params=params(),
        cost_estimate=cost(2 * 8 * rows * width * columns, *chunks, *chunks, *parts),
        name="gathered",
    )(places, *chunks, *parts, *more)


def partial_kernel(counts, starts, groups, blocks, places, *refs):
    lefts, refs = refs[:counts], refs[counts:]
    sets = []
    for size in groups:
        sets.append(refs[:size])
        refs = refs[size:]
    keep_ref, send_ref, weight_buf, sems = refs
    rows = keep_ref.shape[1]
    width = weight_buf.shape[0]
    depth = width // blocks

    @pl.when(pl.program_id(0) == 0)
    def _():
        fills = []
        column = 0
        for parts, start, left in zip(sets, starts, lefts):
            size = left.shape[1]
            place = pl.ds(column, size)
            cut = [part.at[:, pl.ds(start, size)] for part in parts]
            fills += weight_loads(
                cut, places, depth, weight_buf.at[:, place], sems, len(fills)
            )
            column += size
        for fill in fills:
            fill.start()
        for fill in fills:
            fill.wait()

    tile = 512 if width % 512 == 0 else width
    for at in range(0, width, tile):
        total = None
        column = 0
        for left in lefts:
            size = left.shape[1]
            term = mm_nt(left[...], weight_buf[at : at + tile, column : column + size])
            total = term if total is None else total + term
            column += size
        low = total.astype(BF)
        keep_ref[0, :, at : at + tile] = low[:rows]
        send_ref[0, :, at : at + tile] = low[rows:]


def partial_matmul(places, lefts, sets, starts):
    rows = lefts[0][0].shape[0] // 8
    blocks = places.shape[0]
    width = sum(part.shape[0] for part in sets[0])
    used = sum(size for _, _, size in lefts)
    out = jax.ShapeDtypeStruct((4, rows, width), BF)
    block = pl.BlockSpec((1, rows, width), lambda j: (j, 0, 0))
    flat = [part for parts in sets for part in parts]

    def rows_of(place, size):
        return pl.BlockSpec((2 * rows, size), lambda j: (j, place))

    return pl.pallas_call(
        functools.partial(
            partial_kernel, len(lefts), tuple(starts), tuple(len(p) for p in sets), blocks
        ),
        out_shape=(out, out),
        grid=(4,),
        in_specs=[SCALARS]
        + [rows_of(place, size) for _, place, size in lefts]
        + [ANY] * len(flat),
        out_specs=(block, block),
        scratch_shapes=[
            pltpu.VMEM((width, used), BF),
            pltpu.SemaphoreType.DMA((blocks * len(lefts),)),
        ],
        compiler_params=params(),
        cost_estimate=cost(2 * 8 * rows * width * used, out, out, out, out),
        name="partial",
    )(places, *[left for left, _, _ in lefts], *flat)


def combine_kernel(keep, got, own, across, low, diagonal):
    own[...] = keep[0].astype(F32) + got[0].astype(F32)
    for j, out in ((1, across), (2, low), (3, diagonal)):
        out[...] = (keep[j].astype(F32) + got[j].astype(F32)).astype(BF)


def combine(keep, got):
    _, rows, width = keep.shape
    tile = rows // 2
    wide = pl.BlockSpec((4, tile, width), lambda i: (0, i, 0))
    thin = pl.BlockSpec((tile, width), lambda i: (i, 0))
    return pl.pallas_call(
        combine_kernel,
        out_shape=(jax.ShapeDtypeStruct((rows, width), F32),)
        + (jax.ShapeDtypeStruct((rows, width), BF),) * 3,
        grid=(rows // tile,),
        in_specs=[wide, wide],
        out_specs=(thin,) * 4,
        compiler_params=params(),
        cost_estimate=cost(0, keep, keep, got, got),
        name="combine",
    )(keep, got)


def assemble_kernel(*refs):
    chunks, out, sems = refs[:8], refs[8], refs[9]
    rows = chunks[0].shape[0]
    copies = [
        pltpu.make_async_copy(chunks[k], out.at[pl.ds(k * rows, rows)], sems.at[k])
        for k in range(8)
    ]
    for copy in copies:
        copy.start()
    for copy in copies:
        copy.wait()


def assemble(chunks):
    rows, width = chunks[0].shape
    return pl.pallas_call(
        assemble_kernel,
        out_shape=jax.ShapeDtypeStruct((8 * rows, width), BF),
        in_specs=[ANY] * 8,
        out_specs=WHOLE,
        scratch_shapes=[pltpu.SemaphoreType.DMA((8,))],
        compiler_params=params(),
        cost_estimate=cost(0, *chunks, *chunks),
        name="assemble",
    )(*chunks)


def hidden_kernel(counts, blocks, places, dy_ref, *refs):
    chunks, refs = refs[: counts[0]], refs[counts[0] :]
    weights, refs = refs[: counts[1]], refs[counts[1] :]
    x_all, back_ref, activated, x_buf, weight_buf, sems = refs
    step = pl.program_id(0)
    units = activated.shape[1]
    depth = weight_buf.shape[0] // blocks
    rows = chunks[0].shape[0]
    tile = dy_ref.shape[0]
    fills = weight_loads(weights, places, depth, weight_buf, sems, 0)
    pieces = counts[0] if counts[0] > 1 else 2
    size = x_buf.shape[0] // pieces
    loads = []
    for k in range(pieces):
        source = chunks[k] if counts[0] > 1 else chunks[0].at[pl.ds(k * size, size)]
        loads.append(
            pltpu.make_async_copy(source, x_buf.at[pl.ds(k * size, size)], sems.at[blocks + k])
        )
    store = pltpu.make_async_copy(x_buf, x_all, sems.at[blocks + pieces])

    @pl.when(step == 0)
    def _():
        for load in loads + fills:
            load.start()
        for load in loads[: pieces // 2] + fills:
            load.wait()

    @pl.when(step == 1)
    def _():
        for load in loads[pieces // 2 :]:
            load.wait()
        store.start()

    x = x_buf[pl.ds(pl.multiple_of(step * tile, tile), tile), :]
    gate = mm(x, weight_buf[:, :units])
    lift = mm(x, weight_buf[:, units : 2 * units])
    back = mm(dy_ref[...], weight_buf[:, 2 * units :])
    sigmoid = 1.0 / (1.0 + jnp.exp(-gate))
    silu = gate * sigmoid
    activated[...] = (silu * lift).astype(BF)
    back_ref[:, units:] = (back * silu).astype(BF)
    back_ref[:, :units] = (back * lift * (sigmoid * (1.0 + gate * (1.0 - sigmoid)))).astype(BF)

    @pl.when(step == 1)
    def _():
        store.wait()


def hidden_units(places, chunks, dy_all, parts):
    total, width = dy_all.shape
    columns = parts[0].shape[1]
    units = columns // 3
    blocks = places.shape[0]
    tile = total // 2
    return pl.pallas_call(
        functools.partial(hidden_kernel, (len(chunks), len(parts)), blocks),
        out_shape=(
            jax.ShapeDtypeStruct((total, width), BF),
            jax.ShapeDtypeStruct((total, 2 * units), BF),
            jax.ShapeDtypeStruct((total, units), BF),
        ),
        grid=(2,),
        in_specs=[SCALARS, pl.BlockSpec((tile, width), lambda i: (i, 0))]
        + [ANY] * (len(chunks) + len(parts)),
        out_specs=(
            ANY,
            pl.BlockSpec((tile, 2 * units), lambda i: (i, 0)),
            pl.BlockSpec((tile, units), lambda i: (i, 0)),
        ),
        scratch_shapes=[
            pltpu.VMEM((total, width), BF),
            pltpu.VMEM((width, columns), BF),
            pltpu.SemaphoreType.DMA((blocks + max(len(chunks), 2) + 1,)),
        ],
        compiler_params=params(),
        cost_estimate=cost(2 * total * width * columns, dy_all, dy_all, *parts),
        name="hidden",
    )(places, dy_all, *chunks, *parts)


def grads_kernel(counts, highs, flags, *refs):
    lefts, refs = refs[:counts], refs[counts:]
    rights, refs = refs[:counts], refs[counts:]
    outs, refs = refs[: 2 * highs * counts], refs[2 * highs * counts :]
    buffer, sems = refs[-2:]
    sorts = refs[:-2]
    step = pl.program_id(0)
    slot = lax.rem(step, 2)
    depth = buffer.shape[0] // 4

    def stores(high):
        return [
            pltpu.make_async_copy(
                sorts[k].at[high % 2, dy],
                outs[(k * highs + high) * 2 + dy],
                sems.at[high % 2, 2 * k + dy],
            )
            for k in range(counts)
            for dy in range(2)
        ]

    for high in range(2, highs):

        @pl.when(step == high)
        def _(high=high):
            for store in stores(high - 2):
                store.wait()

    for k, (left, right) in enumerate(zip(lefts, rights)):
        size = right.shape[1]
        buffer[:, :size] = mm_tn(left[...], right[...]).astype(BF)
        for low in range(2):
            for dy in range(2):
                place = ((flags[0] ^ low) * 2 + (flags[2] ^ dy)) * depth
                sorts[k][slot, dy, low] = buffer[
                    pl.ds(pl.multiple_of(place, depth), depth), :size
                ]
    for high in range(highs):

        @pl.when(step == high)
        def _(high=high):
            for store in stores(high):
                store.start()
            if high == highs - 1:
                for store in stores(high - 1) + stores(high):
                    store.wait()


def weight_grads(flags, highs, lefts, rights):
    total, width = lefts[0].shape
    depth = width // (4 * highs)
    sizes = [right.shape[1] for right in rights]
    shapes = []
    for size in sizes:
        shapes += [jax.ShapeDtypeStruct((2, depth, size), BF)] * (2 * highs)

    def rows_of(h, flags):
        return (0, lax.rem(flags[1] + h, highs))

    outs = pl.pallas_call(
        functools.partial(grads_kernel, len(lefts), highs),
        out_shape=tuple(shapes),
        grid_spec=pltpu.PrefetchScalarGridSpec(
            num_scalar_prefetch=1,
            grid=(highs,),
            in_specs=[pl.BlockSpec((total, 4 * depth), rows_of) for _ in lefts]
            + [pl.BlockSpec(right.shape, lambda h, flags: (0, 0)) for right in rights],
            out_specs=(ANY,) * len(shapes),
            scratch_shapes=[pltpu.VMEM((2, 2, 2, depth, size), BF) for size in sizes]
            + [
                pltpu.VMEM((4 * depth, max(sizes)), BF),
                pltpu.SemaphoreType.DMA((2, 2 * len(sizes))),
            ],
        ),
        compiler_params=params(),
        cost_estimate=cost(2 * total * width * sum(sizes), *lefts, *rights, *shapes),
        name="grads",
    )(flags, *lefts, *rights)
    each = 2 * highs
    return [
        (list(outs[k * each : (k + 1) * each : 2]), list(outs[k * each + 1 : (k + 1) * each : 2]))
        for k in range(len(lefts))
    ]


def attend_kernel(own, parts, flags, bases, queries, *refs):
    if own:
        pairs, refs = refs[:parts], refs[parts:]
        lows, ends, within, sums, peaks, totals, pair_buf, sems = refs
    else:
        sums, peaks, totals, *refs = refs
        pairs, refs = refs[:parts], refs[parts:]
        lows, ends, within, mixed, log_sums, mixed_low, pair_buf, sems = refs
    count = queries.shape[0]
    half = count // 2
    highs = parts // 2
    loads = []
    for p in range(parts):
        place = pl.ds((p % 2) * count, count)
        loads.append(
            pltpu.make_async_copy(pairs[p], pair_buf.at[p // 2, place], sems.at[p])
        )
    for load in loads:
        load.start()
    for load in loads:
        load.wait()
    for head in range(2):
        columns = slice(head * HD, (head + 1) * HD)
        for side in range(2):
            place = slice(side * half, (side + 1) * half)
            query = queries[place, columns] * jnp.asarray(HD ** (-0.5), BF)
            low, end = lows[place, :], ends[place, :]

            def step(high, base, carry):
                peak, total, accum = carry
                scores = mm_nt(query, pair_buf[high, :, :HD])
                position = within[...] + base
                allowed = (position >= low) & (position <= end)
                scores = jnp.where(allowed, scores, MASKED)
                new_peak = jnp.maximum(peak, jnp.max(scores, axis=1, keepdims=True))
                decay = jnp.exp(peak - new_peak)
                probs = jnp.exp(scores - new_peak)
                total = decay * total + jnp.sum(probs, axis=1, keepdims=True)
                accum = decay * accum + mm(probs.astype(BF), pair_buf[high, :, HD:])
                return new_peak, total, accum

            if own:
                start = (
                    jnp.full((half, 1), MASKED, F32),
                    jnp.zeros((half, 1), F32),
                    jnp.zeros((half, HD), F32),
                )
                peak, total, accum = step(0, bases[0], start)
                peaks[head, place, :] = peak
                totals[head, place, :] = total
                sums[place, columns] = accum
                continue

            def far_step(i, carry):
                high = highs - flags[1] + i
                return step(high, bases[high + 1], carry)

            start = (peaks[head, place, :], totals[head, place, :], sums[place, columns])
            peak, total, accum = lax.fori_loop(0, flags[1], far_step, start)
            out = accum / total
            mixed[place, columns] = out
            mixed_low[place, columns] = out.astype(BF)
            log_sums[head, place, :] = peak + jnp.log(total)


def attend(flags, bases, queries, pairs, lows, ends, within, before=None):
    count = queries.shape[0]
    parts = len(pairs)
    low = jax.ShapeDtypeStruct((count, 2 * HD), BF)
    mixed = jax.ShapeDtypeStruct((count, 2 * HD), F32)
    column = jax.ShapeDtypeStruct((2, count, 1), F32)
    before = before or ()
    return pl.pallas_call(
        functools.partial(attend_kernel, not before, parts),
        out_shape=(mixed, column, low) if before else (mixed, column, column),
        in_specs=[SCALARS, SCALARS]
        + [WHOLE] * (1 + len(before))
        + [ANY] * parts
        + [WHOLE] * 3,
        out_specs=(WHOLE,) * 3,
        scratch_shapes=[
            pltpu.VMEM((parts // 2, 2 * count, 2 * HD), BF),
            pltpu.SemaphoreType.DMA((parts,)),
        ],
        compiler_params=params(),
        cost_estimate=cost(16 * count * count * parts * HD, mixed),
        name="attend",
    )(flags, bases, queries, *before, *pairs, lows, ends, within)


def attend_back_kernel(own, parts, flags, bases, source, back, *refs):
    pairs, refs = refs[:parts], refs[parts:]
    lows, ends, within, stats, deltas, *refs = refs
    if own:
        sum_in, cos_ref, sin_ref, *refs = refs
    outs, out_ref, refs = refs[:parts], refs[parts], refs[parts + 1 :]
    pair_buf, queries, backs, probs_buf, score_buf, query_sum, pair_sum, sems, out_sem = refs
    count = source.shape[0]
    highs = parts // 2
    scale = HD ** (-0.5)
    loads = []
    for p in range(parts):
        loads.append(pltpu.make_async_copy(pairs[p], pair_buf.at[p], sems.at[p]))
    for load in loads:
        load.start()
    for head in range(2):
        place = slice(head * count, (head + 1) * count)
        columns = slice(head * HD, (head + 1) * HD)
        queries[place, :] = source[:, columns] * jnp.asarray(scale, BF)
        backs[place, :] = back[:, columns]
    query_sum[...] = sum_in[...] if own else jnp.zeros_like(query_sum)
    for load in loads:
        load.wait()

    def step(i, carry):
        if own:
            b, base = i, bases[0]
        else:
            b = 2 * (highs - flags[1]) + i
            base = bases[b // 2 + 1]
        keys, values = pair_buf[b, :, :HD], pair_buf[b, :, HD:]
        place = pl.multiple_of(lax.rem(i, 2) * count, count)
        position = within[pl.ds(place, count), :] + base
        allowed = (position >= lows[...]) & (position <= ends[...])
        for head in range(2):
            place = slice(head * count, (head + 1) * count)
            scores = mm_nt(keys, queries[place, :])
            probs = jnp.where(allowed, jnp.exp(scores - stats[head : head + 1, :]), 0.0)
            prob_back = mm_nt(values, backs[place, :])
            probs_buf[:, place] = probs.astype(BF)
            score_buf[:, place] = (probs * (prob_back - deltas[head : head + 1, :])).astype(BF)
        pair_sum[:, :HD] = mm(score_buf[...], queries[...]).astype(BF)
        pair_sum[:, HD:] = mm(probs_buf[...], backs[...]).astype(BF)
        query_sum[...] += mm_tn(score_buf[...], keys)
        for p in range(parts):

            @pl.when(b == p)
            def _(p=p):
                store = pltpu.make_async_copy(pair_sum, outs[p], out_sem)
                store.start()
                store.wait()

        return carry

    lax.fori_loop(0, 2 if own else 2 * flags[1], step, 0)
    if not own:
        out_ref[...] = query_sum[...]
        return
    c, s = cos_ref[...], sin_ref[...]
    for head in range(2):
        grad = query_sum[head * count : (head + 1) * count, :] * scale
        a, b = grad[:, : HD // 2], grad[:, HD // 2 :]
        turned = jnp.concatenate([a * c + b * s, b * c - a * s], axis=1)
        out_ref[:, head * HD : (head + 1) * HD] = turned.astype(BF)


def attend_back(flags, bases, queries, back, pairs, lows, ends, within, stats, deltas, more=()):
    count = queries.shape[0]
    parts = len(pairs)
    low = jax.ShapeDtypeStruct((count, 2 * HD), BF)
    last = low if more else jax.ShapeDtypeStruct((2 * count, HD), F32)
    outs = pl.pallas_call(
        functools.partial(attend_back_kernel, bool(more), parts),
        out_shape=(low,) * parts + (last,),
        in_specs=[SCALARS, SCALARS]
        + [WHOLE] * 2
        + [ANY] * parts
        + [WHOLE] * (5 + len(more)),
        out_specs=(ANY,) * parts + (WHOLE,),
        scratch_shapes=[
            pltpu.VMEM((parts, count, 2 * HD), BF),
            pltpu.VMEM((2 * count, HD), BF),
            pltpu.VMEM((2 * count, HD), BF),
            pltpu.VMEM((count, 2 * count), BF),
            pltpu.VMEM((count, 2 * count), BF),
            pltpu.VMEM((2 * count, HD), F32),
            pltpu.VMEM((count, 2 * HD), BF),
            pltpu.SemaphoreType.DMA((parts,)),
            pltpu.SemaphoreType.DMA,
        ],
        compiler_params=params(),
        cost_estimate=cost(20 * count * count * parts * HD, low, low),
        name="attend_back",
    )(flags, bases, queries, back, *pairs, lows, ends, within, stats, deltas, *more)
    return list(outs[0:parts:2]), list(outs[1:parts:2]), outs[parts]


def tie(values):
    return lax.optimization_barrier(values)


class Bag:
    pass


class Weight:
    def __init__(self, keep):
        self.keep = keep


class Sum:
    pass


class Grad:
    pass


def flatten(bag):
    names = sorted(vars(bag))
    return [getattr(bag, name) for name in names], tuple(names)


def unflatten(kind, names, values):
    bag = kind.__new__(kind)
    for name, value in zip(names, values):
        setattr(bag, name, value)
    return bag


for kind in (Bag, Weight, Sum, Grad):
    jax.tree_util.register_pytree_node(kind, flatten, functools.partial(unflatten, kind))


def halves(zl, array):
    c = array.shape[1] // 2
    left, right = array[:, :c], array[:, c:]
    first = zl == 0
    return jnp.where(first, left, right), jnp.where(first, right, left)


def join(zl, own, received):
    first = zl == 0
    return jnp.concatenate([jnp.where(first, own, received), jnp.where(first, received, own)], axis=1)


def turn_back(vectors, cosines, sines):
    half = vectors.shape[-1] // 2
    a, b = vectors[..., :half], vectors[..., half:]
    return jnp.concatenate([a * cosines + b * sines, b * cosines - a * sines], axis=-1)


def body(
    hidden_in,
    segments,
    attn_gain,
    query_weight,
    key_weight,
    value_weight,
    output_weight,
    mlp_gain,
    gate_weight,
    up_weight,
    down_weight,
    cotangent,
):
    wide_count = lax.axis_size("wide")
    devices = wide_count * 4
    mover = Mover(devices)
    highs = mover.highs
    wide = lax.axis_index("wide")
    tp = lax.axis_index("tp")
    y, zl, zh = wide & 1, (wide >> 1) & 1, wide >> 2
    first = zl == 0
    flags = jnp.stack([zl, zh, y]).astype(jnp.int32)
    micro, local, width = hidden_in.shape
    rows = micro * local
    wide_tokens = segments.shape[1]
    head_rows = 8 * local
    scale = HD ** (-0.5)
    swap = mover.swap
    shifts = range(1, highs)
    places = jnp.stack(
        [
            (((zh + shift) % highs) * 2 + (zl ^ low)) * 2 + (y ^ dy)
            for shift in range(highs)
            for dy in range(2)
            for low in range(2)
        ]
    ).astype(jnp.int32)

    def highs_of(value, causal=False):
        return [mover.from_high(value, shift, causal) for shift in shifts]

    def over_y(values):
        return [swap(value, YDIR) for value in values]

    inputs = hidden_in.reshape(rows, width).astype(F32)
    scale_one = lax.rsqrt(jnp.mean(inputs * inputs, axis=-1, keepdims=True) + EPSILON)
    plain_one = inputs * scale_one

    gain_one = attn_gain.astype(F32)[:, None]
    gain_two = mlp_gain.astype(F32)[:, None]

    def gained(weight, gain):
        return (weight.astype(F32) * gain).astype(BF)

    pair_weight = jnp.concatenate([key_weight, value_weight], axis=1)
    gate_keep, gate_send = halves(zl, gained(gate_weight, gain_two))
    up_keep, up_send = halves(zl, gained(up_weight, gain_two))
    down_keep, down_send = halves(zl, down_weight.T)
    units = 512
    groups = gate_keep.shape[1] // units

    def cut_units(c, gate, up, down):
        cut = slice(c * units, (c + 1) * units)
        return jnp.concatenate([gate[:, cut], up[:, cut], down[:, cut]], axis=1)

    live = Bag()

    def cut():
        vars(live).update(vars(tie(live)))

    def pair_of_segments():
        own, got = live.segments, live.seg_got
        return [jnp.stack([jnp.where(first, own, got), jnp.where(first, got, own)])]

    def blocks_of(weight):
        blocks = [weight.keep, weight.got, weight.yk, weight.yg]
        for group in zip(weight.hk, weight.hg, weight.hyk, weight.hyg):
            blocks += group
        return blocks

    def own_first(row):
        low, high = row[:local], row[local:]
        live.row = jnp.where(first, low, high)
        live.rz = swap(jnp.where(first, high, low), ZLOW)
        live.rx = swap(live.row, XDIR)
        live.rc = [swap(live.row, CORE)]

    def rows_first(row):
        live.row, live.rx, live.rz = row, swap(row, XDIR), swap(row, ZLOW)
        live.rc = [swap(row, CORE)]

    def rows_second():
        live.rd = swap(live.rz, XDIR)
        live.rc += [swap(value, CORE) for value in (live.rx, live.rz)]

    def rows_last():
        row, x, z, d, c = live.row, live.rx, live.rz, live.rd, live.rc
        del live.row, live.rx, live.rz, live.rd, live.rc
        return [row, c[0], x, c[1], z, c[2], d, swap(d, CORE)]

    def stack_first(row):
        low, high = row[:local], row[local:]
        live.row = jnp.where(first, low, high)
        live.rz = swap(jnp.where(first, high, low), ZLOW)

    def stack_second():
        live.stack = jnp.concatenate([live.row, live.rz])
        live.stack_x = swap(live.stack, XDIR)
        live.stack_c = swap(live.stack, CORE)
        del live.row, live.rz

    def stack_last():
        stacks = [live.stack, live.stack_c, live.stack_x, swap(live.stack_x, CORE)]
        del live.stack, live.stack_c, live.stack_x
        return stacks

    def sums_start(pair):
        part = Sum()
        part.keep, part.send = pair
        return part

    def sums_core(part):
        part.send = swap(part.send, CORE)

    def sums_combine(part):
        part.own, part.near, part.low, part.far = combine(part.keep, part.send)
        del part.keep, part.send

    def sums_far(part):
        part.far = swap(part.far, XDIR)

    def sums_near(part):
        low = (part.low.astype(F32) + part.far.astype(F32)).astype(BF)
        part.low, part.near = swap(low, ZLOW), swap(part.near, XDIR)
        del part.far

    def sums_total(part):
        return part.own + part.near.astype(F32) + part.low.astype(F32)

    def own_x(part):
        part.far, part.near = swap(part.far, XDIR), swap(part.near, XDIR)

    def own_zl(part):
        low = (part.low.astype(F32) + part.far.astype(F32)).astype(BF)
        part.low = swap(low, ZLOW)
        del part.far

    def own_total(part):
        mine, other = part.own + part.near.astype(F32), part.low.astype(F32)
        return jnp.concatenate([jnp.where(first, mine, other), jnp.where(first, other, mine)])

    def grad_start(pair):
        part = Grad()
        part.keep, part.send = pair
        return part

    def grad_y_far(part):
        part.send[1:] = [swap(part.send[shift], YDIR) for shift in shifts]

    def grad_y_near(part):
        part.send[0] = swap(part.send[0], YDIR)

    def grad_h(part, low):
        moved = []
        for shift in shifts:
            half = part.keep[shift][low].astype(F32) + part.send[shift][low].astype(F32)
            moved.append(mover.to_high(half.astype(BF), shift))
        if low:
            part.moved_got = moved
        else:
            part.moved_own = moved

    def grad_zl(part):
        totals = []
        for low in range(2):
            total = part.keep[0][low].astype(F32) + part.send[0][low].astype(F32)
            for moved in (part.moved_own, part.moved_got)[low]:
                total = total + moved.astype(F32)
            totals.append(total)
        part.own, part.got = totals[0], swap(totals[1].astype(BF), ZLOW)
        del part.keep, part.send, part.moved_own, part.moved_got

    span = jnp.arange(local, dtype=jnp.int32)
    steps = jnp.arange(4, dtype=jnp.int32)
    within = (
        ((zl ^ jnp.arange(2, dtype=jnp.int32))[:, None, None] * 2 * wide_tokens)
        + ((tp ^ steps) * local)[None, :, None]
        + span[None, None, :]
    ).reshape(head_rows)
    row_positions = (zh * 4 + y) * wide_tokens + within
    bases = jnp.stack([((zh + shift) % highs) * 4 * wide_tokens for shift in range(highs)])
    bases = bases.astype(jnp.int32)
    key_within = jnp.concatenate([within + (y ^ dy) * wide_tokens for dy in range(2)])
    freqs = jnp.exp(-math.log(ROPE_BASE) * (2.0 * jnp.arange(HD // 2, dtype=F32) / HD))
    angles = row_positions.astype(F32)[:, None] * freqs[None, :]
    tables = (jnp.cos(angles), jnp.sin(angles))

    live.upstream = cotangent.reshape(rows, width)
    qkv_own, row_one = tie(
        [
            jnp.concatenate([gained(w, gain_one) for w in (query_weight, pair_weight)], axis=1),
            plain_one.astype(BF),
        ]
    )
    live.q = q = Weight(qkv_own)
    q.hk = highs_of(q.keep)
    q.got = swap(q.keep, ZLOW)
    q.yk = swap(q.keep, YDIR)
    stack_first(row_one)
    live.u_send = [cut_units(c, gate_send, up_send, down_send) for c in range(groups)]
    live.u = u = [Weight(cut_units(c, gate_keep, up_keep, down_keep)) for c in range(groups)]
    live.o_own = output_weight.T
    live.segments = segments
    u[0].yk = swap(u[0].keep, YDIR)
    live.seg_got = swap(segments, ZLOW)
    cut()
    q, u = live.q, live.u
    q.hg = highs_of(q.got)
    q.hyk = over_y(q.hk)
    q.yg = swap(q.got, YDIR)
    stack_second()
    live.o_got = swap(live.o_own, ZLOW)
    live.seg = pair_of_segments()
    live.seg.append(swap(live.seg[0], YDIR))
    cut()
    q, u = live.q, live.u
    q.hyg = over_y(q.hg)
    live.out_pair = jnp.concatenate([live.o_own, live.o_got])
    live.out_h = highs_of(live.out_pair)
    live.seg = [jnp.concatenate(live.seg)]
    live.seg += highs_of(live.seg[0])
    live.dx = swap(live.upstream, XDIR)
    live.normed, live.queries, live.pair = gathered_matmul(
        places, stack_last(), blocks_of(q), tables
    )
    cut()
    u = live.u
    live.pair_h, live.pair_y = highs_of(live.pair, causal=True), swap(live.pair, YDIR)
    live.out_hy = over_y(live.out_h)
    live.dz = swap(live.upstream, ZLOW)
    seg_all = lax.dynamic_index_in_dim(jnp.concatenate(live.seg), zl, 1, keepdims=False)
    own_pair = lax.dynamic_index_in_dim(live.seg[0][:2], zl, 1, keepdims=False)
    del live.seg
    own_rows = jnp.stack(
        [
            lax.dynamic_slice_in_dim(
                lax.dynamic_index_in_dim(own_pair, zl ^ dzl, 0, keepdims=False),
                (tp ^ dtp) * local,
                local,
                0,
            )
            for dzl in range(2)
            for dtp in range(4)
        ]
    ).reshape(head_rows)
    live.starts = jnp.sum(
        (seg_all.reshape(1, -1) < own_rows[:, None]).astype(jnp.int32), axis=1
    )
    spots = (
        live.starts.reshape(head_rows, 1),
        row_positions.reshape(head_rows, 1),
        key_within.reshape(1, 2 * head_rows),
    )
    live.before = attend(flags, bases, live.queries, [live.pair, live.pair_y], *spots)
    cut()
    u = live.u
    pair_hy = over_y(live.pair_h)
    u[0].got = swap(live.u_send[0], ZLOW)
    u[0].hk = highs_of(u[0].keep)
    live.out_y = swap(live.out_pair, YDIR)
    live.dd = swap(live.dz, XDIR)
    live.own_pairs, live.far_pairs = [live.pair, live.pair_y], []
    for values in zip(live.pair_h, pair_hy):
        live.far_pairs += values
    del live.pair, live.pair_y, live.pair_h
    live.mixed, live.log_sums, live.mixed_all = attend(
        flags, bases, live.queries, live.far_pairs, *spots, live.before
    )
    del live.before
    cut()
    u = live.u
    live.o = [live.out_pair, live.out_y]
    for values in zip(live.out_h, live.out_hy):
        live.o += values
    del live.out_pair, live.out_y, live.out_h, live.out_hy
    live.a = sums_start(partial_matmul(places, [(live.mixed_all, 0, 2 * HD)], [live.o], [0]))
    cut()
    u = live.u
    sums_core(live.a)
    u[0].yg = swap(u[0].got, YDIR)
    u[1].got = swap(live.u_send[1], ZLOW)
    sums_combine(live.a)
    own_x(live.a)
    cut()
    u = live.u
    own_zl(live.a)
    live.log_sums = live.log_sums.reshape(2, head_rows)
    live.dc = [swap(d, CORE) for d in (live.upstream, live.dx, live.dz, live.dd)]
    cut()
    u = live.u
    live.hidden = hidden = inputs + own_total(live.a)
    del live.a
    scale_two = lax.rsqrt(jnp.mean(hidden * hidden, axis=-1, keepdims=True) + EPSILON)
    plain_two = hidden * scale_two
    rows_first(plain_two.astype(BF))
    u[0].hg = highs_of(u[0].got)
    u[1].yg = swap(u[1].got, YDIR)
    cut()
    u = live.u
    rows_second()
    u[0].hyk = over_y(u[0].hk)
    u[0].hyg = over_y(u[0].hg)
    u[1].hg = highs_of(u[1].got)
    d_x, d_z, d_d, d_cores = live.dx, live.dz, live.dd, live.dc
    live.dy_all = assemble(
        [live.upstream, d_cores[0], d_x, d_cores[1], d_z, d_cores[2], d_d, d_cores[3]]
    )
    del live.dx, live.dz, live.dd, live.dc
    cut()
    u = live.u
    chunks = rows_last()
    u[1].yk = swap(u[1].keep, YDIR)
    u[1].hk = highs_of(u[1].keep)
    u[1].hyg = over_y(u[1].hg)
    live.backs, live.acts = [None] * 2, [None] * 2

    def unit_work(c, source):
        live.x_all, live.backs[c], live.acts[c] = hidden_units(
            places, source, live.dy_all, blocks_of(live.u[c])
        )

    def unit_grads(c):
        pairs = weight_grads(
            flags, highs, [live.x_all, live.dy_all], [live.backs[c], live.acts[c]]
        )
        return [grad_start(pair) for pair in pairs]

    unit_work(0, chunks)
    live.g = unit_grads(0)
    cut()
    u, g = live.u, live.g
    u[1].hyk = over_y(u[1].hk)
    cut()
    u, g = live.u, live.g
    grad_y_far(g[1])
    unit_work(1, [live.x_all])
    cut()
    g = live.g
    grad_y_far(g[0])
    grad_h(g[1], 0)
    grad_h(g[1], 1)
    live.unit_blocks = [blocks_of(weight) for weight in live.u]
    del live.u
    live.e = sums_start(
        partial_matmul(
            places,
            [(back, 0, 2 * units) for back in live.backs],
            live.unit_blocks,
            [0] * groups,
        )
    )
    cut()
    g = live.g
    sums_core(live.e)
    grad_y_near(g[0])
    grad_h(g[0], 1)
    sums_combine(live.e)
    sums_far(live.e)
    live.g += unit_grads(1)
    cut()
    g = live.g
    sums_near(live.e)
    grad_h(g[0], 0)
    grad_y_far(g[2])
    cut()
    weighted_two = sums_total(live.e)
    del live.e
    hidden_back = live.upstream.astype(F32) + scale_two * (
        weighted_two - plain_two * jnp.mean(weighted_two * plain_two, axis=-1, keepdims=True)
    )
    g = live.g
    own_first(hidden_back.astype(BF))
    grad_y_near(g[2])
    grad_h(g[2], 0)
    live.d = sums_start(
        partial_matmul(
            places,
            [(act, 0, units) for act in live.acts],
            live.unit_blocks,
            [2 * units] * groups,
        )
    )
    del live.acts, live.backs, live.unit_blocks
    cut()
    g = live.g
    rows_second()
    grad_zl(g[0])
    grad_y_far(g[3])
    cut()
    g = live.g
    grad_y_near(g[3])
    grad_h(g[3], 0)
    sums_core(live.d)
    live.attn_back, live.back, live.deltas = gathered_matmul(
        places, rows_last(), live.o, mixed=live.mixed
    )
    cut()
    g = live.g
    grad_y_near(g[1])
    grad_h(g[3], 1)
    live.turned = (
        live.starts.reshape(1, head_rows),
        row_positions.reshape(1, head_rows),
        key_within.reshape(2 * head_rows, 1),
        live.log_sums,
        live.deltas.T,
    )
    live.k_keep, live.k_send, live.query_sum = attend_back(
        flags, bases, live.queries, live.back, live.far_pairs, *live.turned
    )
    cut()
    g = live.g
    live.k_send = [swap(value, YDIR) for value in live.k_send]
    grad_zl(g[1])
    grad_h(g[2], 1)
    grad_zl(g[3])
    keep, send, live.query_back = attend_back(
        flags,
        bases,
        live.queries,
        live.back,
        live.own_pairs,
        *live.turned,
        (live.query_sum, *tables),
    )
    live.k_keep, live.k_send = keep + live.k_keep, send + live.k_send
    del live.turned, live.query_sum
    sums_combine(live.d)
    (grads_out,) = weight_grads(flags, highs, [live.attn_back], [live.mixed_all])
    live.g_out = grad_start(grads_out)
    cut()
    g = live.g
    live.k_moved = []
    for shift in shifts:
        half = live.k_keep[shift].astype(F32) + live.k_send[shift].astype(F32)
        live.k_moved.append(mover.to_high(half.astype(BF), shift, causal=True))
    live.k_near = swap(live.k_send[0], YDIR)
    grad_zl(g[2])
    grad_y_far(live.g_out)
    sums_far(live.d)
    (grads_q,) = weight_grads(flags, highs, [live.normed], [live.query_back])
    live.g_q = grad_start(grads_q)
    cut()
    g = live.g
    total = live.k_keep[0].astype(F32) + live.k_near.astype(F32)
    for moved in live.k_moved:
        total = total + moved.astype(F32)
    del live.k_keep, live.k_send, live.k_moved, live.k_near
    key_back = turn_back(total[:, :HD], *tables).astype(BF)
    live.pair_back = jnp.concatenate([key_back, total[:, HD:].astype(BF)], axis=1)
    grad_y_near(live.g_out)
    grad_h(live.g_out, 0)
    grad_h(live.g_out, 1)
    grad_y_far(live.g_q)
    sums_near(live.d)
    (grads_p,) = weight_grads(flags, highs, [live.normed], [live.pair_back])
    live.g_p = grad_start(grads_p)
    cut()
    g = live.g
    grad_zl(live.g_out)
    grad_y_near(live.g_q)
    grad_h(live.g_q, 0)
    grad_h(live.g_q, 1)
    grad_y_far(live.g_p)
    live.n = sums_start(
        partial_matmul(
            places,
            [(live.query_back, 0, 2 * HD), (live.pair_back, 0, 2 * HD)],
            [blocks_of(live.q)] * 2,
            [0, 2 * HD],
        )
    )
    cut()
    g = live.g
    sums_core(live.n)
    grad_zl(live.g_q)
    grad_y_near(live.g_p)
    grad_h(live.g_p, 0)
    grad_h(live.g_p, 1)
    sums_combine(live.n)
    own_x(live.n)
    cut()
    g = live.g
    own_zl(live.n)
    grad_zl(live.g_p)

    def unit_columns(part, at):
        cut = slice(at * units, (at + 1) * units)
        own = jnp.concatenate([piece.own[:, cut] for piece in part], axis=1)
        return join(
            zl, own, jnp.concatenate([piece.got[:, cut] for piece in part], axis=1).astype(F32)
        )

    gate_plain, up_plain = unit_columns(g[0::2], 0), unit_columns(g[0::2], 1)
    live.shards = (gate_plain * gain_two, up_plain * gain_two, unit_columns(g[1::2], 0).T)
    live.gain_two = jnp.sum(gate_plain * gate_weight.astype(F32), axis=1) + jnp.sum(
        up_plain * up_weight.astype(F32), axis=1
    )
    live.layer_out = (live.hidden + sums_total(live.d)).astype(BF)
    cut()
    weighted_one = own_total(live.n)
    input_grad = hidden_back + scale_one * (
        weighted_one - plain_one * jnp.mean(weighted_one * plain_one, axis=-1, keepdims=True)
    )
    g = live.g
    def columns_of(part):
        return part.own + part.got.astype(F32)

    query_plain, pair_plain = columns_of(live.g_q), columns_of(live.g_p)
    gain_sums = jnp.stack(
        [
            jnp.sum(query_plain * query_weight.astype(F32), axis=1)
            + jnp.sum(pair_plain * pair_weight.astype(F32), axis=1),
            live.gain_two,
        ]
    )
    gain_sums = gain_sums + sum(swap(gain_sums, m) for m in (CORE, XDIR, CORE | XDIR))
    pair_shard = pair_plain * gain_one
    shape = hidden_in.shape
    return (
        live.layer_out.reshape(shape),
        input_grad.reshape(shape),
        gain_sums[0],
        query_plain * gain_one,
        pair_shard[:, :HD],
        pair_shard[:, HD:],
        columns_of(live.g_out).T,
        gain_sums[1],
        *live.shards,
    )


def solution(mesh):
    rows = P(None, ("wide", "tp"), None)
    columns = P("wide", "tp")
    flipped = P("tp", "wide")
    gain = P("wide")
    weights = (columns, columns, columns, flipped, gain, columns, columns, flipped)
    return jax.shard_map(
        body,
        mesh=mesh,
        in_specs=(rows, P(None, "wide"), gain) + weights + (rows,),
        out_specs=(rows, rows, gain) + weights,
        check_vma=False,
    )
```
